128 devices in a mesh: tm: 16 (over x, y_lo, core), space: 8 (over z, y_hi).
Axes of the slice: x: 4, y: 4 (y_hi: 2, y_lo: 2; y = y_hi * 2 + y_lo), z: 4, core: 2. Of those that a mesh axis runs over, the one named last changes fastest.
Arguments:
- input_field: float32 [64, 32, 32, 1024], P('tm', None, 'space'), may hold values from -6 to 6
- cotangent: float32 [64, 32, 32, 1024], P('tm', None, 'space'), may hold values from -6 to 6
- spectral_weights: float32 [2, 2, 16, 32, 32], replicated, may hold values from -0.75 to 0.75
- conv_kernel: float32 [2, 3, 32, 32], replicated, may hold values from -0.625 to 0.625
- mode_list: int32 [16], replicated, may hold values from 0 to 31, as said below
Outputs:
- grad_input: float32 [64, 32, 32, 1024], P('tm', None, 'space')
- grad_spectral: float32 [2, 2, 16, 32, 32], P(None, None, 'tm')
- grad_kernel: float32 [2, 3, 32, 32], replicated
The draws below stay inside these ranges and needn't reach their ends.
Inputs may be any that keep to these rules, and one draw needn't show every extreme that they name: `mode_list`: 16 distinct frequencies in ascending order, with 0 and 31 among them.
All inputs are finite; a program needn't handle non-finite values.
Results may differ from the reference program's by a relative error of at most 0.00014.
Values sent between devices are 32-bit elements; how exact they have to be, the bound alone decides.
No kernel may reach another device: no remote copies, remote signals or barrier semaphores. Data moves between devices by JAX's collectives and lax.ppermute only.
A program may use at most 128 MiB of HBM per device.

```python
import math
import jax
import jax.numpy as jnp
from jax import lax

C = 32
NT = 64
M = 16
S = 1024
L = 2
NX = 32


def draw_mode_list(key, part):
    inner = jax.random.permutation(key, NT // 2 - 2) + 1
    picked = inner[:M - 2].astype(jnp.int32)
    whole = jnp.concatenate([jnp.zeros((1,), jnp.int32), picked, jnp.full((1,), NT // 2 - 1, jnp.int32)])
    return jnp.sort(whole)


def block_scale(stream_key, shape, pieces, low, top_value):
    def one(dim, shards_of):
        steps = jax.random.uniform(jax.random.fold_in(jax.random.fold_in(stream_key, 6), dim), (shards_of,), jnp.float32, low / len(pieces), top_value / len(pieces))
        return jnp.repeat(jnp.exp(steps), shape[dim] // shards_of).reshape((-1,) + (1,) * (len(shape) - dim - 1))

    loudness = one(*pieces[0])
    for cut in pieces[1:]:
        loudness = loudness * one(*cut)
    return loudness


def scatter_about(stream_key, dims, deviation, limit, shards=(), kind=jnp.bfloat16):
    gain = block_scale(stream_key, dims, shards, -0.22, 0.18) if shards else 1.0
    values = jax.random.normal(stream_key, dims, jnp.float32) * deviation * gain
    return jnp.minimum(jnp.maximum(values, -limit), limit).astype(kind)


def setup_inputs(seed: int = 0) -> dict:
    arg_keys = jax.random.split(jax.random.key(seed), 6)
    input_field = scatter_about(arg_keys[0], (NT, C, NX, S), 1.0, 6.0, ((0, 16), (2, 8)), jnp.float32)
    cotangent = scatter_about(arg_keys[1], (NT, C, NX, S), 1.0, 6.0, ((0, 16), (2, 8)), jnp.float32)
    spectral_weights = scatter_about(arg_keys[2], (L, 2, M, C, C), (2 * C) ** -0.5, 0.75, (), jnp.float32)
    conv_kernel = scatter_about(arg_keys[3], (L, 3, C, C), (3 * C) ** -0.5, 0.625, (), jnp.float32)
    mode_list = draw_mode_list(jax.random.fold_in(arg_keys[5], 71), 0)
    return dict(input_field=input_field, cotangent=cotangent, spectral_weights=spectral_weights, conv_kernel=conv_kernel, mode_list=mode_list)


HIGHEST = lax.Precision.HIGHEST

def tables(mode_list, first_step, time_count, total_time):
    time_steps = first_step + jnp.arange(time_count, dtype=jnp.int32)
    phase_index = mode_list[:, None] * time_steps[None, :] % total_time
    angles = phase_index.astype(jnp.float32) * (2.0 * math.pi / total_time)
    return (jnp.cos(angles), jnp.sin(angles))

def forward_dft(cosine_table, sine_table, flattened):
    time_count = flattened.shape[0]
    rows = flattened.reshape(time_count, -1)
    cosine_part = jnp.dot(cosine_table, rows, precision=HIGHEST)
    sine_part = -jnp.dot(sine_table, rows, precision=HIGHEST)
    stacked = jnp.stack([cosine_part, sine_part], axis=1)
    return stacked.reshape(cosine_table.shape[0], 2, flattened.shape[1], flattened.shape[2])

def inverse_dft(cosine_table, sine_table, coefficients, factor):
    mode_count = coefficients.shape[0]
    cosine_term = jnp.dot(cosine_table.T, coefficients[:, 0].reshape(mode_count, -1), precision=HIGHEST)
    sine_term = jnp.dot(sine_table.T, coefficients[:, 1].reshape(mode_count, -1), precision=HIGHEST)
    result = factor * (cosine_term - sine_term)
    return result.reshape(cosine_table.shape[1], coefficients.shape[2], coefficients.shape[3])

def mode_product(values, weight):
    return jnp.einsum('mcn,mcd->mdn', values, weight, precision=HIGHEST)

def channel_mix(coefficients, weight):
    real_part = mode_product(coefficients[:, 0], weight[0]) - mode_product(coefficients[:, 1], weight[1])
    imag_part = mode_product(coefficients[:, 1], weight[0]) + mode_product(coefficients[:, 0], weight[1])
    return jnp.stack([real_part, imag_part], axis=1)

def convolve(padded, kernel, cells_x):
    result = jnp.einsum('tcxs,cd->tdxs', padded[:, :, 0:cells_x], kernel[0], precision=HIGHEST)
    for offset in range(1, 3):
        result = result + jnp.einsum('tcxs,cd->tdxs', padded[:, :, offset:offset + cells_x], kernel[offset], precision=HIGHEST)
    return result

def layer_forward(state_field, weight, kernel, cosine_table, sine_table):
    time_count, channels, cells_x, cells_s = state_field.shape
    flattened = state_field.reshape(time_count, channels, cells_x * cells_s)
    coefficients = forward_dft(cosine_table, sine_table, flattened)
    mixed = channel_mix(coefficients, weight)
    spectral_part = inverse_dft(cosine_table, sine_table, mixed, 2.0 / time_count)
    padded = jnp.pad(state_field, ((0, 0), (0, 0), (1, 1), (0, 0)))
    preact = spectral_part.reshape(state_field.shape) + convolve(padded, kernel, cells_x)
    return jax.nn.gelu(preact, approximate=False)

def reference(input_field, cotangent, spectral_weights, conv_kernel, mode_list):
    cosine_table, sine_table = tables(mode_list, 0, NT, NT)

    def network(state_field, weights, kernels):
        for layer_number in range(L):
            state_field = layer_forward(state_field, weights[layer_number], kernels[layer_number], cosine_table, sine_table)
        return state_field
    output, pullback = jax.vjp(network, input_field, spectral_weights, conv_kernel)
    grad_input, grad_spectral, grad_kernel = pullback(cotangent)
    return (grad_input, grad_spectral, grad_kernel)
```

```python
import functools
import math

import jax
import jax.numpy as jnp
from jax import lax
from jax.experimental import pallas as pl
from jax.experimental.pallas import tpu as pltpu
from jax.sharding import PartitionSpec as P

F32 = jnp.float32
BF16 = jnp.bfloat16
LANES = 128
J = 8
XB = 4
C = 32
VMEM = pl.BlockSpec(memory_space=pltpu.VMEM)
PARAMS = pltpu.CompilerParams(vmem_limit_bytes=56 * 1024 * 1024)


def split(value):
    high = value.astype(BF16)
    low = (value - high.astype(F32)).astype(BF16)
    return high, low


def split_outside(value):
    high = lax.reduce_precision(value, 8, 7)
    return high.astype(BF16), (value - high).astype(BF16)


def dot3(left, right, dims=((1,), (0,))):
    (lh, ll), (rh, rl) = left, right
    (lc,), (rc,) = dims
    a = jnp.concatenate([lh, ll, lh], axis=lc)
    b = jnp.concatenate([rh, rh, rl], axis=rc)
    return lax.dot_general(a, b, (dims, ((), ())), preferred_element_type=F32)


def scatter_kernel(field_ref, out_ref):
    for q in range(field_ref.shape[3] // LANES):
        lanes = slice(q * LANES, (q + 1) * LANES)
        rows = jnp.concatenate([field_ref[0, :, x, lanes] for x in range(XB)], axis=0)
        groups = LANES // J
        out_ref[q * groups : (q + 1) * groups] = rows.T.reshape(groups, J, LANES)


def gather_kernel(blocks_ref, out_ref):
    groups = LANES // J
    for q in range(out_ref.shape[3] // LANES):
        lanes = slice(q * LANES, (q + 1) * LANES)
        rows = blocks_ref[q * groups : (q + 1) * groups].reshape(LANES, LANES).T
        for x in range(XB):
            out_ref[0, :, x, lanes] = rows[x * C : (x + 1) * C]


def to_blocks(field):
    steps, channels, cells, columns = field.shape
    parts = columns // J
    return pl.pallas_call(
        scatter_kernel,
        grid=(steps,),
        in_specs=[pl.BlockSpec((1, channels, cells, columns), lambda t: (t, 0, 0, 0))],
        out_specs=pl.BlockSpec((parts, J, LANES), lambda t: (0, t, 0)),
        out_shape=jax.ShapeDtypeStruct((parts, steps * J, LANES), F32),
        compiler_params=PARAMS,
    )(field)


def from_blocks(blocks):
    parts, rows, _ = blocks.shape
    steps = rows // J
    return pl.pallas_call(
        gather_kernel,
        grid=(steps,),
        in_specs=[pl.BlockSpec((parts, J, LANES), lambda t: (0, t, 0))],
        out_specs=pl.BlockSpec((1, C, XB, parts * J), lambda t: (t, 0, 0, 0)),
        out_shape=jax.ShapeDtypeStruct((steps, C, XB, parts * J), F32),
        compiler_params=PARAMS,
    )(blocks)


def tables(mode_list, total_time):
    def build(row_is_mode):
        modes, times = mode_list.shape[0], total_time
        shape = (modes * 2 * J, times * J) if row_is_mode else (times * J, modes * 2 * J)
        dm, dt = (0, 1) if row_is_mode else (1, 0)
        im = lax.broadcasted_iota(jnp.int32, shape, dm)
        it = lax.broadcasted_iota(jnp.int32, shape, dt)
        mode = jnp.repeat(mode_list, 2 * J, total_repeat_length=modes * 2 * J)
        mode = mode[:, None] if row_is_mode else mode[None, :]
        phase = (mode * (it // J)) % total_time
        angle = phase.astype(F32) * (2.0 * math.pi / total_time)
        value = jnp.where((im // J) % 2 == 0, jnp.cos(angle), -jnp.sin(angle))
        return split_outside(jnp.where(im % J == it % J, value, 0.0))

    return *build(True), *build(False)


def weights_kernel(scale, w_ref, high_ref, low_ref):
    modes = w_ref.shape[2]
    row = lax.broadcasted_iota(jnp.int32, (LANES, LANES), 0) // C
    col = lax.broadcasted_iota(jnp.int32, (LANES, LANES), 1) // C
    same = row == col

    def blocked(value):
        wide = jnp.concatenate([value] * XB, axis=1)
        return jnp.where(same, jnp.concatenate([wide] * XB, axis=0), 0.0)

    def body(m, _):
        re = split(blocked(w_ref[0, 0, m] * scale))
        im = split(blocked(w_ref[0, 1, m] * scale))
        for ref, r, i in ((high_ref, re[0], im[0]), (low_ref, re[1], im[1])):
            ref[0, m, :LANES, :LANES] = r
            ref[0, m, :LANES, LANES:] = i
            ref[0, m, LANES:, :LANES] = -i
            ref[0, m, LANES:, LANES:] = r
        return 0

    lax.fori_loop(0, modes, body, 0)


def block_weights(spectral_weights, scale):
    layers, _, modes, channels, _ = spectral_weights.shape
    out = jax.ShapeDtypeStruct((layers, modes, 2 * LANES, 2 * LANES), BF16)
    spec = pl.BlockSpec((1, modes, 2 * LANES, 2 * LANES), lambda l: (l, 0, 0, 0))
    return pl.pallas_call(
        functools.partial(weights_kernel, scale),
        grid=(layers,),
        in_specs=[
            pl.BlockSpec((1, 2, modes, channels, channels), lambda l: (l, 0, 0, 0, 0))
        ],
        out_specs=[spec, spec],
        out_shape=[out, out],
        compiler_params=PARAMS,
    )(spectral_weights)


def band(kernel):
    zero = jnp.zeros((C, C), F32)
    own = [
        [kernel[x - y + 1] if abs(x - y) <= 1 else zero for y in range(XB)] for x in range(XB)
    ]
    edge = [[zero] * XB for _ in range(XB)]
    edge[XB - 1][0] = kernel[0]
    edge[0][XB - 1] = kernel[2]
    return jnp.block(own + edge)


def bands(conv_kernel):
    forward = jnp.stack([band(k) for k in conv_kernel])
    adjoint = jnp.stack([band(jnp.swapaxes(k[::-1], 1, 2)) for k in conv_kernel])
    return *split_outside(forward), *split_outside(adjoint)


def lane_block():
    return lax.broadcasted_iota(jnp.int32, (1, LANES), 1) // C


def put_split(value, s, high_ref, low_ref):
    high, low = split(value)
    high_ref[s] = high
    low_ref[s] = low


def with_neighbours(ref, s):
    own = ref[s]
    x = lane_block()
    zero = jnp.zeros_like(own)
    before = ref[s - 1] if s > 0 else zero
    after = ref[s + 1] if s + 1 < ref.shape[0] else zero
    edge = jnp.where(x == XB - 1, before, jnp.where(x == 0, after, zero))
    return jnp.concatenate([own, edge], axis=1)


def analyse(table, high_ref, low_ref, coef_ref):
    for s in range(0, high_ref.shape[0], 2):
        right = [jnp.concatenate([r[s], r[s + 1]], axis=1) for r in (high_ref, low_ref)]
        result = dot3(table, right)
        coef_ref[s] = result[:, :LANES]
        coef_ref[s + 1] = result[:, LANES:]


def mix(coef_ref, wh_ref, wl_ref, l, mixed_ref, dims):
    bricks = coef_ref.shape[0]
    for m in range(wh_ref.shape[1]):
        re, im = slice(2 * J * m, 2 * J * m + J), slice(2 * J * m + J, 2 * J * (m + 1))
        value = jnp.concatenate(
            [coef_ref[:, re].reshape(bricks * J, LANES), coef_ref[:, im].reshape(bricks * J, LANES)],
            axis=1,
        )
        result = dot3(split(value), (wh_ref[l, m], wl_ref[l, m]), dims)
        mixed_ref[:, re] = result[:, :LANES].reshape(bricks, J, LANES)
        mixed_ref[:, im] = result[:, LANES:].reshape(bricks, J, LANES)


def synthesise(table, mixed_ref, bh, bl, high_ref, low_ref, emit):
    for s in range(0, mixed_ref.shape[0], 2):
        right = split(jnp.concatenate([mixed_ref[s], mixed_ref[s + 1]], axis=1))
        spectral = dot3(table, right)
        for o in range(2):
            value = (with_neighbours(high_ref, s + o), with_neighbours(low_ref, s + o))
            total = spectral[:, o * LANES : (o + 1) * LANES] + dot3(value, (bh, bl))
            emit(s + o, total)


def gelu_parts(z):
    cdf = 0.5 * (1.0 + lax.erf(z * math.sqrt(0.5)))
    slope = cdf + z * (jnp.exp(-0.5 * z * z) * (1.0 / math.sqrt(2.0 * math.pi)))
    return z * cdf, slope


def brick(ref, s):
    return ref[:, s].reshape(-1, LANES)


def forward_kernel(
    x_ref, ah, al, sh, sl, wh, wl, bh, bl,
    coef1, coef2, slope1, slope2, x1h, x1l, x2h, x2l, mixed,
):
    bricks = x_ref.shape[1]
    for s in range(bricks):
        put_split(brick(x_ref, s), s, x1h, x1l)
    analysis, synthesis = (ah[...], al[...]), (sh[...], sl[...])

    def first(s, z):
        value, slope = gelu_parts(z)
        slope1[s] = slope
        put_split(value, s, x2h, x2l)

    def second(s, z):
        slope2[s] = gelu_parts(z)[1]

    for l, (h, low, coef, emit) in enumerate(
        ((x1h, x1l, coef1, first), (x2h, x2l, coef2, second))
    ):
        analyse(analysis, h, low, coef)
        mix(coef, wh, wl, l, mixed, ((1,), (0,)))
        synthesise(synthesis, mixed, bh[l], bl[l], h, low, emit)


def forward(field, tabs, weights, bands_):
    _, bricks, _, _ = field.shape
    rows = tabs[0].shape[1]
    modes = tabs[0].shape[0]
    coef = jax.ShapeDtypeStruct((bricks, modes, LANES), F32)
    full = jax.ShapeDtypeStruct((bricks, rows, LANES), F32)
    half = jax.ShapeDtypeStruct((bricks, rows, LANES), BF16)
    return pl.pallas_call(
        forward_kernel,
        in_specs=[VMEM] * 9,
        out_specs=[VMEM] * 8,
        out_shape=[coef, coef, full, full, half, half, half, half],
        scratch_shapes=[pltpu.VMEM((bricks, modes, LANES), F32)],
        compiler_params=PARAMS,
    )(field, *tabs, *weights, *bands_[:2])


def backward_kernel(
    g_ref, slope1, slope2, ah, al, sh, sl, wh, wl, bh, bl,
    out_ref, sens1, sens2, z1h, z1l, z2h, z2l, mixed,
):
    bricks = g_ref.shape[1]
    for s in range(bricks):
        put_split(brick(g_ref, s) * slope2[s], s, z2h, z2l)
    analysis, synthesis = (ah[...], al[...]), (sh[...], sl[...])

    def second(s, g):
        put_split(g * slope1[s], s, z1h, z1l)

    def first(s, g):
        out_ref[:, s] = g.reshape(out_ref.shape[0], out_ref.shape[2], LANES)

    for l, (h, low, sens, emit) in ((1, (z2h, z2l, sens2, second)), (0, (z1h, z1l, sens1, first))):
        analyse(analysis, h, low, sens)
        mix(sens, wh, wl, l, mixed, ((1,), (1,)))
        synthesise(synthesis, mixed, bh[l], bl[l], h, low, emit)


def backward(cotangent, slope1, slope2, tabs, weights, bands_):
    _, bricks, _, _ = cotangent.shape
    rows = tabs[0].shape[1]
    modes = tabs[0].shape[0]
    coef = jax.ShapeDtypeStruct((bricks, modes, LANES), F32)
    half = jax.ShapeDtypeStruct((bricks, rows, LANES), BF16)
    return pl.pallas_call(
        backward_kernel,
        in_specs=[VMEM] * 11,
        out_specs=[VMEM] * 7,
        out_shape=[jax.ShapeDtypeStruct(cotangent.shape, F32), coef, coef, half, half, half, half],
        scratch_shapes=[pltpu.VMEM((bricks, modes, LANES), F32)],
        compiler_params=PARAMS,
    )(cotangent, slope1, slope2, *tabs, *weights, *bands_[2:])


ROWS = ((0,), (0,))


def weight_kernel(
    scale, coef1, coef2, sens1, sens2, x1h, x1l, x2h, x2l, z1h, z1l, z2h, z2l, out_ref
):
    bricks = coef1.shape[0]
    modes = coef1.shape[1] // (2 * J)
    for m in range(modes):
        re, im = slice(2 * J * m, 2 * J * m + J), slice(2 * J * m + J, 2 * J * (m + 1))
        pieces = []
        for coef, sens in ((coef1, sens1), (coef2, sens2)):
            cr, ci, zr, zi = (
                r[:, p].reshape(bricks * J, LANES)
                for r, p in ((coef, re), (coef, im), (sens, re), (sens, im))
            )
            left = jnp.concatenate([cr, ci], axis=0)
            right = jnp.concatenate(
                [jnp.concatenate([zr, zi], axis=1), jnp.concatenate([zi, -zr], axis=1)], axis=0
            )
            product = dot3(split(left), split(right), ROWS) * scale
            for part in range(2):
                pieces.append(
                    sum(
                        product[x * C : (x + 1) * C, part * LANES + x * C : part * LANES + (x + 1) * C]
                        for x in range(XB)
                    )
                )
        out_ref[m, :C] = jnp.concatenate(pieces, axis=1)
    lines = 2 * C // modes
    for l, (xh, xl, zh, zl) in enumerate(((x1h, x1l, z1h, z1l), (x2h, x2l, z2h, z2l))):
        total = jnp.zeros((LANES, 2 * LANES), F32)
        for s in range(bricks):
            value = (with_neighbours(xh, s), with_neighbours(xl, s))
            total = total + dot3((zh[s], zl[s]), value, ROWS)
        taps = []
        for j in range(3):
            pairs = [(x, x - j + 1) for x in range(XB) if 0 <= x - j + 1 < XB]
            tap = sum(total[y * C : (y + 1) * C, x * C : (x + 1) * C] for x, y in pairs)
            if j == 0:
                tap = tap + total[:C, LANES + (XB - 1) * C :]
            if j == 2:
                tap = tap + total[(XB - 1) * C :, LANES : LANES + C]
            taps.append(tap)
        wide = jnp.concatenate([*taps, jnp.zeros((C, C), F32)], axis=1)
        for i in range(modes // 2):
            out_ref[l * (modes // 2) + i, C : C + lines] = wide[i * lines : (i + 1) * lines]
    out_ref[:, C + lines :] = jnp.zeros((modes, out_ref.shape[1] - C - lines, LANES), F32)


def weight_gradients(scale, *operands):
    modes = operands[0].shape[1] // (2 * J)
    return pl.pallas_call(
        functools.partial(weight_kernel, scale),
        in_specs=[VMEM] * 12,
        out_specs=VMEM,
        out_shape=jax.ShapeDtypeStruct((modes, C + 8, LANES), F32),
        compiler_params=PARAMS,
    )(*operands)


def on_device(input_field, cotangent, spectral_weights, conv_kernel, mode_list):
    groups = lax.axis_size("tm")
    bricks = lax.axis_size("space")
    everyone = ("tm", "space")
    steps = input_field.shape[0]
    total_time = steps * groups
    layers, _, modes, _, _ = spectral_weights.shape
    scale = 2.0 / total_time
    exchange = functools.partial(lax.all_to_all, split_axis=0, concat_axis=0, tiled=True)

    received = exchange(to_blocks(input_field), everyone)
    cot_blocks = to_blocks(cotangent)
    tabs = tables(mode_list, total_time)
    weights = block_weights(spectral_weights, scale)
    bands_ = bands(conv_kernel)
    received, cot_blocks = lax.optimization_barrier((received, cot_blocks))
    cot_received = exchange(cot_blocks, everyone)
    shape = (groups, bricks, steps * J, LANES)
    coef1, coef2, slope1, slope2, x1h, x1l, x2h, x2l = forward(
        received.reshape(shape), tabs, weights, bands_
    )
    grad, sens1, sens2, z1h, z1l, z2h, z2l = backward(
        cot_received.reshape(shape), slope1, slope2, tabs, weights, bands_
    )
    returned = exchange(grad.reshape(cot_received.shape), everyone)
    partial = weight_gradients(
        scale, coef1, coef2, sens1, sens2, x1h, x1l, x2h, x2l, z1h, z1l, z2h, z2l
    )
    partial = reduce_over(partial, groups, "tm")
    spread = jnp.broadcast_to(partial[None], (bricks, *partial.shape))
    total = reduce_over(spread, bricks, "space")
    mode_total = total[:C].reshape(C, layers, 2, 1, C).transpose(1, 2, 3, 0, 4)
    lines = layers * C // groups
    own = total[C : C + lines]
    lined = exchange(jnp.broadcast_to(own[None], (groups, *own.shape)), "tm")
    kernel_total = lined.reshape(layers, C, LANES)[:, :, : 3 * C]
    kernel_total = kernel_total.reshape(layers, C, 3, C).transpose(0, 2, 3, 1)
    return (from_blocks(returned), mode_total, kernel_total)


def reduce_over(pieces, size, axis):
    got = lax.all_to_all(pieces, axis, split_axis=0, concat_axis=0, tiled=True)
    return jnp.sum(got.reshape(size, -1, LANES), axis=0)


def solution(mesh):
    placed = (P("tm", None, "space", None), P("tm", None, "space", None), P(), P(), P())
    return jax.shard_map(
        on_device,
        mesh=mesh,
        in_specs=placed,
        out_specs=(P("tm", None, "space", None), P(None, None, "tm", None, None), P()),
        check_vma=False,
    )
```

```python
import functools
import math

import jax
import jax.numpy as jnp
from jax import lax
from jax.experimental import pallas as pl
from jax.experimental.pallas import tpu as pltpu
from jax.sharding import PartitionSpec as P

F32 = jnp.float32
BF16 = jnp.bfloat16
LANES = 128
J = 8
XB = 4
C = 32
VMEM = pl.BlockSpec(memory_space=pltpu.VMEM)
PARAMS = pltpu.CompilerParams(vmem_limit_bytes=56 * 1024 * 1024)


def split(value):
    high = value.astype(BF16)
    low = (value - high.astype(F32)).astype(BF16)
    return high, low


def split_outside(value):
    high = lax.reduce_precision(value, 8, 7)
    return high.astype(BF16), (value - high).astype(BF16)


def dot3(left, right, dims=((1,), (0,))):
    (lh, ll), (rh, rl) = left, right
    (lc,), (rc,) = dims
    a = jnp.concatenate([lh, ll, lh], axis=lc)
    b = jnp.concatenate([rh, rh, rl], axis=rc)
    return lax.dot_general(a, b, (dims, ((), ())), preferred_element_type=F32)


def scatter_kernel(field_ref, out_ref):
    for q in range(field_ref.shape[3] // LANES):
        lanes = slice(q * LANES, (q + 1) * LANES)
        rows = jnp.concatenate([field_ref[0, :, x, lanes] for x in range(XB)], axis=0)
        groups = LANES // J
        out_ref[q * groups : (q + 1) * groups] = rows.T.reshape(groups, J, LANES)


def gather_kernel(blocks_ref, out_ref):
    groups = LANES // J
    for q in range(out_ref.shape[3] // LANES):
        lanes = slice(q * LANES, (q + 1) * LANES)
        rows = blocks_ref[q * groups : (q + 1) * groups].reshape(LANES, LANES).T
        for x in range(XB):
            out_ref[0, :, x, lanes] = rows[x * C : (x + 1) * C]


def to_blocks(field):
    steps, channels, cells, columns = field.shape
    parts = columns // J
    return pl.pallas_call(
        scatter_kernel,
        grid=(steps,),
        in_specs=[pl.BlockSpec((1, channels, cells, columns), lambda t: (t, 0, 0, 0))],
        out_specs=pl.BlockSpec((parts, J, LANES), lambda t: (0, t, 0)),
        out_shape=jax.ShapeDtypeStruct((parts, steps * J, LANES), F32),
        compiler_params=PARAMS,
    )(field)


def from_blocks(blocks):
    parts, rows, _ = blocks.shape
    steps = rows // J
    return pl.pallas_call(
        gather_kernel,
        grid=(steps,),
        in_specs=[pl.BlockSpec((parts, J, LANES), lambda t: (0, t, 0))],
        out_specs=pl.BlockSpec((1, C, XB, parts * J), lambda t: (t, 0, 0, 0)),
        out_shape=jax.ShapeDtypeStruct((steps, C, XB, parts * J), F32),
        compiler_params=PARAMS,
    )(blocks)


def tables(mode_list, total_time):
    def build(row_is_mode):
        modes, times = mode_list.shape[0], total_time
        shape = (modes * 2 * J, times * J) if row_is_mode else (times * J, modes * 2 * J)
        dm, dt = (0, 1) if row_is_mode else (1, 0)
        im = lax.broadcasted_iota(jnp.int32, shape, dm)
        it = lax.broadcasted_iota(jnp.int32, shape, dt)
        mode = jnp.repeat(mode_list, 2 * J, total_repeat_length=modes * 2 * J)
        mode = mode[:, None] if row_is_mode else mode[None, :]
        phase = (mode * (it // J)) % total_time
        angle = phase.astype(F32) * (2.0 * math.pi / total_time)
        value = jnp.where((im // J) % 2 == 0, jnp.cos(angle), -jnp.sin(angle))
        return split_outside(jnp.where(im % J == it % J, value, 0.0))

    return *build(True), *build(False)


def weights_kernel(scale, w_ref, high_ref, low_ref):
    modes = w_ref.shape[2]
    row = lax.broadcasted_iota(jnp.int32, (LANES, LANES), 0) // C
    col = lax.broadcasted_iota(jnp.int32, (LANES, LANES), 1) // C
    same = row == col

    def blocked(value):
        wide = jnp.concatenate([value] * XB, axis=1)
        return jnp.where(same, jnp.concatenate([wide] * XB, axis=0), 0.0)

    def body(m, _):
        re = split(blocked(w_ref[0, 0, m] * scale))
        im = split(blocked(w_ref[0, 1, m] * scale))
        for ref, r, i in ((high_ref, re[0], im[0]), (low_ref, re[1], im[1])):
            ref[0, m, :LANES, :LANES] = r
            ref[0, m, :LANES, LANES:] = i
            ref[0, m, LANES:, :LANES] = -i
            ref[0, m, LANES:, LANES:] = r
        return 0

    lax.fori_loop(0, modes, body, 0)


def block_weights(spectral_weights, scale):
    layers, _, modes, channels, _ = spectral_weights.shape
    out = jax.ShapeDtypeStruct((layers, modes, 2 * LANES, 2 * LANES), BF16)
    spec = pl.BlockSpec((1, modes, 2 * LANES, 2 * LANES), lambda l: (l, 0, 0, 0))
    return pl.pallas_call(
        functools.partial(weights_kernel, scale),
        grid=(layers,),
        in_specs=[
            pl.BlockSpec((1, 2, modes, channels, channels), lambda l: (l, 0, 0, 0, 0))
        ],
        out_specs=[spec, spec],
        out_shape=[out, out],
        compiler_params=PARAMS,
    )(spectral_weights)


def band(kernel):
    zero = jnp.zeros((C, C), F32)
    own = [
        [kernel[x - y + 1] if abs(x - y) <= 1 else zero for y in range(XB)] for x in range(XB)
    ]
    edge = [[zero] * XB for _ in range(XB)]
    edge[XB - 1][0] = kernel[0]
    edge[0][XB - 1] = kernel[2]
    return jnp.block(own + edge)


def bands(conv_kernel):
    forward = jnp.stack([band(k) for k in conv_kernel])
    adjoint = jnp.stack([band(jnp.swapaxes(k[::-1], 1, 2)) for k in conv_kernel])
    return *split_outside(forward), *split_outside(adjoint)


def lane_block():
    return lax.broadcasted_iota(jnp.int32, (1, LANES), 1) // C


def put_split(value, s, high_ref, low_ref):
    high, low = split(value)
    high_ref[s] = high
    low_ref[s] = low


def with_neighbours(ref, s):
    own = ref[s]
    x = lane_block()
    zero = jnp.zeros_like(own)
    before = ref[s - 1] if s > 0 else zero
    after = ref[s + 1] if s + 1 < ref.shape[0] else zero
    edge = jnp.where(x == XB - 1, before, jnp.where(x == 0, after, zero))
    return jnp.concatenate([own, edge], axis=1)


def analyse(table, high_ref, low_ref, coef_ref):
    for s in range(0, high_ref.shape[0], 2):
        right = [jnp.concatenate([r[s], r[s + 1]], axis=1) for r in (high_ref, low_ref)]
        result = dot3(table, right)
        coef_ref[s] = result[:, :LANES]
        coef_ref[s + 1] = result[:, LANES:]


def mix(coef_ref, wh_ref, wl_ref, l, mixed_ref, dims):
    bricks = coef_ref.shape[0]
    for m in range(wh_ref.shape[1]):
        re, im = slice(2 * J * m, 2 * J * m + J), slice(2 * J * m + J, 2 * J * (m + 1))
        value = jnp.concatenate(
            [coef_ref[:, re].reshape(bricks * J, LANES), coef_ref[:, im].reshape(bricks * J, LANES)],
            axis=1,
        )
        result = dot3(split(value), (wh_ref[l, m], wl_ref[l, m]), dims)
        mixed_ref[:, re] = result[:, :LANES].reshape(bricks, J, LANES)
        mixed_ref[:, im] = result[:, LANES:].reshape(bricks, J, LANES)


def synthesise(table, mixed_ref, bh, bl, high_ref, low_ref, emit):
    for s in range(0, mixed_ref.shape[0], 2):
        right = split(jnp.concatenate([mixed_ref[s], mixed_ref[s + 1]], axis=1))
        spectral = dot3(table, right)
        for o in range(2):
            value = (with_neighbours(high_ref, s + o), with_neighbours(low_ref, s + o))
            total = spectral[:, o * LANES : (o + 1) * LANES] + dot3(value, (bh, bl))
            emit(s + o, total)


def gelu_parts(z):
    cdf = 0.5 * (1.0 + lax.erf(z * math.sqrt(0.5)))
    slope = cdf + z * (jnp.exp(-0.5 * z * z) * (1.0 / math.sqrt(2.0 * math.pi)))
    return z * cdf, slope


def brick(ref, s):
    return ref[:, s].reshape(-1, LANES)


def forward_kernel(
    x_ref, ah, al, sh, sl, wh, wl, bh, bl,
    coef1, coef2, slope1, slope2, x1h, x1l, x2h, x2l, mixed,
):
    bricks = x_ref.shape[1]
    for s in range(bricks):
        put_split(brick(x_ref, s), s, x1h, x1l)
    analysis, synthesis = (ah[...], al[...]), (sh[...], sl[...])

    def first(s, z):
        value, slope = gelu_parts(z)
        slope1[s] = slope
        put_split(value, s, x2h, x2l)

    def second(s, z):
        slope2[s] = gelu_parts(z)[1]

    for l, (h, low, coef, emit) in enumerate(
        ((x1h, x1l, coef1, first), (x2h, x2l, coef2, second))
    ):
        analyse(analysis, h, low, coef)
        mix(coef, wh, wl, l, mixed, ((1,), (0,)))
        synthesise(synthesis, mixed, bh[l], bl[l], h, low, emit)


def forward(field, tabs, weights, bands_):
    _, bricks, _, _ = field.shape
    rows = tabs[0].shape[1]
    modes = tabs[0].shape[0]
    coef = jax.ShapeDtypeStruct((bricks, modes, LANES), F32)
    full = jax.ShapeDtypeStruct((bricks, rows, LANES), F32)
    half = jax.ShapeDtypeStruct((bricks, rows, LANES), BF16)
    return pl.pallas_call(
        forward_kernel,
        in_specs=[VMEM] * 9,
        out_specs=[VMEM] * 8,
        out_shape=[coef, coef, full, full, half, half, half, half],
        scratch_shapes=[pltpu.VMEM((bricks, modes, LANES), F32)],
        compiler_params=PARAMS,
    )(field, *tabs, *weights, *bands_[:2])


def backward_kernel(
    g_ref, slope1, slope2, ah, al, sh, sl, wh, wl, bh, bl,
    out_ref, sens1, sens2, z1h, z1l, z2h, z2l, mixed,
):
    bricks = g_ref.shape[1]
    for s in range(bricks):
        put_split(brick(g_ref, s) * slope2[s], s, z2h, z2l)
    analysis, synthesis = (ah[...], al[...]), (sh[...], sl[...])

    def second(s, g):
        put_split(g * slope1[s], s, z1h, z1l)

    def first(s, g):
        out_ref[:, s] = g.reshape(out_ref.shape[0], out_ref.shape[2], LANES)

    for l, (h, low, sens, emit) in ((1, (z2h, z2l, sens2, second)), (0, (z1h, z1l, sens1, first))):
        analyse(analysis, h, low, sens)
        mix(sens, wh, wl, l, mixed, ((1,), (1,)))
        synthesise(synthesis, mixed, bh[l], bl[l], h, low, emit)


def backward(cotangent, slope1, slope2, tabs, weights, bands_):
    _, bricks, _, _ = cotangent.shape
    rows = tabs[0].shape[1]
    modes = tabs[0].shape[0]
    coef = jax.ShapeDtypeStruct((bricks, modes, LANES), F32)
    half = jax.ShapeDtypeStruct((bricks, rows, LANES), BF16)
    return pl.pallas_call(
        backward_kernel,
        in_specs=[VMEM] * 11,
        out_specs=[VMEM] * 7,
        out_shape=[jax.ShapeDtypeStruct(cotangent.shape, F32), coef, coef, half, half, half, half],
        scratch_shapes=[pltpu.VMEM((bricks, modes, LANES), F32)],
        compiler_params=PARAMS,
    )(cotangent, slope1, slope2, *tabs, *weights, *bands_[2:])


ROWS = ((0,), (0,))
RADIX = 4


def slot(place, owner):
    low = (owner % RADIX - place[1] + RADIX) % RADIX
    high = (owner // RADIX - place[0] + RADIX) % RADIX
    return low * RADIX + high


def weight_kernel(
    scale, place, coef1, coef2, sens1, sens2, x1h, x1l, x2h, x2l, z1h, z1l, z2h, z2l, out_ref
):
    bricks = coef1.shape[0]
    modes = coef1.shape[1] // (2 * J)
    for m in range(modes):
        re, im = slice(2 * J * m, 2 * J * m + J), slice(2 * J * m + J, 2 * J * (m + 1))
        pieces = []
        for coef, sens in ((coef1, sens1), (coef2, sens2)):
            cr, ci, zr, zi = (
                r[:, p].reshape(bricks * J, LANES)
                for r, p in ((coef, re), (coef, im), (sens, re), (sens, im))
            )
            left = jnp.concatenate([cr, ci], axis=0)
            right = jnp.concatenate(
                [jnp.concatenate([zr, zi], axis=1), jnp.concatenate([zi, -zr], axis=1)], axis=0
            )
            product = dot3(split(left), split(right), ROWS) * scale
            for part in range(2):
                pieces.append(
                    sum(
                        product[x * C : (x + 1) * C, part * LANES + x * C : part * LANES + (x + 1) * C]
                        for x in range(XB)
                    )
                )
        out_ref[slot(place, m), :C] = jnp.concatenate(pieces, axis=1)
    lines = 2 * C // modes
    for l, (xh, xl, zh, zl) in enumerate(((x1h, x1l, z1h, z1l), (x2h, x2l, z2h, z2l))):
        total = jnp.zeros((LANES, 2 * LANES), F32)
        for s in range(bricks):
            value = (with_neighbours(xh, s), with_neighbours(xl, s))
            total = total + dot3((zh[s], zl[s]), value, ROWS)
        taps = []
        for j in range(3):
            pairs = [(x, x - j + 1) for x in range(XB) if 0 <= x - j + 1 < XB]
            tap = sum(total[y * C : (y + 1) * C, x * C : (x + 1) * C] for x, y in pairs)
            if j == 0:
                tap = tap + total[:C, LANES + (XB - 1) * C :]
            if j == 2:
                tap = tap + total[(XB - 1) * C :, LANES : LANES + C]
            taps.append(tap)
        wide = jnp.concatenate([*taps, jnp.zeros((C, C), F32)], axis=1)
        for i in range(modes // 2):
            part = wide[i * lines : (i + 1) * lines]
            out_ref[slot(place, l * (modes // 2) + i), C : C + lines] = part
    out_ref[:, C + lines :] = jnp.zeros((modes, out_ref.shape[1] - C - lines, LANES), F32)


def weight_gradients(scale, *operands):
    modes = operands[1].shape[1] // (2 * J)
    return pl.pallas_call(
        functools.partial(weight_kernel, scale),
        in_specs=[pl.BlockSpec(memory_space=pltpu.SMEM)] + [VMEM] * 12,
        out_specs=VMEM,
        out_shape=jax.ShapeDtypeStruct((modes, C + 8, LANES), F32),
        compiler_params=PARAMS,
    )(*operands)


def on_device(input_field, cotangent, spectral_weights, conv_kernel, mode_list):
    groups = lax.axis_size("tm")
    bricks = lax.axis_size("space")
    everyone = ("tm", "space")
    steps = input_field.shape[0]
    total_time = steps * groups
    layers, _, modes, _, _ = spectral_weights.shape
    scale = 2.0 / total_time
    exchange = functools.partial(lax.all_to_all, split_axis=0, concat_axis=0, tiled=True)

    received = exchange(to_blocks(input_field), everyone)
    cot_blocks = to_blocks(cotangent)
    tabs = tables(mode_list, total_time)
    weights = block_weights(spectral_weights, scale)
    bands_ = bands(conv_kernel)
    received, cot_blocks, tabs, weights, bands_ = lax.optimization_barrier(
        (received, cot_blocks, tabs, weights, bands_)
    )
    cot_received = exchange(cot_blocks, everyone)
    shape = (groups, bricks, steps * J, LANES)
    coef1, coef2, slope1, slope2, x1h, x1l, x2h, x2l = forward(
        received.reshape(shape), tabs, weights, bands_
    )
    grad, sens1, sens2, z1h, z1l, z2h, z2l = backward(
        cot_received.reshape(shape), slope1, slope2, tabs, weights, bands_
    )
    returned = exchange(grad.reshape(cot_received.shape), everyone)
    me = lax.axis_index("tm")
    place = jnp.stack([me // RADIX, me % RADIX]).astype(jnp.int32)
    partial = weight_gradients(
        scale, place, coef1, coef2, sens1, sens2, x1h, x1l, x2h, x2l, z1h, z1l, z2h, z2l
    )
    partial = partial.reshape(RADIX, RADIX, *partial.shape[1:])
    partial = shifted_sum(list(partial), "tm", groups, 1)
    partial = shifted_sum(list(partial), "tm", groups, RADIX)
    partial = shifted_sum([partial] * RADIX, "space", bricks, bricks // RADIX)
    total = shifted_sum([partial] * (bricks // RADIX), "space", bricks, 1)
    mode_total = total[:C].reshape(C, layers, 2, 1, C).transpose(1, 2, 3, 0, 4)
    lines = layers * C // groups
    returned, own = lax.optimization_barrier((returned, total[C : C + lines]))
    lined = exchange(jnp.broadcast_to(own[None], (groups, *own.shape)), "tm")
    kernel_total = lined.reshape(layers, C, LANES)[:, :, : 3 * C]
    kernel_total = kernel_total.reshape(layers, C, 3, C).transpose(0, 2, 3, 1)
    return (from_blocks(returned), mode_total, kernel_total)


def shifted_sum(pieces, axis, size, stride):
    count = len(pieces)
    got = [pieces[0]]
    for r in range(1, count):
        perm = []
        for i in range(size):
            digit = i // stride % count
            perm.append((i, i + ((digit + r) % count - digit) * stride))
        got.append(lax.ppermute(pieces[r], axis, perm))
    if count == 2:
        return got[0] + got[1]
    return (got[0] + got[2]) + (got[1] + got[3])


def solution(mesh):
    placed = (P("tm", None, "space", None), P("tm", None, "space", None), P(), P(), P())
    return jax.shard_map(
        on_device,
        mesh=mesh,
        in_specs=placed,
        out_specs=(P("tm", None, "space", None), P(None, None, "tm", None, None), P()),
        check_vma=False,
    )
```

```python
import functools
import math

import jax
import jax.numpy as jnp
from jax import lax
from jax.experimental import pallas as pl
from jax.experimental.pallas import tpu as pltpu
from jax.sharding import PartitionSpec as P

F32 = jnp.float32
BF16 = jnp.bfloat16
LANES = 128
J = 8
XB = 4
C = 32
VMEM = pl.BlockSpec(memory_space=pltpu.VMEM)
ANY = pl.BlockSpec(memory_space=pl.ANY)
HBM = pl.BlockSpec(memory_space=pltpu.HBM)
PARAMS = pltpu.CompilerParams(vmem_limit_bytes=40 * 1024 * 1024)


def in_hbm(*values):
    return [pltpu.with_memory_space_constraint(v, pltpu.HBM) for v in values]


def split(value):
    high = value.astype(BF16)
    low = (value - high.astype(F32)).astype(BF16)
    return high, low


def dot3(left, right, dims=((1,), (0,))):
    (lh, ll), (rh, rl) = left, right
    (lc,), (rc,) = dims
    a = jnp.concatenate([lh, ll, lh], axis=lc)
    b = jnp.concatenate([rh, rh, rl], axis=rc)
    return lax.dot_general(a, b, (dims, ((), ())), preferred_element_type=F32)


def scatter_kernel(field_any, out_any, field, out, load_sem, store_sem):
    steps, _, _, columns = field.shape
    groups = LANES // J
    loads = [
        pltpu.make_async_copy(field_any.at[t], field.at[t], load_sem.at[t]) for t in range(steps)
    ]
    for copy in loads:
        copy.start()
    stores = []
    for q in range(columns // LANES):
        lanes = slice(q * LANES, (q + 1) * LANES)
        part = pl.ds(q * groups, groups)
        for t in range(steps):
            if q == 0:
                loads[t].wait()
            rows = jnp.concatenate([field[t, :, x, lanes] for x in range(XB)], axis=0)
            out[part, t * J : (t + 1) * J] = rows.T.reshape(groups, J, LANES)
        stores.append(pltpu.make_async_copy(out.at[part], out_any.at[part], store_sem.at[q]))
        stores[-1].start()
    for copy in stores:
        copy.wait()


def gather_kernel(blocks_any, out_any, blocks, out, load_sem, store_sem):
    steps, _, _, columns = out.shape
    groups = LANES // J
    count = columns // LANES
    loads = []
    for q in range(count):
        part = pl.ds(q * groups, groups)
        loads.append(pltpu.make_async_copy(blocks_any.at[part], blocks.at[part], load_sem.at[q]))
        loads[-1].start()
    stores = []
    for q in range(count):
        lanes = slice(q * LANES, (q + 1) * LANES)
        loads[q].wait()
        for t in range(steps):
            rows = blocks[q * groups : (q + 1) * groups, t * J : (t + 1) * J]
            rows = rows.reshape(LANES, LANES).T
            for x in range(XB):
                out[t, :, x, lanes] = rows[x * C : (x + 1) * C]
        if q % 2 == 1:
            done = pl.ds((q - 1) * LANES, 2 * LANES)
            stores.append(
                pltpu.make_async_copy(
                    out.at[:, :, :, done], out_any.at[:, :, :, done], store_sem.at[q // 2]
                )
            )
            stores[-1].start()
    for copy in stores:
        copy.wait()


def to_blocks(field):
    steps, _, _, columns = field.shape
    shape = (columns // J, steps * J, LANES)
    return pl.pallas_call(
        scatter_kernel,
        in_specs=[HBM],
        out_specs=HBM,
        out_shape=pltpu.HBM(shape, F32),
        scratch_shapes=[
            pltpu.VMEM(field.shape, F32),
            pltpu.VMEM(shape, F32),
            pltpu.SemaphoreType.DMA((steps,)),
            pltpu.SemaphoreType.DMA((columns // LANES,)),
        ],
        compiler_params=PARAMS,
    )(*in_hbm(field))


def from_blocks(blocks):
    parts, rows, _ = blocks.shape
    shape = (rows // J, C, XB, parts * J)
    count = shape[3] // LANES
    return pl.pallas_call(
        gather_kernel,
        in_specs=[ANY],
        out_specs=HBM,
        out_shape=pltpu.HBM(shape, F32),
        scratch_shapes=[
            pltpu.VMEM(blocks.shape, F32),
            pltpu.VMEM(shape, F32),
            pltpu.SemaphoreType.DMA((count,)),
            pltpu.SemaphoreType.DMA((count // 2,)),
        ],
        compiler_params=PARAMS,
    )(blocks)


def angles(mode_list, total_time):
    steps = jnp.arange(total_time, dtype=jnp.int32)
    phase = (mode_list[:, None] * steps[None, :]) % total_time
    angle = phase.astype(F32) * (2.0 * math.pi / total_time)
    both = jnp.stack([jnp.cos(angle), -jnp.sin(angle)], axis=1)
    return both.reshape(2 * mode_list.shape[0], total_time)


def widened(value):
    rows, cols = value.shape
    spread = lax.broadcasted_iota(jnp.int32, (cols, cols * J), 1) // J
    spread = (spread == lax.broadcasted_iota(jnp.int32, (cols, cols * J), 0)).astype(BF16)
    shape = (rows * J, cols * J)
    same = (
        lax.broadcasted_iota(jnp.int32, shape, 0) % J
        == lax.broadcasted_iota(jnp.int32, shape, 1) % J
    )
    for piece in split(value):
        wide = jnp.dot(piece, spread, preferred_element_type=F32)
        wide = jnp.broadcast_to(wide[:, None, :], (rows, J, cols * J)).reshape(shape)
        yield jnp.where(same, wide, 0.0).astype(BF16)


def band(kernel):
    zero = jnp.zeros((C, C), F32)
    rows = [
        [kernel[x - y + 1] if abs(x - y) <= 1 else zero for y in range(XB)] for x in range(XB)
    ]
    edge = [[zero] * XB for _ in range(XB)]
    edge[XB - 1][0] = kernel[0]
    edge[0][XB - 1] = kernel[2]
    return jnp.concatenate([jnp.concatenate(r, axis=1) for r in rows + edge], axis=0)


def prepare_kernel(scale, tab_ref, tabt_ref, w_ref, k_ref, ah, al, sh, sl, wh, wl, vh, vl, fh, fl, bh, bl):
    ah[...], al[...] = widened(tab_ref[...])
    sh[...], sl[...] = widened(tabt_ref[...])
    for l in range(w_ref.shape[0]):

        def body(m, _):
            re, im = w_ref[l, 0, m] * scale, w_ref[l, 1, m] * scale
            wh[l, m], wl[l, m] = split(jnp.concatenate([re] * XB + [im] * XB, axis=1))
            re, im = re.T, -im.T
            vh[l, m], vl[l, m] = split(jnp.concatenate([re] * XB + [im] * XB, axis=1))
            return 0

        lax.fori_loop(0, w_ref.shape[2], body, 0)
        taps = [k_ref[l, j] for j in range(3)]
        fh[l], fl[l] = split(band(taps))
        bh[l], bl[l] = split(band([t.T for t in taps[::-1]]))


def prepare(scale, spectral_weights, conv_kernel, mode_list, total_time):
    layers, _, modes, channels, _ = spectral_weights.shape
    tab = angles(mode_list, total_time)
    rows, cols = 2 * modes * J, total_time * J
    shapes = [(rows, cols)] * 2 + [(cols, rows)] * 2
    shapes += [(layers, modes, channels, 2 * LANES)] * 4 + [(layers, 2 * LANES, LANES)] * 4
    return pl.pallas_call(
        functools.partial(prepare_kernel, scale),
        in_specs=[VMEM] * 4,
        out_specs=[VMEM] * 12,
        out_shape=[pltpu.HBM(shape, BF16) for shape in shapes],
        compiler_params=PARAMS,
    )(tab, tab.T, spectral_weights, conv_kernel)


def lane_block():
    return lax.broadcasted_iota(jnp.int32, (1, LANES), 1) // C


def put_split(value, s, high_ref, low_ref):
    high, low = split(value)
    high_ref[s] = high
    low_ref[s] = low


def with_neighbours(ref, s):
    own = ref[s]
    x = lane_block()
    zero = jnp.zeros_like(own)
    before = ref[s - 1] if s > 0 else zero
    after = ref[s + 1] if s + 1 < ref.shape[0] else zero
    edge = jnp.where(x == XB - 1, before, jnp.where(x == 0, after, zero))
    return jnp.concatenate([own, edge], axis=1)


def analyse(table, high_ref, low_ref, coef_ref):
    for s in range(0, high_ref.shape[0], 2):
        right = [jnp.concatenate([r[s], r[s + 1]], axis=1) for r in (high_ref, low_ref)]
        result = dot3(table, right)
        coef_ref[s] = result[:, :LANES]
        coef_ref[s + 1] = result[:, LANES:]


def mixing_matrix(w_ref, l, m):
    row = lax.broadcasted_iota(jnp.int32, (LANES, 2 * LANES), 0) // C
    col = lax.broadcasted_iota(jnp.int32, (LANES, 2 * LANES), 1) // C % XB
    wide = jnp.concatenate([w_ref[l, m]] * XB, axis=0)
    top = jnp.where(row == col, wide, jnp.zeros_like(wide))
    return jnp.concatenate(
        [top, jnp.concatenate([-top[:, LANES:], top[:, :LANES]], axis=1)], axis=0
    )


def mix(coef_ref, wh_ref, wl_ref, l, mixed_ref):
    bricks = coef_ref.shape[0]
    for m in range(wh_ref.shape[1]):
        re, im = slice(2 * J * m, 2 * J * m + J), slice(2 * J * m + J, 2 * J * (m + 1))
        value = jnp.concatenate(
            [coef_ref[:, re].reshape(bricks * J, LANES), coef_ref[:, im].reshape(bricks * J, LANES)],
            axis=1,
        )
        matrix = (mixing_matrix(wh_ref, l, m), mixing_matrix(wl_ref, l, m))
        result = dot3(split(value), matrix)
        mixed_ref[:, re] = result[:, :LANES].reshape(bricks, J, LANES)
        mixed_ref[:, im] = result[:, LANES:].reshape(bricks, J, LANES)


def synthesise(table, mixed_ref, bh, bl, high_ref, low_ref, emit):
    for s in range(0, mixed_ref.shape[0], 2):
        right = split(jnp.concatenate([mixed_ref[s], mixed_ref[s + 1]], axis=1))
        spectral = dot3(table, right)
        for o in range(2):
            value = (with_neighbours(high_ref, s + o), with_neighbours(low_ref, s + o))
            total = spectral[:, o * LANES : (o + 1) * LANES] + dot3(value, (bh, bl))
            emit(s + o, total)


def gelu_parts(z):
    cdf = 0.5 * (1.0 + lax.erf(z * math.sqrt(0.5)))
    slope = cdf + z * (jnp.exp(-0.5 * z * z) * (1.0 / math.sqrt(2.0 * math.pi)))
    return z * cdf, slope


def brick(ref, s):
    return ref[:, s].reshape(-1, LANES)


def forward_kernel(
    x_ref, ah, al, sh, sl, wh, wl, bh, bl,
    coef1, coef2, slope1, slope2, x1h, x1l, x2h, x2l, mixed,
):
    bricks = x_ref.shape[1]
    for s in range(bricks):
        put_split(brick(x_ref, s), s, x1h, x1l)
    analysis, synthesis = (ah[...], al[...]), (sh[...], sl[...])

    def first(s, z):
        value, slope = gelu_parts(z)
        slope1[s] = slope
        put_split(value, s, x2h, x2l)

    def second(s, z):
        slope2[s] = gelu_parts(z)[1]

    for l, (h, low, coef, emit) in enumerate(
        ((x1h, x1l, coef1, first), (x2h, x2l, coef2, second))
    ):
        analyse(analysis, h, low, coef)
        mix(coef, wh, wl, l, mixed)
        synthesise(synthesis, mixed, bh[l], bl[l], h, low, emit)


def forward(field, tabs, weights, bands_):
    _, bricks, _, _ = field.shape
    rows = tabs[0].shape[1]
    modes = tabs[0].shape[0]
    coef = pltpu.HBM((bricks, modes, LANES), F32)
    full = pltpu.HBM((bricks, rows, LANES), F32)
    half = pltpu.HBM((bricks, rows, LANES), BF16)
    return pl.pallas_call(
        forward_kernel,
        in_specs=[VMEM] * 9,
        out_specs=[VMEM] * 8,
        out_shape=[coef, coef, full, full, half, half, half, half],
        scratch_shapes=[pltpu.VMEM((bricks, modes, LANES), F32)],
        compiler_params=PARAMS,
    )(field, *in_hbm(*tabs, *weights, *bands_))


def backward_kernel(*refs):
    g_any, slope1_any, slope2_any = refs[:3]
    small_any = refs[3:11]
    out_any, sens1_any, sens2_any = refs[11:14]
    z_any = refs[14:18]
    g, slope1, slope2 = refs[18:21]
    small = refs[21:29]
    sens1, sens2, z1h, z1l, z2h, z2l, out, mixed, load_sem, small_sem, store_sem = refs[29:]
    ah, al, sh, sl, wh, wl, bh, bl = small
    bricks = g.shape[0]
    copy = pltpu.make_async_copy

    loads = [
        (
            copy(g_any.at[:, s], g.at[s], load_sem.at[0, s]),
            copy(slope2_any.at[s], slope2.at[s], load_sem.at[1, s]),
            copy(slope1_any.at[s], slope1.at[s], load_sem.at[2, s]),
        )
        for s in range(bricks)
    ]
    tables = [copy(a, r, small_sem.at[i]) for i, (a, r) in enumerate(zip(small_any, small))]
    for s in range(bricks):
        loads[s][0].start()
        loads[s][1].start()
        if s == 1:
            tables[0].start()
            tables[1].start()
    for i in (4, 5, 2, 3, 6, 7):
        tables[i].start()
    for s in range(bricks):
        loads[s][2].start()

    stores = []

    def store(source, target):
        stores.append(copy(source, target, store_sem.at[len(stores)]))
        stores[-1].start()

    for s in range(bricks):
        loads[s][0].wait()
        loads[s][1].wait()
        put_split(g[s].reshape(-1, LANES) * slope2[s], s, z2h, z2l)
    store(z2h, z_any[2])
    store(z2l, z_any[3])
    for i in (0, 1):
        tables[i].wait()
    analysis = (ah[...], al[...])
    analyse(analysis, z2h, z2l, sens2)
    store(sens2, sens2_any)
    for i in range(2, 8):
        tables[i].wait()
    synthesis = (sh[...], sl[...])

    def second(s, value):
        loads[s][2].wait()
        put_split(value * slope1[s], s, z1h, z1l)

    def first(s, value):
        out[s] = value.reshape(out.shape[1:])
        store(out.at[s], out_any.at[:, s])

    mix(sens2, wh, wl, 1, mixed)
    synthesise(synthesis, mixed, bh[1], bl[1], z2h, z2l, second)
    store(z1h, z_any[0])
    store(z1l, z_any[1])
    analyse(analysis, z1h, z1l, sens1)
    store(sens1, sens1_any)
    mix(sens1, wh, wl, 0, mixed)
    synthesise(synthesis, mixed, bh[0], bl[0], z1h, z1l, first)
    for done in stores:
        done.wait()


def backward(cotangent, slope1, slope2, tabs, weights, bands_):
    groups, bricks, lines, _ = cotangent.shape
    rows = tabs[0].shape[1]
    modes = tabs[0].shape[0]
    coef = ((bricks, modes, LANES), F32)
    half = ((bricks, rows, LANES), BF16)
    brick_shape = ((bricks, groups, lines, LANES), F32)
    outs = [(cotangent.shape, F32), coef, coef, half, half, half, half]
    operands = (cotangent, slope1, slope2, *tabs, *weights, *bands_)
    scratch = [brick_shape] + [(o.shape, o.dtype) for o in operands[1:]]
    scratch += [coef, coef, half, half, half, half, brick_shape, coef]
    return pl.pallas_call(
        backward_kernel,
        in_specs=[ANY] + [HBM] * 10,
        out_specs=[HBM] * 7,
        out_shape=[pltpu.HBM(*o) for o in outs],
        scratch_shapes=[pltpu.VMEM(*o) for o in scratch]
        + [
            pltpu.SemaphoreType.DMA((3, bricks)),
            pltpu.SemaphoreType.DMA((8,)),
            pltpu.SemaphoreType.DMA((6 + bricks,)),
        ],
        compiler_params=PARAMS,
    )(cotangent, *in_hbm(*operands[1:]))


ROWS = ((0,), (0,))
TAPS = 3


def weight_kernel(scale, me_ref, *refs):
    coef1_any, coef2_any, sens1_any, sens2_any = refs[:4]
    half_any = refs[4:12]
    modes = refs[0].shape[1] // (2 * J)
    outs = refs[12 : 12 + modes]
    coef1, coef2, sens1, sens2 = refs[12 + modes : 16 + modes]
    half = refs[16 + modes : 24 + modes]
    spectral, load_sem, half_sem = refs[24 + modes :]
    bricks = coef1.shape[0]
    copy = pltpu.make_async_copy

    halves = [
        [
            copy(a.at[s], r.at[s], half_sem.at[i, s])
            for i, (a, r) in enumerate(zip(half_any, half))
        ]
        for s in range(bricks)
    ]
    pairs = zip((coef1_any, coef2_any, sens1_any, sens2_any), (coef1, coef2, sens1, sens2))
    loads = [copy(a, r, load_sem.at[i]) for i, (a, r) in enumerate(pairs)]
    x1h, x1l, x2h, x2l, z1h, z1l, z2h, z2l = half
    for l in range(2):
        for s in range(bricks):
            for i in (0, 1, 4, 5) if l == 0 else (2, 3, 6, 7):
                halves[s][i].start()
    for c in loads:
        c.start()

    blocks = []
    for l, (xh, xl, zh, zl) in enumerate(((x1h, x1l, z1h, z1l), (x2h, x2l, z2h, z2l))):
        total = jnp.zeros((LANES, 2 * LANES), F32)
        for s in range(bricks):
            for ahead in (0, 1) if s == 0 else (s + 1,):
                if ahead < bricks:
                    for i in (0, 1, 4, 5) if l == 0 else (2, 3, 6, 7):
                        halves[ahead][i].wait()
            value = (with_neighbours(xh, s), with_neighbours(xl, s))
            total = total + dot3((zh[s], zl[s]), value, ROWS)
        for j in range(TAPS):
            pairs = [(x, x - j + 1) for x in range(XB) if 0 <= x - j + 1 < XB]
            tap = sum(total[y * C : (y + 1) * C, x * C : (x + 1) * C] for x, y in pairs)
            if j == 0:
                tap = tap + total[:C, LANES + (XB - 1) * C :]
            if j == 2:
                tap = tap + total[(XB - 1) * C :, LANES : LANES + C]
            blocks.append(tap)
    half_rows = C // 2
    first = jnp.concatenate(blocks[:4], axis=1)
    rest = [b[i * half_rows : (i + 1) * half_rows] for b in blocks[4:] for i in range(2)]
    kernels = jnp.concatenate([first, jnp.concatenate(rest, axis=1)], axis=0)

    for c in loads:
        c.wait()
    for m in range(modes):
        re, im = slice(2 * J * m, 2 * J * m + J), slice(2 * J * m + J, 2 * J * (m + 1))
        pieces = []
        for coef, sens in ((coef1, sens1), (coef2, sens2)):
            cr, ci, zr, zi = (
                r[:, p].reshape(bricks * J, LANES)
                for r, p in ((coef, re), (coef, im), (sens, re), (sens, im))
            )
            left = jnp.concatenate([cr, ci], axis=0)
            right = jnp.concatenate(
                [jnp.concatenate([zr, zi], axis=1), jnp.concatenate([zi, -zr], axis=1)], axis=0
            )
            product = dot3(split(left), split(right), ROWS) * scale
            for part in range(2):
                pieces.append(
                    sum(
                        product[x * C : (x + 1) * C, part * LANES + x * C : part * LANES + (x + 1) * C]
                        for x in range(XB)
                    )
                )
        spectral[m] = jnp.concatenate(pieces, axis=1)
    for r, out in enumerate(outs):
        out[:C] = spectral[(me_ref[0] + r) % modes]
        out[C:] = kernels


def weight_gradients(scale, me, *operands):
    modes = operands[0].shape[1] // (2 * J)
    rows = C + 2 * TAPS * C // XB
    return pl.pallas_call(
        functools.partial(weight_kernel, scale),
        in_specs=[pl.BlockSpec(memory_space=pltpu.SMEM)] + [HBM] * 12,
        out_specs=[VMEM] * modes,
        out_shape=[jax.ShapeDtypeStruct((rows, LANES), F32)] * modes,
        scratch_shapes=[pltpu.VMEM(o.shape, o.dtype) for o in operands]
        + [
            pltpu.VMEM((modes, C, LANES), F32),
            pltpu.SemaphoreType.DMA((4,)),
            pltpu.SemaphoreType.DMA((8, operands[0].shape[0])),
        ],
        compiler_params=PARAMS,
    )(me, *in_hbm(*operands))


def rotate(pieces, axis):
    size = len(pieces)
    return [pieces[0]] + [
        lax.ppermute(pieces[r], axis, [(i, (i + r) % size) for i in range(size)])
        for r in range(1, size)
    ]


def ring_sum_kernel(*refs):
    values = [r[...] for r in refs[:-1]]
    while len(values) > 1:
        half = len(values) // 2
        values = [values[i] + values[i + half] for i in range(half)]
    for i in range(refs[-1].shape[0]):
        refs[-1][i] = values[0]


def ring_sum(pieces, copies):
    return pl.pallas_call(
        ring_sum_kernel,
        in_specs=[VMEM] * len(pieces),
        out_specs=VMEM,
        out_shape=jax.ShapeDtypeStruct((copies, *pieces[0].shape), F32),
        compiler_params=PARAMS,
    )(*pieces)


def finish_kernel(total_ref, mode_ref, kernel_ref):
    total = total_ref[0]
    for i in range(1, total_ref.shape[0]):
        total = total + total_ref[i]
    layers = mode_ref.shape[0]
    for l in range(layers):
        for part in range(2):
            at = (2 * l + part) * C
            mode_ref[l, part, 0] = total[:C, at : at + C]
    low = C // 2
    blocks = [total[C : 2 * C, b * C : (b + 1) * C] for b in range(XB)]
    for b in range(2):
        top, bottom = (total[2 * C :, (2 * b + i) * C : (2 * b + i + 1) * C] for i in range(2))
        blocks.append(jnp.concatenate([top, bottom], axis=0))
    for i, block in enumerate(blocks):
        kernel_ref[i // TAPS, i % TAPS] = block.T


def finish(total, layers):
    return pl.pallas_call(
        finish_kernel,
        in_specs=[VMEM],
        out_specs=[VMEM] * 2,
        out_shape=[
            jax.ShapeDtypeStruct((layers, 2, 1, C, C), F32),
            jax.ShapeDtypeStruct((layers, TAPS, C, C), F32),
        ],
        compiler_params=PARAMS,
    )(total)


def on_device(input_field, cotangent, spectral_weights, conv_kernel, mode_list):
    groups = lax.axis_size("tm")
    bricks = lax.axis_size("space")
    everyone = ("tm", "space")
    steps = input_field.shape[0]
    total_time = steps * groups
    layers, _, modes, _, _ = spectral_weights.shape
    scale = 2.0 / total_time
    exchange = functools.partial(lax.all_to_all, split_axis=0, concat_axis=0, tiled=True)

    received = exchange(to_blocks(input_field), everyone)
    cot_blocks = to_blocks(cotangent)
    prepared = prepare(scale, spectral_weights, conv_kernel, mode_list, total_time)
    received, cot_blocks, prepared = lax.optimization_barrier((received, cot_blocks, prepared))
    tabs = prepared[:4]
    cot_received = exchange(cot_blocks, everyone)
    shape = (groups, bricks, steps * J, LANES)
    coef1, coef2, slope1, slope2, x1h, x1l, x2h, x2l = forward(
        received.reshape(shape), tabs, prepared[4:6], prepared[8:10]
    )
    grad, sens1, sens2, z1h, z1l, z2h, z2l = backward(
        cot_received.reshape(shape), slope1, slope2, tabs, prepared[6:8], prepared[10:]
    )
    returned = exchange(grad.reshape(cot_received.shape), everyone)
    me = lax.axis_index("tm").astype(jnp.int32).reshape(1)
    pieces = weight_gradients(
        scale, me, coef1, coef2, sens1, sens2, x1h, x1l, x2h, x2l, z1h, z1l, z2h, z2l
    )
    spread = ring_sum(rotate(pieces, "tm"), bricks)
    returned, spread = lax.optimization_barrier((returned, spread))
    mode_total, kernel_total = finish(exchange(spread, "space"), layers)
    return (from_blocks(returned), mode_total, kernel_total)


def solution(mesh):
    placed = (P("tm", None, "space", None), P("tm", None, "space", None), P(), P(), P())
    return jax.shard_map(
        on_device,
        mesh=mesh,
        in_specs=placed,
        out_specs=(P("tm", None, "space", None), P(None, None, "tm", None, None), P()),
        check_vma=False,
    )
```

```python
import functools
import math

import jax
import jax.numpy as jnp
from jax import lax
from jax.experimental import pallas as pl
from jax.experimental.pallas import tpu as pltpu
from jax.sharding import PartitionSpec as P

F32 = jnp.float32
BF16 = jnp.bfloat16
LANES = 128
J = 8
XB = 4
C = 32
VMEM = pl.BlockSpec(memory_space=pltpu.VMEM)
ANY = pl.BlockSpec(memory_space=pl.ANY)
HBM = pl.BlockSpec(memory_space=pltpu.HBM)
PARAMS = pltpu.CompilerParams(vmem_limit_bytes=40 * 1024 * 1024)


def in_hbm(*values):
    return [pltpu.with_memory_space_constraint(v, pltpu.HBM) for v in values]


def split(value):
    high = value.astype(BF16)
    low = (value - high.astype(F32)).astype(BF16)
    return high, low


def dot3(left, right, dims=((1,), (0,))):
    (lh, ll), (rh, rl) = left, right
    (lc,), (rc,) = dims
    a = jnp.concatenate([lh, ll, lh], axis=lc)
    b = jnp.concatenate([rh, rh, rl], axis=rc)
    return lax.dot_general(a, b, (dims, ((), ())), preferred_element_type=F32)


def scatter_kernel(field_any, out_any, field, out, load_sem, store_sem):
    steps, _, _, columns = field.shape
    groups = LANES // J
    loads = [
        pltpu.make_async_copy(field_any.at[t], field.at[t], load_sem.at[t]) for t in range(steps)
    ]
    for copy in loads:
        copy.start()
    stores = []
    for q in range(columns // LANES):
        lanes = slice(q * LANES, (q + 1) * LANES)
        part = pl.ds(q * groups, groups)
        for t in range(steps):
            if q == 0:
                loads[t].wait()
            rows = jnp.concatenate([field[t, :, x, lanes] for x in range(XB)], axis=0)
            out[part, t * J : (t + 1) * J] = rows.T.reshape(groups, J, LANES)
        stores.append(pltpu.make_async_copy(out.at[part], out_any.at[part], store_sem.at[q]))
        stores[-1].start()
    for copy in stores:
        copy.wait()


def gather_kernel(blocks_any, out_any, blocks, out, load_sem, store_sem):
    steps, _, _, columns = out.shape
    groups = LANES // J
    count = columns // LANES
    loads = []
    for q in range(count):
        part = pl.ds(q * groups, groups)
        loads.append(pltpu.make_async_copy(blocks_any.at[part], blocks.at[part], load_sem.at[q]))
        loads[-1].start()
    stores = []
    for q in range(count):
        lanes = slice(q * LANES, (q + 1) * LANES)
        loads[q].wait()
        for t in range(steps):
            rows = blocks[q * groups : (q + 1) * groups, t * J : (t + 1) * J]
            rows = rows.reshape(LANES, LANES).T
            for x in range(XB):
                out[t, :, x, lanes] = rows[x * C : (x + 1) * C]
        if q % 2 == 1:
            done = pl.ds((q - 1) * LANES, 2 * LANES)
            stores.append(
                pltpu.make_async_copy(
                    out.at[:, :, :, done], out_any.at[:, :, :, done], store_sem.at[q // 2]
                )
            )
            stores[-1].start()
    for copy in stores:
        copy.wait()


def to_blocks(field):
    steps, _, _, columns = field.shape
    shape = (columns // J, steps * J, LANES)
    return pl.pallas_call(
        scatter_kernel,
        in_specs=[HBM],
        out_specs=HBM,
        out_shape=pltpu.HBM(shape, F32),
        scratch_shapes=[
            pltpu.VMEM(field.shape, F32),
            pltpu.VMEM(shape, F32),
            pltpu.SemaphoreType.DMA((steps,)),
            pltpu.SemaphoreType.DMA((columns // LANES,)),
        ],
        compiler_params=PARAMS,
    )(*in_hbm(field))


def from_blocks(blocks):
    parts, rows, _ = blocks.shape
    shape = (rows // J, C, XB, parts * J)
    count = shape[3] // LANES
    return pl.pallas_call(
        gather_kernel,
        in_specs=[ANY],
        out_specs=HBM,
        out_shape=pltpu.HBM(shape, F32),
        scratch_shapes=[
            pltpu.VMEM(blocks.shape, F32),
            pltpu.VMEM(shape, F32),
            pltpu.SemaphoreType.DMA((count,)),
            pltpu.SemaphoreType.DMA((count // 2,)),
        ],
        compiler_params=PARAMS,
    )(blocks)


def angles(mode_list, total_time):
    steps = jnp.arange(total_time, dtype=jnp.int32)
    phase = (mode_list[:, None] * steps[None, :]) % total_time
    angle = phase.astype(F32) * (2.0 * math.pi / total_time)
    both = jnp.stack([jnp.cos(angle), -jnp.sin(angle)], axis=1)
    return both.reshape(2 * mode_list.shape[0], total_time)


def widened(value):
    rows, cols = value.shape
    spread = lax.broadcasted_iota(jnp.int32, (cols, cols * J), 1) // J
    spread = (spread == lax.broadcasted_iota(jnp.int32, (cols, cols * J), 0)).astype(BF16)
    shape = (rows * J, cols * J)
    same = (
        lax.broadcasted_iota(jnp.int32, shape, 0) % J
        == lax.broadcasted_iota(jnp.int32, shape, 1) % J
    )
    for piece in split(value):
        wide = jnp.dot(piece, spread, preferred_element_type=F32)
        wide = jnp.broadcast_to(wide[:, None, :], (rows, J, cols * J)).reshape(shape)
        yield jnp.where(same, wide, 0.0).astype(BF16)


def blocks_of(kernel, places, cols):
    zero = jnp.zeros((C, C), F32)
    rows = [
        jnp.concatenate([kernel[p[y]] if y in p else zero for y in range(cols)], axis=1)
        for p in places
    ]
    return jnp.concatenate(rows, axis=0)


def band(kernel):
    cells = 2 * XB
    own = [{y: x - y + 1 for y in range(cells) if abs(x - y) <= 1} for x in range(cells)]
    before, after = {0: 0}, {cells - 1: 2}
    own = split(blocks_of(kernel, own, cells))
    both = split(blocks_of(kernel, [after, before, after, before], cells))
    edge = split(blocks_of(kernel, [after, {}, {}, before], cells))
    return jnp.concatenate([own[0], own[0], own[1], both[0], edge[1]], axis=0)


def prepare_kernel(scale, tab_ref, tabt_ref, w_ref, k_ref, ah, al, sh, sl, wh, wl, vh, vl, fb, bb):
    ah[...], al[...] = widened(tab_ref[...])
    sh[...], sl[...] = widened(tabt_ref[...])
    for l in range(w_ref.shape[0]):

        def body(m, _):
            re, im = w_ref[l, 0, m] * scale, w_ref[l, 1, m] * scale
            wh[l, m], wl[l, m] = split(jnp.concatenate([re] * XB + [im] * XB, axis=1))
            re, im = re.T, -im.T
            vh[l, m], vl[l, m] = split(jnp.concatenate([re] * XB + [im] * XB, axis=1))
            return 0

        lax.fori_loop(0, w_ref.shape[2], body, 0)
        taps = [k_ref[l, j] for j in range(3)]
        fb[l] = band(taps)
        bb[l] = band([t.T for t in taps[::-1]])


def prepare(scale, spectral_weights, conv_kernel, mode_list, total_time):
    layers, _, modes, channels, _ = spectral_weights.shape
    tab = angles(mode_list, total_time)
    rows, cols = 2 * modes * J, total_time * J
    shapes = [(rows, cols)] * 2 + [(cols, rows)] * 2
    shapes += [(layers, modes, channels, 2 * LANES)] * 4 + [(layers, 8 * LANES, 2 * LANES)] * 2
    return pl.pallas_call(
        functools.partial(prepare_kernel, scale),
        in_specs=[VMEM] * 4,
        out_specs=[VMEM] * 10,
        out_shape=[pltpu.HBM(shape, BF16) for shape in shapes],
        compiler_params=PARAMS,
    )(tab, tab.T, spectral_weights, conv_kernel)


def lane_block():
    return lax.broadcasted_iota(jnp.int32, (1, LANES), 1) // C


def put_split(value, s, high_ref, low_ref):
    high, low = split(value)
    high_ref[s] = high
    low_ref[s] = low


def with_neighbours(ref, s):
    own = ref[s]
    x = lane_block()
    zero = jnp.zeros_like(own)
    before = ref[s - 1] if s > 0 else zero
    after = ref[s + 1] if s + 1 < ref.shape[0] else zero
    edge = jnp.where(x == XB - 1, before, jnp.where(x == 0, after, zero))
    return jnp.concatenate([own, edge], axis=1)


def pair_operand(high_ref, low_ref, s):
    x = lane_block()
    bricks = high_ref.shape[0]

    def edges(ref):
        zero = jnp.zeros_like(ref[s])
        before = ref[s - 1] if s > 0 else zero
        after = ref[s + 2] if s + 2 < bricks else zero
        return jnp.where(x == XB - 1, before, jnp.where(x == 0, after, zero))

    high = [high_ref[s], high_ref[s + 1]]
    low = [low_ref[s], low_ref[s + 1]]
    edge, edge_low = edges(high_ref), edges(low_ref)
    half = LANES // 2
    swapped = jnp.concatenate([edge_low[:, half:], edge_low[:, :half]], axis=1)
    both = jnp.where((x == 0) | (x == XB - 1), edge, swapped)
    return jnp.concatenate([*high, *low, *high, both, edge], axis=1)


def analyse_pair(table, high_ref, low_ref, coef_ref, s):
    right = [jnp.concatenate([r[s], r[s + 1]], axis=1) for r in (high_ref, low_ref)]
    result = dot3(table, right)
    coef_ref[s] = result[:, :LANES]
    coef_ref[s + 1] = result[:, LANES:]


def analyse(table, high_ref, low_ref, coef_ref):
    for s in range(0, high_ref.shape[0], 2):
        analyse_pair(table, high_ref, low_ref, coef_ref, s)


def mixing_matrix(w_ref, l, m):
    row = lax.broadcasted_iota(jnp.int32, (LANES, 2 * LANES), 0) // C
    col = lax.broadcasted_iota(jnp.int32, (LANES, 2 * LANES), 1) // C % XB
    wide = jnp.concatenate([w_ref[l, m]] * XB, axis=0)
    top = jnp.where(row == col, wide, jnp.zeros_like(wide))
    return jnp.concatenate(
        [top, jnp.concatenate([-top[:, LANES:], top[:, :LANES]], axis=1)], axis=0
    )


def mix(coef_ref, wh_ref, wl_ref, l, mixed_ref):
    bricks = coef_ref.shape[0]
    for m in range(wh_ref.shape[1]):
        re, im = slice(2 * J * m, 2 * J * m + J), slice(2 * J * m + J, 2 * J * (m + 1))
        value = jnp.concatenate(
            [coef_ref[:, re].reshape(bricks * J, LANES), coef_ref[:, im].reshape(bricks * J, LANES)],
            axis=1,
        )
        matrix = (mixing_matrix(wh_ref, l, m), mixing_matrix(wl_ref, l, m))
        result = dot3(split(value), matrix)
        mixed_ref[:, re] = result[:, :LANES].reshape(bricks, J, LANES)
        mixed_ref[:, im] = result[:, LANES:].reshape(bricks, J, LANES)


def synthesise(table, mixed_ref, matrix, high_ref, low_ref, emit):
    for s in range(0, mixed_ref.shape[0], 2):
        right = split(jnp.concatenate([mixed_ref[s], mixed_ref[s + 1]], axis=1))
        total = dot3(table, right) + jnp.dot(
            pair_operand(high_ref, low_ref, s), matrix, preferred_element_type=F32
        )
        emit(s, total[:, :LANES])
        emit(s + 1, total[:, LANES:])


def gelu_parts(z):
    cdf = 0.5 * (1.0 + lax.erf(z * math.sqrt(0.5)))
    slope = cdf + z * (jnp.exp(-0.5 * z * z) * (1.0 / math.sqrt(2.0 * math.pi)))
    return z * cdf, slope


def brick(ref, s):
    return ref[:, s].reshape(-1, LANES)


def forward_kernel(
    x_ref, ah, al, sh, sl, wh, wl, fb,
    coef1, coef2, slope1, slope2, x1h, x1l, x2h, x2l, mixed,
):
    bricks = x_ref.shape[1]
    for s in range(bricks):
        put_split(brick(x_ref, s), s, x1h, x1l)
    analysis, synthesis = (ah[...], al[...]), (sh[...], sl[...])

    def first(s, z):
        value, slope = gelu_parts(z)
        slope1[s] = slope
        put_split(value, s, x2h, x2l)

    def second(s, z):
        slope2[s] = gelu_parts(z)[1]

    for l, (h, low, coef, emit) in enumerate(
        ((x1h, x1l, coef1, first), (x2h, x2l, coef2, second))
    ):
        analyse(analysis, h, low, coef)
        mix(coef, wh, wl, l, mixed)
        synthesise(synthesis, mixed, fb[l], h, low, emit)


def forward(field, tabs, weights, bands_):
    _, bricks, _, _ = field.shape
    rows = tabs[0].shape[1]
    modes = tabs[0].shape[0]
    coef = pltpu.HBM((bricks, modes, LANES), F32)
    full = pltpu.HBM((bricks, rows, LANES), F32)
    half = pltpu.HBM((bricks, rows, LANES), BF16)
    return pl.pallas_call(
        forward_kernel,
        in_specs=[VMEM] * 8,
        out_specs=[VMEM] * 8,
        out_shape=[coef, coef, full, full, half, half, half, half],
        scratch_shapes=[pltpu.VMEM((bricks, modes, LANES), F32)],
        compiler_params=PARAMS,
    )(field, *in_hbm(*tabs, *weights, *bands_))


def backward_kernel(*refs):
    g_any, slope1_any, slope2_any = refs[:3]
    small_any = refs[3:10]
    out_any, sens1_any, sens2_any = refs[10:13]
    z_any = refs[13:17]
    g, slope1, slope2 = refs[17:20]
    small = refs[20:27]
    sens1, sens2, z1h, z1l, z2h, z2l, out, mixed, load_sem, small_sem, store_sem = refs[27:]
    ah, al, sh, sl, wh, wl, bb = small
    bricks = g.shape[0]
    copy = pltpu.make_async_copy

    loads = [
        (
            copy(g_any.at[:, s], g.at[s], load_sem.at[0, s]),
            copy(slope2_any.at[s], slope2.at[s], load_sem.at[1, s]),
            copy(slope1_any.at[s], slope1.at[s], load_sem.at[2, s]),
        )
        for s in range(bricks)
    ]
    tables = [copy(a, r, small_sem.at[i]) for i, (a, r) in enumerate(zip(small_any, small))]
    for s in range(bricks):
        loads[s][0].start()
        loads[s][1].start()
        if s == 1:
            tables[0].start()
            tables[1].start()
    for i in (4, 5, 2, 3, 6):
        tables[i].start()
    for s in range(bricks):
        loads[s][2].start()

    stores = []

    def store(source, target):
        stores.append(copy(source, target, store_sem.at[len(stores)]))
        stores[-1].start()

    for s in range(0, bricks, 2):
        for o in (s, s + 1):
            loads[o][0].wait()
            loads[o][1].wait()
        if s == 0:
            tables[0].wait()
            tables[1].wait()
        for o in (s, s + 1):
            put_split(g[o].reshape(-1, LANES) * slope2[o], o, z2h, z2l)
        analyse_pair((ah[...], al[...]), z2h, z2l, sens2, s)
    store(z2h, z_any[2])
    store(z2l, z_any[3])
    store(sens2, sens2_any)
    for i in range(2, 7):
        tables[i].wait()
    analysis, synthesis = (ah[...], al[...]), (sh[...], sl[...])

    def second(s, value):
        loads[s][2].wait()
        put_split(value * slope1[s], s, z1h, z1l)

    def first(s, value):
        out[s] = value.reshape(out.shape[1:])
        store(out.at[s], out_any.at[:, s])

    mix(sens2, wh, wl, 1, mixed)
    synthesise(synthesis, mixed, bb[1], z2h, z2l, second)
    store(z1h, z_any[0])
    store(z1l, z_any[1])
    analyse(analysis, z1h, z1l, sens1)
    store(sens1, sens1_any)
    mix(sens1, wh, wl, 0, mixed)
    synthesise(synthesis, mixed, bb[0], z1h, z1l, first)
    for done in stores:
        done.wait()


def backward(cotangent, slope1, slope2, tabs, weights, bands_):
    groups, bricks, lines, _ = cotangent.shape
    rows = tabs[0].shape[1]
    modes = tabs[0].shape[0]
    coef = ((bricks, modes, LANES), F32)
    half = ((bricks, rows, LANES), BF16)
    brick_shape = ((bricks, groups, lines, LANES), F32)
    outs = [(cotangent.shape, F32), coef, coef, half, half, half, half]
    operands = (cotangent, slope1, slope2, *tabs, *weights, *bands_)
    scratch = [brick_shape] + [(o.shape, o.dtype) for o in operands[1:]]
    scratch += [coef, coef, half, half, half, half, brick_shape, coef]
    return pl.pallas_call(
        backward_kernel,
        in_specs=[ANY] + [HBM] * 9,
        out_specs=[HBM] * 7,
        out_shape=[pltpu.HBM(*o) for o in outs],
        scratch_shapes=[pltpu.VMEM(*o) for o in scratch]
        + [
            pltpu.SemaphoreType.DMA((3, bricks)),
            pltpu.SemaphoreType.DMA((7,)),
            pltpu.SemaphoreType.DMA((6 + bricks,)),
        ],
        compiler_params=PARAMS,
    )(cotangent, *in_hbm(*operands[1:]))


ROWS = ((0,), (0,))
TAPS = 3
RADIX = 4


def weight_kernel(scale, me_ref, *refs):
    coef1_any, coef2_any, sens1_any, sens2_any = refs[:4]
    half_any = refs[4:12]
    modes = refs[0].shape[1] // (2 * J)
    outs = refs[12 : 12 + RADIX]
    coef1, coef2, sens1, sens2 = refs[12 + RADIX : 16 + RADIX]
    half = refs[16 + RADIX : 24 + RADIX]
    spectral, load_sem, half_sem = refs[24 + RADIX :]
    bricks = coef1.shape[0]
    copy = pltpu.make_async_copy

    halves = [
        [
            copy(a.at[s], r.at[s], half_sem.at[i, s])
            for i, (a, r) in enumerate(zip(half_any, half))
        ]
        for s in range(bricks)
    ]
    pairs = zip((coef1_any, coef2_any, sens1_any, sens2_any), (coef1, coef2, sens1, sens2))
    loads = [copy(a, r, load_sem.at[i]) for i, (a, r) in enumerate(pairs)]
    x1h, x1l, x2h, x2l, z1h, z1l, z2h, z2l = half
    for l in range(2):
        for s in range(bricks):
            for i in (0, 1, 4, 5) if l == 0 else (2, 3, 6, 7):
                halves[s][i].start()
    for c in loads:
        c.start()

    blocks = []
    for l, (xh, xl, zh, zl) in enumerate(((x1h, x1l, z1h, z1l), (x2h, x2l, z2h, z2l))):
        total = jnp.zeros((LANES, 2 * LANES), F32)
        for s in range(bricks):
            for ahead in (0, 1) if s == 0 else (s + 1,):
                if ahead < bricks:
                    for i in (0, 1, 4, 5) if l == 0 else (2, 3, 6, 7):
                        halves[ahead][i].wait()
            value = (with_neighbours(xh, s), with_neighbours(xl, s))
            total = total + dot3((zh[s], zl[s]), value, ROWS)
        for j in range(TAPS):
            pairs = [(x, x - j + 1) for x in range(XB) if 0 <= x - j + 1 < XB]
            tap = sum(total[y * C : (y + 1) * C, x * C : (x + 1) * C] for x, y in pairs)
            if j == 0:
                tap = tap + total[:C, LANES + (XB - 1) * C :]
            if j == 2:
                tap = tap + total[(XB - 1) * C :, LANES : LANES + C]
            blocks.append(tap)
    half_rows = C // 2
    first = jnp.concatenate(blocks[:4], axis=1)
    rest = [b[i * half_rows : (i + 1) * half_rows] for b in blocks[4:] for i in range(2)]
    kernels = jnp.concatenate([first, jnp.concatenate(rest, axis=1)], axis=0)

    for c in loads:
        c.wait()
    for m in range(modes):
        re, im = slice(2 * J * m, 2 * J * m + J), slice(2 * J * m + J, 2 * J * (m + 1))
        pieces = []
        for coef, sens in ((coef1, sens1), (coef2, sens2)):
            cr, ci, zr, zi = (
                r[:, p].reshape(bricks * J, LANES)
                for r, p in ((coef, re), (coef, im), (sens, re), (sens, im))
            )
            left = jnp.concatenate([cr, ci], axis=0)
            right = jnp.concatenate(
                [jnp.concatenate([zr, zi], axis=1), jnp.concatenate([zi, -zr], axis=1)], axis=0
            )
            product = dot3(split(left), split(right), ROWS) * scale
            for part in range(2):
                pieces.append(
                    sum(
                        product[x * C : (x + 1) * C, part * LANES + x * C : part * LANES + (x + 1) * C]
                        for x in range(XB)
                    )
                )
        spectral[m] = jnp.concatenate(pieces, axis=1)
    for r, out in enumerate(outs):
        high = (me_ref[0] + r) % RADIX
        for q in range(RADIX):
            low = (me_ref[1] + q) % RADIX
            out[q * C : (q + 1) * C] = spectral[high * RADIX + low]
        out[RADIX * C :] = kernels


def weight_gradients(scale, me, *operands):
    modes = operands[0].shape[1] // (2 * J)
    rows = RADIX * C + 2 * TAPS * C // XB
    return pl.pallas_call(
        functools.partial(weight_kernel, scale),
        in_specs=[pl.BlockSpec(memory_space=pltpu.SMEM)] + [HBM] * 12,
        out_specs=[VMEM] * RADIX,
        out_shape=[jax.ShapeDtypeStruct((rows, LANES), F32)] * RADIX,
        scratch_shapes=[pltpu.VMEM(o.shape, o.dtype) for o in operands]
        + [
            pltpu.VMEM((modes, C, LANES), F32),
            pltpu.SemaphoreType.DMA((4,)),
            pltpu.SemaphoreType.DMA((8, operands[0].shape[0])),
        ],
        compiler_params=PARAMS,
    )(me, *in_hbm(*operands))


def shifted(pieces, axis, size, stride):
    count = len(pieces)
    got = [pieces[0]]
    for r in range(1, count):
        perm = []
        for i in range(size):
            digit = i // stride % count
            perm.append((i, i + ((digit + r) % count - digit) * stride))
        got.append(lax.ppermute(pieces[r], axis, perm))
    return got


def ring_sum(values):
    while len(values) > 1:
        half = len(values) // 2
        values = [values[i] + values[i + half] for i in range(half)]
    return values[0]


def split_sum_kernel(*refs):
    total = ring_sum([r[...] for r in refs[:RADIX]])
    for q, out in enumerate(refs[RADIX:]):
        out[:C] = total[q * C : (q + 1) * C]
        out[C:] = total[RADIX * C :]


def split_sum(pieces):
    rows = pieces[0].shape[0] - (RADIX - 1) * C
    return pl.pallas_call(
        split_sum_kernel,
        in_specs=[VMEM] * RADIX,
        out_specs=[VMEM] * RADIX,
        out_shape=[jax.ShapeDtypeStruct((rows, LANES), F32)] * RADIX,
        compiler_params=PARAMS,
    )(*pieces)


def finish_kernel(one_ref, other_ref, mode_ref, kernel_ref):
    total = one_ref[...] + other_ref[...]
    layers = mode_ref.shape[0]
    for l in range(layers):
        for part in range(2):
            at = (2 * l + part) * C
            mode_ref[l, part, 0] = total[:C, at : at + C]
    low = C // 2
    blocks = [total[C : 2 * C, b * C : (b + 1) * C] for b in range(XB)]
    for b in range(2):
        top, bottom = (total[2 * C :, (2 * b + i) * C : (2 * b + i + 1) * C] for i in range(2))
        blocks.append(jnp.concatenate([top, bottom], axis=0))
    for i, block in enumerate(blocks):
        kernel_ref[i // TAPS, i % TAPS] = block.T


def finish(one, other, layers):
    return pl.pallas_call(
        finish_kernel,
        in_specs=[VMEM] * 2,
        out_specs=[VMEM] * 2,
        out_shape=[
            jax.ShapeDtypeStruct((layers, 2, 1, C, C), F32),
            jax.ShapeDtypeStruct((layers, TAPS, C, C), F32),
        ],
        compiler_params=PARAMS,
    )(one, other)


def on_device(input_field, cotangent, spectral_weights, conv_kernel, mode_list):
    groups = lax.axis_size("tm")
    bricks = lax.axis_size("space")
    everyone = ("tm", "space")
    steps = input_field.shape[0]
    total_time = steps * groups
    layers, _, modes, _, _ = spectral_weights.shape
    scale = 2.0 / total_time
    exchange = functools.partial(lax.all_to_all, split_axis=0, concat_axis=0, tiled=True)

    received = exchange(to_blocks(input_field), everyone)
    cot_blocks = to_blocks(cotangent)
    prepared = prepare(scale, spectral_weights, conv_kernel, mode_list, total_time)
    received, cot_blocks, prepared = lax.optimization_barrier((received, cot_blocks, prepared))
    tabs = prepared[:4]
    cot_received = exchange(cot_blocks, everyone)
    shape = (groups, bricks, steps * J, LANES)
    coef1, coef2, slope1, slope2, x1h, x1l, x2h, x2l = forward(
        received.reshape(shape), tabs, prepared[4:6], prepared[8:9]
    )
    grad, sens1, sens2, z1h, z1l, z2h, z2l = backward(
        cot_received.reshape(shape), slope1, slope2, tabs, prepared[6:8], prepared[9:]
    )
    returned = exchange(grad.reshape(cot_received.shape), everyone)
    me = lax.axis_index("tm").astype(jnp.int32)
    place = jnp.stack([me // RADIX, me % RADIX])
    pieces = weight_gradients(
        scale, place, coef1, coef2, sens1, sens2, x1h, x1l, x2h, x2l, z1h, z1l, z2h, z2l
    )
    pieces = split_sum(shifted(pieces, "tm", groups, RADIX))
    grad_input, pieces = lax.optimization_barrier(
        (from_blocks(returned), shifted(pieces, "tm", groups, 1))
    )
    total = ring_sum(pieces)
    total = ring_sum(shifted([total] * RADIX, "space", bricks, bricks // RADIX))
    mode_total, kernel_total = finish(*shifted([total] * 2, "space", bricks, 1), layers)
    return (grad_input, mode_total, kernel_total)


def solution(mesh):
    placed = (P("tm", None, "space", None), P("tm", None, "space", None), P(), P(), P())
    return jax.shard_map(
        on_device,
        mesh=mesh,
        in_specs=placed,
        out_specs=(P("tm", None, "space", None), P(None, None, "tm", None, None), P()),
        check_vma=False,
    )
```

```python
import functools
import math

import jax
import jax.numpy as jnp
from jax import lax
from jax.experimental import pallas as pl
from jax.experimental.pallas import tpu as pltpu
from jax.sharding import PartitionSpec as P

F32 = jnp.float32
BF16 = jnp.bfloat16
LANES = 128
J = 8
XB = 4
C = 32
VMEM = pl.BlockSpec(memory_space=pltpu.VMEM)
ANY = pl.BlockSpec(memory_space=pl.ANY)
HBM = pl.BlockSpec(memory_space=pltpu.HBM)
PARAMS = pltpu.CompilerParams(vmem_limit_bytes=40 * 1024 * 1024)


def in_hbm(*values):
    return [pltpu.with_memory_space_constraint(v, pltpu.HBM) for v in values]


def split(value):
    high = value.astype(BF16)
    low = (value - high.astype(F32)).astype(BF16)
    return high, low


def dot3(left, right, dims=((1,), (0,))):
    (lh, ll), (rh, rl) = left, right
    (lc,), (rc,) = dims
    a = jnp.concatenate([lh, ll, lh], axis=lc)
    b = jnp.concatenate([rh, rh, rl], axis=rc)
    return lax.dot_general(a, b, (dims, ((), ())), preferred_element_type=F32)


FETCHED = 1
SENT = 4


def scatter_kernel(field_any, out_any, field, out, load_sem, store_sem):
    _, steps, _, columns = field.shape
    groups = LANES // J
    loads = []
    for x in range(XB):
        loads.append(
            pltpu.make_async_copy(field_any.at[:, :, x, :], field.at[x], load_sem.at[x])
        )
        loads[-1].start()
    for load in loads:
        load.wait()
    stores = []
    count = columns // LANES
    for q in range(count):
        lanes = slice(q * LANES, (q + 1) * LANES)
        for t in range(steps):
            rows = jnp.concatenate([field[x, t, :, lanes] for x in range(XB)], axis=0)
            rows = rows.T.reshape(groups, J, LANES)
            out[q * groups : (q + 1) * groups, t * J : (t + 1) * J] = rows
        if (q + 1) % (count // SENT) == 0:
            size = groups * count // SENT
            part = pl.ds((q + 1) * groups - size, size)
            sem = store_sem.at[len(stores)]
            stores.append(pltpu.make_async_copy(out.at[part], out_any.at[part], sem))
            stores[-1].start()
    for store in stores:
        store.wait()


def gather_kernel(blocks_any, out_any, blocks, out, load_sem, store_sem):
    steps, _, _, columns = out.shape
    groups = LANES // J
    count = columns // LANES
    loads = []
    for i in range(FETCHED):
        part = pl.ds(i * groups * count // FETCHED, groups * count // FETCHED)
        loads.append(pltpu.make_async_copy(blocks_any.at[part], blocks.at[part], load_sem.at[i]))
        loads[-1].start()
    stores = []
    for t in range(steps):
        for q in range(count):
            lanes = slice(q * LANES, (q + 1) * LANES)
            if t == 0 and q % (count // FETCHED) == 0:
                loads[q // (count // FETCHED)].wait()
            rows = blocks[q * groups : (q + 1) * groups, t * J : (t + 1) * J]
            rows = rows.reshape(LANES, LANES).T
            for x in range(XB):
                out[t, :, x, lanes] = rows[x * C : (x + 1) * C]
        if (t + 1) % (steps // SENT) == 0:
            part = pl.ds(t + 1 - steps // SENT, steps // SENT)
            sem = store_sem.at[len(stores)]
            stores.append(pltpu.make_async_copy(out.at[part], out_any.at[part], sem))
            stores[-1].start()
    for store in stores:
        store.wait()


def to_blocks(field):
    steps, _, _, columns = field.shape
    shape = (columns // J, steps * J, LANES)
    return pl.pallas_call(
        scatter_kernel,
        in_specs=[HBM],
        out_specs=HBM,
        out_shape=pltpu.HBM(shape, F32),
        scratch_shapes=[
            pltpu.VMEM((XB, steps, C, columns), F32),
            pltpu.VMEM(shape, F32),
            pltpu.SemaphoreType.DMA((XB,)),
            pltpu.SemaphoreType.DMA((SENT,)),
        ],
        compiler_params=PARAMS,
    )(*in_hbm(field))


def from_blocks(blocks):
    parts, rows, _ = blocks.shape
    shape = (rows // J, C, XB, parts * J)
    return pl.pallas_call(
        gather_kernel,
        in_specs=[ANY],
        out_specs=HBM,
        out_shape=pltpu.HBM(shape, F32),
        scratch_shapes=[
            pltpu.VMEM(blocks.shape, F32),
            pltpu.VMEM(shape, F32),
            pltpu.SemaphoreType.DMA((FETCHED,)),
            pltpu.SemaphoreType.DMA((SENT,)),
        ],
        compiler_params=PARAMS,
    )(blocks)


def angles(mode_list, total_time):
    steps = jnp.arange(total_time, dtype=jnp.int32)
    phase = (mode_list[:, None] * steps[None, :]) % total_time
    angle = phase.astype(F32) * (2.0 * math.pi / total_time)
    both = jnp.stack([jnp.cos(angle), -jnp.sin(angle)], axis=1)
    return both.reshape(2 * mode_list.shape[0], total_time)


def widened(value):
    rows, cols = value.shape
    spread = lax.broadcasted_iota(jnp.int32, (cols, cols * J), 1) // J
    spread = (spread == lax.broadcasted_iota(jnp.int32, (cols, cols * J), 0)).astype(BF16)
    shape = (rows * J, cols * J)
    same = (
        lax.broadcasted_iota(jnp.int32, shape, 0) % J
        == lax.broadcasted_iota(jnp.int32, shape, 1) % J
    )
    for piece in split(value):
        wide = jnp.dot(piece, spread, preferred_element_type=F32)
        wide = jnp.broadcast_to(wide[:, None, :], (rows, J, cols * J)).reshape(shape)
        yield jnp.where(same, wide, 0.0).astype(BF16)


def blocks_of(kernel, places, cols):
    zero = jnp.zeros((C, C), F32)
    rows = [
        jnp.concatenate([kernel[p[y]] if y in p else zero for y in range(cols)], axis=1)
        for p in places
    ]
    return jnp.concatenate(rows, axis=0)


def band(kernel):
    cells = 2 * XB
    own = [{y: x - y + 1 for y in range(cells) if abs(x - y) <= 1} for x in range(cells)]
    before, after = {0: 0}, {cells - 1: 2}
    own = split(blocks_of(kernel, own, cells))
    both = split(blocks_of(kernel, [after, before, after, before], cells))
    edge = split(blocks_of(kernel, [after, {}, {}, before], cells))
    return jnp.concatenate([own[0], own[0], own[1], both[0], edge[1]], axis=0)


def prepare_kernel(scale, tab_ref, tabt_ref, w_ref, k_ref, at, st, wt, vt, fb, bb):
    at[0], at[1] = widened(tab_ref[...])
    st[0], st[1] = widened(tabt_ref[...])
    for l in range(w_ref.shape[0]):

        def body(m, _):
            re, im = w_ref[l, 0, m] * scale, w_ref[l, 1, m] * scale
            wt[0, l, m], wt[1, l, m] = split(jnp.concatenate([re] * XB + [im] * XB, axis=1))
            re, im = re.T, -im.T
            vt[0, l, m], vt[1, l, m] = split(jnp.concatenate([re] * XB + [im] * XB, axis=1))
            return 0

        lax.fori_loop(0, w_ref.shape[2], body, 0)
        taps = [k_ref[l, j] for j in range(3)]
        fb[l] = band(taps)
        bb[l] = band([t.T for t in taps[::-1]])


def prepare(scale, spectral_weights, conv_kernel, mode_list, total_time):
    layers, _, modes, channels, _ = spectral_weights.shape
    tab = angles(mode_list, total_time)
    rows, cols = 2 * modes * J, total_time * J
    shapes = [(2, rows, cols), (2, cols, rows)]
    shapes += [(2, layers, modes, channels, 2 * LANES)] * 2 + [(layers, 8 * LANES, 2 * LANES)] * 2
    return pl.pallas_call(
        functools.partial(prepare_kernel, scale),
        in_specs=[VMEM] * 4,
        out_specs=[VMEM] * 6,
        out_shape=[pltpu.HBM(shape, BF16) for shape in shapes],
        compiler_params=PARAMS,
    )(tab, tab.T, spectral_weights, conv_kernel)


def lane_block():
    return lax.broadcasted_iota(jnp.int32, (1, LANES), 1) // C


def put_split(value, s, high_ref, low_ref):
    high, low = split(value)
    high_ref[s] = high
    low_ref[s] = low


def with_neighbours(ref, s):
    own = ref[s]
    x = lane_block()
    zero = jnp.zeros_like(own)
    before = ref[s - 1] if s > 0 else zero
    after = ref[s + 1] if s + 1 < ref.shape[0] else zero
    edge = jnp.where(x == XB - 1, before, jnp.where(x == 0, after, zero))
    return jnp.concatenate([own, edge], axis=1)


def pair_operand(high_ref, low_ref, s):
    x = lane_block()
    bricks = high_ref.shape[0]

    def edges(ref):
        zero = jnp.zeros_like(ref[s])
        before = ref[s - 1] if s > 0 else zero
        after = ref[s + 2] if s + 2 < bricks else zero
        return jnp.where(x == XB - 1, before, jnp.where(x == 0, after, zero))

    high = [high_ref[s], high_ref[s + 1]]
    low = [low_ref[s], low_ref[s + 1]]
    edge, edge_low = edges(high_ref), edges(low_ref)
    half = LANES // 2
    swapped = jnp.concatenate([edge_low[:, half:], edge_low[:, :half]], axis=1)
    both = jnp.where((x == 0) | (x == XB - 1), edge, swapped)
    return jnp.concatenate([*high, *low, *high, both, edge], axis=1)


def analyse_pair(table, high_ref, low_ref, coef_ref, s):
    right = [jnp.concatenate([r[s], r[s + 1]], axis=1) for r in (high_ref, low_ref)]
    result = dot3(table, right)
    coef_ref[s] = result[:, :LANES]
    coef_ref[s + 1] = result[:, LANES:]


def analyse(table, high_ref, low_ref, coef_ref):
    for s in range(0, high_ref.shape[0], 2):
        analyse_pair(table, high_ref, low_ref, coef_ref, s)


def mixing_matrix(w_ref, piece, l, m):
    row = lax.broadcasted_iota(jnp.int32, (LANES, 2 * LANES), 0) // C
    col = lax.broadcasted_iota(jnp.int32, (LANES, 2 * LANES), 1) // C % XB
    wide = jnp.concatenate([w_ref[piece, l, m]] * XB, axis=0)
    top = jnp.where(row == col, wide, jnp.zeros_like(wide))
    return jnp.concatenate(
        [top, jnp.concatenate([-top[:, LANES:], top[:, :LANES]], axis=1)], axis=0
    )


def mix(coef_ref, w_ref, l, mixed_ref):
    bricks = coef_ref.shape[0]
    for m in range(w_ref.shape[2]):
        re, im = slice(2 * J * m, 2 * J * m + J), slice(2 * J * m + J, 2 * J * (m + 1))
        value = jnp.concatenate(
            [coef_ref[:, re].reshape(bricks * J, LANES), coef_ref[:, im].reshape(bricks * J, LANES)],
            axis=1,
        )
        matrix = tuple(mixing_matrix(w_ref, piece, l, m) for piece in range(2))
        result = dot3(split(value), matrix)
        mixed_ref[:, re] = result[:, :LANES].reshape(bricks, J, LANES)
        mixed_ref[:, im] = result[:, LANES:].reshape(bricks, J, LANES)


def synthesise(table, mixed_ref, matrix, high_ref, low_ref, emit):
    for s in range(0, mixed_ref.shape[0], 2):
        right = split(jnp.concatenate([mixed_ref[s], mixed_ref[s + 1]], axis=1))
        total = dot3(table, right) + jnp.dot(
            pair_operand(high_ref, low_ref, s), matrix, preferred_element_type=F32
        )
        emit(s, total[:, :LANES])
        emit(s + 1, total[:, LANES:])


def gelu_parts(z):
    cdf = 0.5 * (1.0 + lax.erf(z * math.sqrt(0.5)))
    slope = cdf + z * (jnp.exp(-0.5 * z * z) * (1.0 / math.sqrt(2.0 * math.pi)))
    return z * cdf, slope


def brick(ref, s):
    return ref[:, s].reshape(-1, LANES)


def forward_kernel(
    x_ref, at, st, wt, fb,
    coef1, coef2, slope1, slope2, x1h, x1l, x2h, x2l, mixed,
):
    bricks = x_ref.shape[1]
    for s in range(bricks):
        put_split(brick(x_ref, s), s, x1h, x1l)
    analysis, synthesis = (at[0], at[1]), (st[0], st[1])

    def first(s, z):
        value, slope = gelu_parts(z)
        slope1[s] = slope
        put_split(value, s, x2h, x2l)

    def second(s, z):
        slope2[s] = gelu_parts(z)[1]

    for l, (h, low, coef, emit) in enumerate(
        ((x1h, x1l, coef1, first), (x2h, x2l, coef2, second))
    ):
        analyse(analysis, h, low, coef)
        mix(coef, wt, l, mixed)
        synthesise(synthesis, mixed, fb[l], h, low, emit)


def forward(field, *tables):
    _, bricks, _, _ = field.shape
    _, modes, rows = tables[0].shape
    coef = pltpu.HBM((bricks, modes, LANES), F32)
    full = pltpu.HBM((bricks, rows, LANES), F32)
    half = pltpu.HBM((bricks, rows, LANES), BF16)
    return pl.pallas_call(
        forward_kernel,
        in_specs=[VMEM] * 5,
        out_specs=[VMEM] * 8,
        out_shape=[coef, coef, full, full, half, half, half, half],
        scratch_shapes=[pltpu.VMEM((bricks, modes, LANES), F32)],
        compiler_params=PARAMS,
    )(field, *in_hbm(*tables))


def backward_kernel(*refs):
    g_any, slope1_any, slope2_any = refs[:3]
    small_any = refs[3:7]
    out_any, sens1_any, sens2_any = refs[7:10]
    z_any = refs[10:14]
    g, slope1, slope2 = refs[14:17]
    small = refs[17:21]
    sens1, sens2, z1h, z1l, z2h, z2l, out, mixed, load_sem, small_sem, store_sem = refs[21:]
    at, st, wt, bb = small
    bricks = slope1.shape[0]
    copy = pltpu.make_async_copy

    half = bricks // 2
    loads = []
    for i, part in enumerate((pl.ds(0, half), pl.ds(half, half))):
        loads.append(copy(g_any.at[:, part], g.at[:, part], load_sem.at[2 * i]))
        loads.append(copy(slope2_any.at[part], slope2.at[part], load_sem.at[2 * i + 1]))
    loads.append(copy(slope1_any, slope1, load_sem.at[4]))
    tables = [copy(a, r, small_sem.at[i]) for i, (a, r) in enumerate(zip(small_any, small))]
    tables[0].start()
    for load in loads[:4]:
        load.start()

    stores = []

    def store(source, target):
        stores.append(copy(source, target, store_sem.at[len(stores)]))
        stores[-1].start()

    for load in (tables[0], loads[0], loads[1]):
        load.wait()
    for load in (tables[2], tables[1], tables[3], loads[4]):
        load.start()
    analysis = (at[0], at[1])
    for s in range(0, bricks, 2):
        if s == half:
            for load in loads[2:4]:
                load.wait()
        for o in (s, s + 1):
            put_split(brick(g, o) * slope2[o], o, z2h, z2l)
        analyse_pair(analysis, z2h, z2l, sens2, s)
    store(z2h, z_any[2])
    store(z2l, z_any[3])
    store(sens2, sens2_any)
    tables[2].wait()
    mix(sens2, wt, 1, mixed)
    tables[1].wait()
    tables[3].wait()
    synthesis = (st[0], st[1])

    def second(s, value):
        if s == 0:
            loads[4].wait()
        put_split(value * slope1[s], s, z1h, z1l)

    def first(s, value):
        out[:, s] = value.reshape(out.shape[0], -1, LANES)
        if s % STORED == STORED - 1:
            done = pl.ds(s - STORED + 1, STORED)
            store(out.at[:, done], out_any.at[:, done])

    synthesise(synthesis, mixed, bb[1], z2h, z2l, second)
    store(z1h, z_any[0])
    store(z1l, z_any[1])
    analyse(analysis, z1h, z1l, sens1)
    store(sens1, sens1_any)
    mix(sens1, wt, 0, mixed)
    synthesise(synthesis, mixed, bb[0], z1h, z1l, first)
    for done in stores:
        done.wait()


STORED = 4


def backward(cotangent, slope1, slope2, *tables):
    groups, bricks, lines, _ = cotangent.shape
    _, modes, rows = tables[0].shape
    coef = ((bricks, modes, LANES), F32)
    half = ((bricks, rows, LANES), BF16)
    outs = [(cotangent.shape, F32), coef, coef, half, half, half, half]
    operands = (cotangent, slope1, slope2, *tables)
    scratch = [(o.shape, o.dtype) for o in operands]
    scratch += [coef, coef, half, half, half, half, (cotangent.shape, F32), coef]
    return pl.pallas_call(
        backward_kernel,
        in_specs=[ANY] + [HBM] * 6,
        out_specs=[HBM] * 7,
        out_shape=[pltpu.HBM(*o) for o in outs],
        scratch_shapes=[pltpu.VMEM(*o) for o in scratch]
        + [
            pltpu.SemaphoreType.DMA((5,)),
            pltpu.SemaphoreType.DMA((4,)),
            pltpu.SemaphoreType.DMA((6 + bricks // STORED,)),
        ],
        compiler_params=PARAMS,
    )(cotangent, *in_hbm(*operands[1:]))


ROWS = ((0,), (0,))
TAPS = 3
RADIX = 4


def weight_kernel(scale, me_ref, *refs):
    coef1_any, coef2_any, sens1_any, sens2_any = refs[:4]
    half_any = refs[4:12]
    modes = refs[0].shape[1] // (2 * J)
    outs = refs[12 : 12 + RADIX]
    coef1, coef2, sens1, sens2 = refs[12 + RADIX : 16 + RADIX]
    half = refs[16 + RADIX : 24 + RADIX]
    spectral, load_sem, half_sem = refs[24 + RADIX :]
    bricks = coef1.shape[0]
    copy = pltpu.make_async_copy

    halves = [
        [
            copy(a.at[s], r.at[s], half_sem.at[i, s])
            for i, (a, r) in enumerate(zip(half_any, half))
        ]
        for s in range(bricks)
    ]
    pairs = zip((coef1_any, coef2_any, sens1_any, sens2_any), (coef1, coef2, sens1, sens2))
    loads = [copy(a, r, load_sem.at[i]) for i, (a, r) in enumerate(pairs)]
    x1h, x1l, x2h, x2l, z1h, z1l, z2h, z2l = half
    for l in range(2):
        for s in range(bricks):
            for i in (0, 1, 4, 5) if l == 0 else (2, 3, 6, 7):
                halves[s][i].start()
    for c in loads:
        c.start()

    blocks = []
    for l, (xh, xl, zh, zl) in enumerate(((x1h, x1l, z1h, z1l), (x2h, x2l, z2h, z2l))):
        total = jnp.zeros((LANES, 2 * LANES), F32)
        for s in range(bricks):
            for ahead in (0, 1) if s == 0 else (s + 1,):
                if ahead < bricks:
                    for i in (0, 1, 4, 5) if l == 0 else (2, 3, 6, 7):
                        halves[ahead][i].wait()
            value = (with_neighbours(xh, s), with_neighbours(xl, s))
            total = total + dot3((zh[s], zl[s]), value, ROWS)
        for j in range(TAPS):
            pairs = [(x, x - j + 1) for x in range(XB) if 0 <= x - j + 1 < XB]
            tap = sum(total[y * C : (y + 1) * C, x * C : (x + 1) * C] for x, y in pairs)
            if j == 0:
                tap = tap + total[:C, LANES + (XB - 1) * C :]
            if j == 2:
                tap = tap + total[(XB - 1) * C :, LANES : LANES + C]
            blocks.append(tap)
    half_rows = C // 2
    first = jnp.concatenate(blocks[:4], axis=1)
    rest = [b[i * half_rows : (i + 1) * half_rows] for b in blocks[4:] for i in range(2)]
    kernels = jnp.concatenate([first, jnp.concatenate(rest, axis=1)], axis=0)

    for c in loads:
        c.wait()
    for m in range(modes):
        re, im = slice(2 * J * m, 2 * J * m + J), slice(2 * J * m + J, 2 * J * (m + 1))
        pieces = []
        for coef, sens in ((coef1, sens1), (coef2, sens2)):
            cr, ci, zr, zi = (
                r[:, p].reshape(bricks * J, LANES)
                for r, p in ((coef, re), (coef, im), (sens, re), (sens, im))
            )
            left = jnp.concatenate([cr, ci], axis=0)
            right = jnp.concatenate(
                [jnp.concatenate([zr, zi], axis=1), jnp.concatenate([zi, -zr], axis=1)], axis=0
            )
            product = dot3(split(left), split(right), ROWS) * scale
            for part in range(2):
                pieces.append(
                    sum(
                        product[x * C : (x + 1) * C, part * LANES + x * C : part * LANES + (x + 1) * C]
                        for x in range(XB)
                    )
                )
        spectral[m] = jnp.concatenate(pieces, axis=1)
    for r, out in enumerate(outs):
        high = (me_ref[0] + r) % RADIX
        for q in range(RADIX):
            low = (me_ref[1] + q) % RADIX
            out[q * C : (q + 1) * C] = spectral[high * RADIX + low]
        out[RADIX * C :] = kernels


def weight_gradients(scale, me, *operands):
    modes = operands[0].shape[1] // (2 * J)
    rows = RADIX * C + 2 * TAPS * C // XB
    return pl.pallas_call(
        functools.partial(weight_kernel, scale),
        in_specs=[pl.BlockSpec(memory_space=pltpu.SMEM)] + [HBM] * 12,
        out_specs=[VMEM] * RADIX,
        out_shape=[jax.ShapeDtypeStruct((rows, LANES), F32)] * RADIX,
        scratch_shapes=[pltpu.VMEM(o.shape, o.dtype) for o in operands]
        + [
            pltpu.VMEM((modes, C, LANES), F32),
            pltpu.SemaphoreType.DMA((4,)),
            pltpu.SemaphoreType.DMA((8, operands[0].shape[0])),
        ],
        compiler_params=PARAMS,
    )(me, *in_hbm(*operands))


def shifted(pieces, axis, size, stride):
    count = len(pieces)
    got = [pieces[0]]
    for r in range(1, count):
        perm = []
        for i in range(size):
            digit = i // stride % count
            perm.append((i, i + ((digit + r) % count - digit) * stride))
        got.append(lax.ppermute(pieces[r], axis, perm))
    return got


def ring_sum(values):
    while len(values) > 1:
        half = len(values) // 2
        values = [values[i] + values[i + half] for i in range(half)]
    return values[0]


def split_sum_kernel(*refs):
    total = ring_sum([r[...] for r in refs[:RADIX]])
    for q, out in enumerate(refs[RADIX:]):
        out[:C] = total[q * C : (q + 1) * C]
        out[C:] = total[RADIX * C :]


def split_sum(pieces):
    rows = pieces[0].shape[0] - (RADIX - 1) * C
    return pl.pallas_call(
        split_sum_kernel,
        in_specs=[VMEM] * RADIX,
        out_specs=[VMEM] * RADIX,
        out_shape=[jax.ShapeDtypeStruct((rows, LANES), F32)] * RADIX,
        compiler_params=PARAMS,
    )(*pieces)


def finish_kernel(one_ref, other_ref, mode_ref, kernel_ref):
    total = one_ref[...] + other_ref[...]
    layers = mode_ref.shape[0]
    for l in range(layers):
        for part in range(2):
            at = (2 * l + part) * C
            mode_ref[l, part, 0] = total[:C, at : at + C]
    low = C // 2
    blocks = [total[C : 2 * C, b * C : (b + 1) * C] for b in range(XB)]
    for b in range(2):
        top, bottom = (total[2 * C :, (2 * b + i) * C : (2 * b + i + 1) * C] for i in range(2))
        blocks.append(jnp.concatenate([top, bottom], axis=0))
    for i, block in enumerate(blocks):
        kernel_ref[i // TAPS, i % TAPS] = block.T


def finish(one, other, layers):
    return pl.pallas_call(
        finish_kernel,
        in_specs=[VMEM] * 2,
        out_specs=[VMEM] * 2,
        out_shape=[
            jax.ShapeDtypeStruct((layers, 2, 1, C, C), F32),
            jax.ShapeDtypeStruct((layers, TAPS, C, C), F32),
        ],
        compiler_params=PARAMS,
    )(one, other)


def on_device(input_field, cotangent, spectral_weights, conv_kernel, mode_list):
    groups = lax.axis_size("tm")
    bricks = lax.axis_size("space")
    everyone = ("tm", "space")
    steps = input_field.shape[0]
    total_time = steps * groups
    layers, _, modes, _, _ = spectral_weights.shape
    scale = 2.0 / total_time
    exchange = functools.partial(lax.all_to_all, split_axis=0, concat_axis=0, tiled=True)

    received = exchange(to_blocks(input_field), everyone)
    cot_blocks = to_blocks(cotangent)
    prepared = prepare(scale, spectral_weights, conv_kernel, mode_list, total_time)
    received, cot_blocks, prepared = lax.optimization_barrier((received, cot_blocks, prepared))
    analysis, synthesis, mix_forward, mix_backward, band_forward, band_backward = prepared
    cot_received = exchange(cot_blocks, everyone)
    shape = (groups, bricks, steps * J, LANES)
    coef1, coef2, slope1, slope2, x1h, x1l, x2h, x2l = forward(
        received.reshape(shape), analysis, synthesis, mix_forward, band_forward
    )
    grad, sens1, sens2, z1h, z1l, z2h, z2l = backward(
        cot_received.reshape(shape),
        slope1,
        slope2,
        analysis,
        synthesis,
        mix_backward,
        band_backward,
    )
    returned = exchange(grad.reshape(cot_received.shape), everyone)
    me = lax.axis_index("tm").astype(jnp.int32)
    place = jnp.stack([me // RADIX, me % RADIX])
    pieces = weight_gradients(
        scale, place, coef1, coef2, sens1, sens2, x1h, x1l, x2h, x2l, z1h, z1l, z2h, z2l
    )
    pieces = split_sum(shifted(pieces, "tm", groups, RADIX))
    grad_input, pieces = lax.optimization_barrier(
        (from_blocks(returned), shifted(pieces, "tm", groups, 1))
    )
    total = ring_sum(pieces)
    total = ring_sum(shifted([total] * RADIX, "space", bricks, bricks // RADIX))
    mode_total, kernel_total = finish(*shifted([total] * 2, "space", bricks, 1), layers)
    return (grad_input, mode_total, kernel_total)


def solution(mesh):
    placed = (P("tm", None, "space", None), P("tm", None, "space", None), P(), P(), P())
    return jax.shard_map(
        on_device,
        mesh=mesh,
        in_specs=placed,
        out_specs=(P("tm", None, "space", None), P(None, None, "tm", None, None), P()),
        check_vma=False,
    )
```

```python
import functools
import math

import jax
import jax.numpy as jnp
from jax import lax
from jax.experimental import pallas as pl
from jax.experimental.pallas import tpu as pltpu
from jax.sharding import PartitionSpec as P

F32 = jnp.float32
BF16 = jnp.bfloat16
LANES = 128
J = 8
XB = 4
C = 32
VMEM = pl.BlockSpec(memory_space=pltpu.VMEM)
ANY = pl.BlockSpec(memory_space=pl.ANY)
HBM = pl.BlockSpec(memory_space=pltpu.HBM)
PARAMS = pltpu.CompilerParams(vmem_limit_bytes=40 * 1024 * 1024)


def in_hbm(*values):
    return [pltpu.with_memory_space_constraint(v, pltpu.HBM) for v in values]


def split(value):
    high = value.astype(BF16)
    low = (value - high.astype(F32)).astype(BF16)
    return high, low


def dot3(left, right, dims=((1,), (0,))):
    (lh, ll), (rh, rl) = left, right
    (lc,), (rc,) = dims
    a = jnp.concatenate([lh, ll, lh], axis=lc)
    b = jnp.concatenate([rh, rh, rl], axis=rc)
    return lax.dot_general(a, b, (dims, ((), ())), preferred_element_type=F32)


FETCHED = 1
SENT = 4


def scatter_kernel(first_any, second_any, out_any, field, out, load_sem, store_sem):
    _, _, steps, _, columns = field.shape
    groups = LANES // J
    loads = [
        pltpu.make_async_copy(
            source.at[:, :, x, :], field.at[which, x], load_sem.at[which, x]
        )
        for which, source in enumerate((first_any, second_any))
        for x in range(XB)
    ]
    for load in loads:
        load.start()
    stores = []
    count = columns // LANES
    for which in range(2):
        for load in loads[which * XB : (which + 1) * XB]:
            load.wait()
        for q in range(count):
            lanes = slice(q * LANES, (q + 1) * LANES)
            for t in range(steps):
                at = (which * steps + t) * J
                rows = jnp.concatenate([field[which, x, t, :, lanes] for x in range(XB)], axis=0)
                rows = rows.T.reshape(groups, J, LANES)
                out[q * groups : (q + 1) * groups, at : at + J] = rows
            if which == 1 and (q + 1) % (count // SENT) == 0:
                size = groups * count // SENT
                part = pl.ds((q + 1) * groups - size, size)
                sem = store_sem.at[len(stores)]
                stores.append(pltpu.make_async_copy(out.at[part], out_any.at[part], sem))
                stores[-1].start()
    for store in stores:
        store.wait()


def gather_kernel(blocks_any, out_any, blocks, out, load_sem, store_sem):
    steps, _, _, columns = out.shape
    groups = LANES // J
    count = columns // LANES
    loads = []
    for i in range(FETCHED):
        part = pl.ds(i * groups * count // FETCHED, groups * count // FETCHED)
        loads.append(pltpu.make_async_copy(blocks_any.at[part], blocks.at[part], load_sem.at[i]))
        loads[-1].start()
    stores = []
    for t in range(steps):
        for q in range(count):
            lanes = slice(q * LANES, (q + 1) * LANES)
            if t == 0 and q % (count // FETCHED) == 0:
                loads[q // (count // FETCHED)].wait()
            rows = blocks[q * groups : (q + 1) * groups, t * J : (t + 1) * J]
            rows = rows.reshape(LANES, LANES).T
            for x in range(XB):
                out[t, :, x, lanes] = rows[x * C : (x + 1) * C]
        if (t + 1) % (steps // SENT) == 0:
            part = pl.ds(t + 1 - steps // SENT, steps // SENT)
            sem = store_sem.at[len(stores)]
            stores.append(pltpu.make_async_copy(out.at[part], out_any.at[part], sem))
            stores[-1].start()
    for store in stores:
        store.wait()


def to_blocks(first, second):
    steps, _, _, columns = first.shape
    shape = (columns // J, 2 * steps * J, LANES)
    return pl.pallas_call(
        scatter_kernel,
        in_specs=[HBM] * 2,
        out_specs=HBM,
        out_shape=pltpu.HBM(shape, F32),
        scratch_shapes=[
            pltpu.VMEM((2, XB, steps, C, columns), F32),
            pltpu.VMEM(shape, F32),
            pltpu.SemaphoreType.DMA((2, XB)),
            pltpu.SemaphoreType.DMA((SENT,)),
        ],
        compiler_params=PARAMS,
    )(*in_hbm(first, second))


def from_blocks(blocks):
    parts, rows, _ = blocks.shape
    shape = (rows // J, C, XB, parts * J)
    return pl.pallas_call(
        gather_kernel,
        in_specs=[ANY],
        out_specs=HBM,
        out_shape=pltpu.HBM(shape, F32),
        scratch_shapes=[
            pltpu.VMEM(blocks.shape, F32),
            pltpu.VMEM(shape, F32),
            pltpu.SemaphoreType.DMA((FETCHED,)),
            pltpu.SemaphoreType.DMA((SENT,)),
        ],
        compiler_params=PARAMS,
    )(blocks)


def angles(mode_list, total_time):
    steps = jnp.arange(total_time, dtype=jnp.int32)
    phase = (mode_list[:, None] * steps[None, :]) % total_time
    angle = phase.astype(F32) * (2.0 * math.pi / total_time)
    both = jnp.stack([jnp.cos(angle), -jnp.sin(angle)], axis=1)
    return both.reshape(2 * mode_list.shape[0], total_time)


def widened(value):
    rows, cols = value.shape
    spread = lax.broadcasted_iota(jnp.int32, (cols, cols * J), 1) // J
    spread = (spread == lax.broadcasted_iota(jnp.int32, (cols, cols * J), 0)).astype(BF16)
    shape = (rows * J, cols * J)
    same = (
        lax.broadcasted_iota(jnp.int32, shape, 0) % J
        == lax.broadcasted_iota(jnp.int32, shape, 1) % J
    )
    for piece in split(value):
        wide = jnp.dot(piece, spread, preferred_element_type=F32)
        wide = jnp.broadcast_to(wide[:, None, :], (rows, J, cols * J)).reshape(shape)
        yield jnp.where(same, wide, 0.0).astype(BF16)


def blocks_of(kernel, places, cols):
    zero = jnp.zeros((C, C), F32)
    rows = [
        jnp.concatenate([kernel[p[y]] if y in p else zero for y in range(cols)], axis=1)
        for p in places
    ]
    return jnp.concatenate(rows, axis=0)


def band(kernel):
    cells = 2 * XB
    own = [{y: x - y + 1 for y in range(cells) if abs(x - y) <= 1} for x in range(cells)]
    before, after = {0: 0}, {cells - 1: 2}
    own = split(blocks_of(kernel, own, cells))
    both = split(blocks_of(kernel, [after, before, after, before], cells))
    edge = split(blocks_of(kernel, [after, {}, {}, before], cells))
    return jnp.concatenate([own[0], own[0], own[1], both[0], edge[1]], axis=0)


def prepare_kernel(scale, tab_ref, tabt_ref, w_ref, k_ref, at, st, wt, vt, fb, bb):
    at[0], at[1] = widened(tab_ref[...])
    st[0], st[1] = widened(tabt_ref[...])
    for l in range(w_ref.shape[0]):

        def body(m, _):
            re, im = w_ref[l, 0, m] * scale, w_ref[l, 1, m] * scale
            wt[0, l, m], wt[1, l, m] = split(jnp.concatenate([re] * XB + [im] * XB, axis=1))
            re, im = re.T, -im.T
            vt[0, l, m], vt[1, l, m] = split(jnp.concatenate([re] * XB + [im] * XB, axis=1))
            return 0

        lax.fori_loop(0, w_ref.shape[2], body, 0)
        taps = [k_ref[l, j] for j in range(3)]
        fb[l] = band(taps)
        bb[l] = band([t.T for t in taps[::-1]])


def prepare(scale, spectral_weights, conv_kernel, mode_list, total_time):
    layers, _, modes, channels, _ = spectral_weights.shape
    tab = angles(mode_list, total_time)
    rows, cols = 2 * modes * J, total_time * J
    shapes = [(2, rows, cols), (2, cols, rows)]
    shapes += [(2, layers, modes, channels, 2 * LANES)] * 2 + [(layers, 8 * LANES, 2 * LANES)] * 2
    return pl.pallas_call(
        functools.partial(prepare_kernel, scale),
        in_specs=[VMEM] * 4,
        out_specs=[VMEM] * 6,
        out_shape=[pltpu.HBM(shape, BF16) for shape in shapes],
        compiler_params=PARAMS,
    )(tab, tab.T, spectral_weights, conv_kernel)


def lane_block():
    return lax.broadcasted_iota(jnp.int32, (1, LANES), 1) // C


def put_split(value, s, high_ref, low_ref):
    high, low = split(value)
    high_ref[s] = high
    low_ref[s] = low


def with_neighbours(ref, s):
    own = ref[s]
    x = lane_block()
    zero = jnp.zeros_like(own)
    before = ref[s - 1] if s > 0 else zero
    after = ref[s + 1] if s + 1 < ref.shape[0] else zero
    edge = jnp.where(x == XB - 1, before, jnp.where(x == 0, after, zero))
    return jnp.concatenate([own, edge], axis=1)


def pair_operand(high_ref, low_ref, s):
    x = lane_block()
    bricks = high_ref.shape[0]

    def edges(ref):
        zero = jnp.zeros_like(ref[s])
        before = ref[s - 1] if s > 0 else zero
        after = ref[s + 2] if s + 2 < bricks else zero
        return jnp.where(x == XB - 1, before, jnp.where(x == 0, after, zero))

    high = [high_ref[s], high_ref[s + 1]]
    low = [low_ref[s], low_ref[s + 1]]
    edge, edge_low = edges(high_ref), edges(low_ref)
    half = LANES // 2
    swapped = jnp.concatenate([edge_low[:, half:], edge_low[:, :half]], axis=1)
    both = jnp.where((x == 0) | (x == XB - 1), edge, swapped)
    return jnp.concatenate([*high, *low, *high, both, edge], axis=1)


def analyse_pair(table, high_ref, low_ref, coef_ref, s):
    right = [jnp.concatenate([r[s], r[s + 1]], axis=1) for r in (high_ref, low_ref)]
    result = dot3(table, right)
    coef_ref[s] = result[:, :LANES]
    coef_ref[s + 1] = result[:, LANES:]


def analyse(table, high_ref, low_ref, coef_ref):
    for s in range(0, high_ref.shape[0], 2):
        analyse_pair(table, high_ref, low_ref, coef_ref, s)


def mixing_matrix(w_ref, piece, l, m):
    row = lax.broadcasted_iota(jnp.int32, (LANES, 2 * LANES), 0) // C
    col = lax.broadcasted_iota(jnp.int32, (LANES, 2 * LANES), 1) // C % XB
    wide = jnp.concatenate([w_ref[piece, l, m]] * XB, axis=0)
    top = jnp.where(row == col, wide, jnp.zeros_like(wide))
    return jnp.concatenate(
        [top, jnp.concatenate([-top[:, LANES:], top[:, :LANES]], axis=1)], axis=0
    )


def mix(coef_ref, w_ref, l, mixed_ref):
    bricks = coef_ref.shape[0]
    for m in range(w_ref.shape[2]):
        re, im = slice(2 * J * m, 2 * J * m + J), slice(2 * J * m + J, 2 * J * (m + 1))
        value = jnp.concatenate(
            [coef_ref[:, re].reshape(bricks * J, LANES), coef_ref[:, im].reshape(bricks * J, LANES)],
            axis=1,
        )
        matrix = tuple(mixing_matrix(w_ref, piece, l, m) for piece in range(2))
        result = dot3(split(value), matrix)
        mixed_ref[:, re] = result[:, :LANES].reshape(bricks, J, LANES)
        mixed_ref[:, im] = result[:, LANES:].reshape(bricks, J, LANES)


def synthesise(table, mixed_ref, matrix, high_ref, low_ref, emit):
    for s in range(0, mixed_ref.shape[0], 2):
        right = split(jnp.concatenate([mixed_ref[s], mixed_ref[s + 1]], axis=1))
        total = dot3(table, right) + jnp.dot(
            pair_operand(high_ref, low_ref, s), matrix, preferred_element_type=F32
        )
        emit(s, total[:, :LANES])
        emit(s + 1, total[:, LANES:])


def gelu_parts(z):
    cdf = 0.5 * (1.0 + lax.erf(z * math.sqrt(0.5)))
    slope = cdf + z * (jnp.exp(-0.5 * z * z) * (1.0 / math.sqrt(2.0 * math.pi)))
    return z * cdf, slope


STORED = 4


def layers_kernel(*refs):
    both = refs[0]
    small_any = refs[1:7]
    out_any = refs[7]
    kept_any = refs[8:20]
    small = refs[20:26]
    kept = refs[26:38]
    field, sens, slope1, out, mixed, load_sem, small_sem, store_sem = refs[38:]
    analysis_ref, synthesis_ref, mix_forward, mix_backward, band_forward, band_backward = small
    coef1, coef2, sens1, sens2, x1h, x1l, x2h, x2l, z1h, z1l, z2h, z2l = kept
    groups, bricks, lines, _ = both.shape
    lines = lines // 2
    copy = pltpu.make_async_copy

    tables = [copy(a, r, small_sem.at[i]) for i, (a, r) in enumerate(zip(small_any, small))]
    half = bricks // 2
    loads = [
        copy(both.at[:, at, pl.ds(0, lines)], field.at[:, at], load_sem.at[i])
        for i, at in enumerate((pl.ds(0, half), pl.ds(half, half)))
    ]
    loads.append(copy(both.at[:, :, pl.ds(lines, lines)], sens, load_sem.at[2]))
    for load in (tables[0], loads[0], loads[1], tables[2], tables[1], tables[4]):
        load.start()
    stores = []

    def store(source, target):
        stores.append(copy(source, target, store_sem.at[len(stores)]))
        stores[-1].start()

    def keep(*places):
        for i in places:
            store(kept[i], kept_any[i])

    def brick(ref, s):
        return ref[:, s].reshape(-1, LANES)

    def first_out(s, value):
        value, slope = gelu_parts(value)
        slope1[s] = slope
        put_split(value, s, x2h, x2l)

    def second_out(s, value):
        put_split(brick(sens, s) * gelu_parts(value)[1], s, z2h, z2l)

    def second_back(s, value):
        put_split(value * slope1[s], s, z1h, z1l)

    def first_back(s, value):
        out[:, s] = value.reshape(groups, lines, LANES)
        if s % STORED == STORED - 1:
            done = pl.ds(s - STORED + 1, STORED)
            store(out.at[:, done], out_any.at[:, done])

    tables[0].wait()
    analysis = (analysis_ref[0], analysis_ref[1])
    for s in range(0, bricks, 2):
        if s % half == 0:
            loads[s // half].wait()
        for o in (s, s + 1):
            put_split(brick(field, o), o, x1h, x1l)
        analyse_pair(analysis, x1h, x1l, coef1, s)
    for load in (loads[2], tables[3], tables[5]):
        load.start()
    keep(0, 4, 5)
    tables[2].wait()
    mix(coef1, mix_forward, 0, mixed)
    tables[1].wait()
    tables[4].wait()
    synthesis = (synthesis_ref[0], synthesis_ref[1])
    synthesise(synthesis, mixed, band_forward[0], x1h, x1l, first_out)
    analyse(analysis, x2h, x2l, coef2)
    keep(1, 6, 7)
    mix(coef2, mix_forward, 1, mixed)
    loads[2].wait()
    synthesise(synthesis, mixed, band_forward[1], x2h, x2l, second_out)
    analyse(analysis, z2h, z2l, sens2)
    keep(3, 10, 11)
    tables[3].wait()
    mix(sens2, mix_backward, 1, mixed)
    tables[5].wait()
    synthesise(synthesis, mixed, band_backward[1], z2h, z2l, second_back)
    analyse(analysis, z1h, z1l, sens1)
    keep(2, 8, 9)
    mix(sens1, mix_backward, 0, mixed)
    synthesise(synthesis, mixed, band_backward[0], z1h, z1l, first_back)
    for done in stores:
        done.wait()


def run_layers(both, *tables):
    groups, bricks, lines, _ = both.shape
    _, modes, rows = tables[0].shape
    coef = ((bricks, modes, LANES), F32)
    full = ((bricks, rows, LANES), F32)
    half = ((bricks, rows, LANES), BF16)
    result = ((groups, bricks, lines // 2, LANES), F32)
    kept = [coef] * 4 + [half] * 8
    scratch = [(t.shape, t.dtype) for t in tables] + kept + [result, result, full, result, coef]
    return pl.pallas_call(
        layers_kernel,
        in_specs=[ANY] + [HBM] * 6,
        out_specs=[HBM] * 13,
        out_shape=[pltpu.HBM(*o) for o in (result, *kept)],
        scratch_shapes=[pltpu.VMEM(*o) for o in scratch]
        + [
            pltpu.SemaphoreType.DMA((3,)),
            pltpu.SemaphoreType.DMA((6,)),
            pltpu.SemaphoreType.DMA((len(kept) + bricks // STORED,)),
        ],
        compiler_params=PARAMS,
    )(both, *in_hbm(*tables))


ROWS = ((0,), (0,))
TAPS = 3
RADIX = 4


def weight_kernel(scale, me_ref, *refs):
    coef1_any, coef2_any, sens1_any, sens2_any = refs[:4]
    half_any = refs[4:12]
    modes = refs[0].shape[1] // (2 * J)
    outs = refs[12 : 12 + RADIX]
    coef1, coef2, sens1, sens2 = refs[12 + RADIX : 16 + RADIX]
    half = refs[16 + RADIX : 24 + RADIX]
    spectral, load_sem, half_sem = refs[24 + RADIX :]
    bricks = coef1.shape[0]
    copy = pltpu.make_async_copy

    halves = [
        [
            copy(a.at[s], r.at[s], half_sem.at[i, s])
            for i, (a, r) in enumerate(zip(half_any, half))
        ]
        for s in range(bricks)
    ]
    pairs = zip((coef1_any, coef2_any, sens1_any, sens2_any), (coef1, coef2, sens1, sens2))
    loads = [copy(a, r, load_sem.at[i]) for i, (a, r) in enumerate(pairs)]
    x1h, x1l, x2h, x2l, z1h, z1l, z2h, z2l = half
    for l in range(2):
        for s in range(bricks):
            for i in (0, 1, 4, 5) if l == 0 else (2, 3, 6, 7):
                halves[s][i].start()
    for c in loads:
        c.start()

    blocks = []
    for l, (xh, xl, zh, zl) in enumerate(((x1h, x1l, z1h, z1l), (x2h, x2l, z2h, z2l))):
        total = jnp.zeros((LANES, 2 * LANES), F32)
        for s in range(bricks):
            for ahead in (0, 1) if s == 0 else (s + 1,):
                if ahead < bricks:
                    for i in (0, 1, 4, 5) if l == 0 else (2, 3, 6, 7):
                        halves[ahead][i].wait()
            value = (with_neighbours(xh, s), with_neighbours(xl, s))
            total = total + dot3((zh[s], zl[s]), value, ROWS)
        for j in range(TAPS):
            pairs = [(x, x - j + 1) for x in range(XB) if 0 <= x - j + 1 < XB]
            tap = sum(total[y * C : (y + 1) * C, x * C : (x + 1) * C] for x, y in pairs)
            if j == 0:
                tap = tap + total[:C, LANES + (XB - 1) * C :]
            if j == 2:
                tap = tap + total[(XB - 1) * C :, LANES : LANES + C]
            blocks.append(tap)
    half_rows = C // 2
    first = jnp.concatenate(blocks[:4], axis=1)
    rest = [b[i * half_rows : (i + 1) * half_rows] for b in blocks[4:] for i in range(2)]
    kernels = jnp.concatenate([first, jnp.concatenate(rest, axis=1)], axis=0)

    for c in loads:
        c.wait()
    for m in range(modes):
        re, im = slice(2 * J * m, 2 * J * m + J), slice(2 * J * m + J, 2 * J * (m + 1))
        pieces = []
        for coef, sens in ((coef1, sens1), (coef2, sens2)):
            cr, ci, zr, zi = (
                r[:, p].reshape(bricks * J, LANES)
                for r, p in ((coef, re), (coef, im), (sens, re), (sens, im))
            )
            left = jnp.concatenate([cr, ci], axis=0)
            right = jnp.concatenate(
                [jnp.concatenate([zr, zi], axis=1), jnp.concatenate([zi, -zr], axis=1)], axis=0
            )
            product = dot3(split(left), split(right), ROWS) * scale
            for part in range(2):
                pieces.append(
                    sum(
                        product[x * C : (x + 1) * C, part * LANES + x * C : part * LANES + (x + 1) * C]
                        for x in range(XB)
                    )
                )
        spectral[m] = jnp.concatenate(pieces, axis=1)
    for r, out in enumerate(outs):
        high = (me_ref[0] + r) % RADIX
        for q in range(RADIX):
            low = (me_ref[1] + q) % RADIX
            out[q * C : (q + 1) * C] = spectral[high * RADIX + low]
        out[RADIX * C :] = kernels


def weight_gradients(scale, me, *operands):
    modes = operands[0].shape[1] // (2 * J)
    rows = RADIX * C + 2 * TAPS * C // XB
    return pl.pallas_call(
        functools.partial(weight_kernel, scale),
        in_specs=[pl.BlockSpec(memory_space=pltpu.SMEM)] + [HBM] * 12,
        out_specs=[VMEM] * RADIX,
        out_shape=[jax.ShapeDtypeStruct((rows, LANES), F32)] * RADIX,
        scratch_shapes=[pltpu.VMEM(o.shape, o.dtype) for o in operands]
        + [
            pltpu.VMEM((modes, C, LANES), F32),
            pltpu.SemaphoreType.DMA((4,)),
            pltpu.SemaphoreType.DMA((8, operands[0].shape[0])),
        ],
        compiler_params=PARAMS,
    )(me, *in_hbm(*operands))


def shifted(pieces, axis, size, stride):
    count = len(pieces)
    got = [pieces[0]]
    for r in range(1, count):
        perm = []
        for i in range(size):
            digit = i // stride % count
            perm.append((i, i + ((digit + r) % count - digit) * stride))
        got.append(lax.ppermute(pieces[r], axis, perm))
    return got


def ring_sum(values):
    while len(values) > 1:
        half = len(values) // 2
        values = [values[i] + values[i + half] for i in range(half)]
    return values[0]


def split_sum_kernel(*refs):
    total = ring_sum([r[...] for r in refs[:RADIX]])
    for q, out in enumerate(refs[RADIX:]):
        out[:C] = total[q * C : (q + 1) * C]
        out[C:] = total[RADIX * C :]


def split_sum(pieces):
    rows = pieces[0].shape[0] - (RADIX - 1) * C
    return pl.pallas_call(
        split_sum_kernel,
        in_specs=[VMEM] * RADIX,
        out_specs=[VMEM] * RADIX,
        out_shape=[jax.ShapeDtypeStruct((rows, LANES), F32)] * RADIX,
        compiler_params=PARAMS,
    )(*pieces)


def finish_kernel(one_ref, other_ref, mode_ref, kernel_ref):
    total = one_ref[...] + other_ref[...]
    layers = mode_ref.shape[0]
    for l in range(layers):
        for part in range(2):
            at = (2 * l + part) * C
            mode_ref[l, part, 0] = total[:C, at : at + C]
    low = C // 2
    blocks = [total[C : 2 * C, b * C : (b + 1) * C] for b in range(XB)]
    for b in range(2):
        top, bottom = (total[2 * C :, (2 * b + i) * C : (2 * b + i + 1) * C] for i in range(2))
        blocks.append(jnp.concatenate([top, bottom], axis=0))
    for i, block in enumerate(blocks):
        kernel_ref[i // TAPS, i % TAPS] = block.T


def finish(one, other, layers):
    return pl.pallas_call(
        finish_kernel,
        in_specs=[VMEM] * 2,
        out_specs=[VMEM] * 2,
        out_shape=[
            jax.ShapeDtypeStruct((layers, 2, 1, C, C), F32),
            jax.ShapeDtypeStruct((layers, TAPS, C, C), F32),
        ],
        compiler_params=PARAMS,
    )(one, other)


def on_device(input_field, cotangent, spectral_weights, conv_kernel, mode_list):
    groups = lax.axis_size("tm")
    bricks = lax.axis_size("space")
    everyone = ("tm", "space")
    steps = input_field.shape[0]
    total_time = steps * groups
    layers, _, modes, _, _ = spectral_weights.shape
    scale = 2.0 / total_time
    exchange = functools.partial(lax.all_to_all, split_axis=0, concat_axis=0, tiled=True)

    received = exchange(to_blocks(input_field, cotangent), everyone)
    prepared = prepare(scale, spectral_weights, conv_kernel, mode_list, total_time)
    received, prepared = lax.optimization_barrier((received, prepared))
    grad, *kept = run_layers(
        received.reshape(groups, bricks, 2 * steps * J, LANES), *prepared
    )
    returned = exchange(grad.reshape(groups * bricks, steps * J, LANES), everyone)
    me = lax.axis_index("tm").astype(jnp.int32)
    place = jnp.stack([me // RADIX, me % RADIX])
    pieces = weight_gradients(scale, place, *kept)
    pieces = split_sum(shifted(pieces, "tm", groups, RADIX))
    grad_input, pieces = lax.optimization_barrier(
        (from_blocks(returned), shifted(pieces, "tm", groups, 1))
    )
    total = ring_sum(pieces)
    total = ring_sum(shifted([total] * RADIX, "space", bricks, bricks // RADIX))
    mode_total, kernel_total = finish(*shifted([total] * 2, "space", bricks, 1), layers)
    return (grad_input, mode_total, kernel_total)


def solution(mesh):
    placed = (P("tm", None, "space", None), P("tm", None, "space", None), P(), P(), P())
    return jax.shard_map(
        on_device,
        mesh=mesh,
        in_specs=placed,
        out_specs=(P("tm", None, "space", None), P(None, None, "tm", None, None), P()),
        check_vma=False,
    )
```

```python
import functools
import math

import jax
import jax.numpy as jnp
from jax import lax
from jax.experimental import pallas as pl
from jax.experimental.pallas import tpu as pltpu
from jax.sharding import PartitionSpec as P

F32 = jnp.float32
BF16 = jnp.bfloat16
LANES = 128
J = 8
XB = 4
C = 32
VMEM = pl.BlockSpec(memory_space=pltpu.VMEM)
ANY = pl.BlockSpec(memory_space=pl.ANY)
HBM = pl.BlockSpec(memory_space=pltpu.HBM)
PARAMS = pltpu.CompilerParams(vmem_limit_bytes=40 * 1024 * 1024)


def in_hbm(*values):
    return [pltpu.with_memory_space_constraint(v, pltpu.HBM) for v in values]


def split(value):
    high = value.astype(BF16)
    low = (value - high.astype(F32)).astype(BF16)
    return high, low


def dot3(left, right, dims=((1,), (0,))):
    (lh, ll), (rh, rl) = left, right
    (lc,), (rc,) = dims
    a = jnp.concatenate([lh, ll, lh], axis=lc)
    b = jnp.concatenate([rh, rh, rl], axis=rc)
    return lax.dot_general(a, b, (dims, ((), ())), preferred_element_type=F32)


FETCHED = 1
SENT = 4


def scatter_kernel(first_any, second_any, out_any, field, out, load_sem, store_sem):
    _, _, steps, _, columns = field.shape
    groups = LANES // J
    loads = [
        pltpu.make_async_copy(
            source.at[:, :, x, :], field.at[which, x], load_sem.at[which, x]
        )
        for which, source in enumerate((first_any, second_any))
        for x in range(XB)
    ]
    for load in loads:
        load.start()
    stores = []
    count = columns // LANES
    for which in range(2):
        for load in loads[which * XB : (which + 1) * XB]:
            load.wait()
        for q in range(count):
            lanes = slice(q * LANES, (q + 1) * LANES)
            for t in range(steps):
                at = (which * steps + t) * J
                rows = jnp.concatenate([field[which, x, t, :, lanes] for x in range(XB)], axis=0)
                rows = rows.T.reshape(groups, J, LANES)
                out[q * groups : (q + 1) * groups, at : at + J] = rows
            if which == 1 and (q + 1) % (count // SENT) == 0:
                size = groups * count // SENT
                part = pl.ds((q + 1) * groups - size, size)
                sem = store_sem.at[len(stores)]
                stores.append(pltpu.make_async_copy(out.at[part], out_any.at[part], sem))
                stores[-1].start()
    for store in stores:
        store.wait()


def gather_kernel(blocks_any, out_any, blocks, out, load_sem, store_sem):
    steps, _, _, columns = out.shape
    groups = LANES // J
    count = columns // LANES
    loads = []
    for i in range(FETCHED):
        part = pl.ds(i * groups * count // FETCHED, groups * count // FETCHED)
        loads.append(pltpu.make_async_copy(blocks_any.at[part], blocks.at[part], load_sem.at[i]))
        loads[-1].start()
    stores = []
    for t in range(steps):
        for q in range(count):
            lanes = slice(q * LANES, (q + 1) * LANES)
            if t == 0 and q % (count // FETCHED) == 0:
                loads[q // (count // FETCHED)].wait()
            rows = blocks[q * groups : (q + 1) * groups, t * J : (t + 1) * J]
            rows = rows.reshape(LANES, LANES).T
            for x in range(XB):
                out[t, :, x, lanes] = rows[x * C : (x + 1) * C]
        if (t + 1) % (steps // SENT) == 0:
            part = pl.ds(t + 1 - steps // SENT, steps // SENT)
            sem = store_sem.at[len(stores)]
            stores.append(pltpu.make_async_copy(out.at[part], out_any.at[part], sem))
            stores[-1].start()
    for store in stores:
        store.wait()


def to_blocks(first, second):
    steps, _, _, columns = first.shape
    shape = (columns // J, 2 * steps * J, LANES)
    return pl.pallas_call(
        scatter_kernel,
        in_specs=[HBM] * 2,
        out_specs=HBM,
        out_shape=pltpu.HBM(shape, F32),
        scratch_shapes=[
            pltpu.VMEM((2, XB, steps, C, columns), F32),
            pltpu.VMEM(shape, F32),
            pltpu.SemaphoreType.DMA((2, XB)),
            pltpu.SemaphoreType.DMA((SENT,)),
        ],
        compiler_params=PARAMS,
    )(*in_hbm(first, second))


def from_blocks(blocks):
    parts, rows, _ = blocks.shape
    shape = (rows // J, C, XB, parts * J)
    return pl.pallas_call(
        gather_kernel,
        in_specs=[ANY],
        out_specs=HBM,
        out_shape=pltpu.HBM(shape, F32),
        scratch_shapes=[
            pltpu.VMEM(blocks.shape, F32),
            pltpu.VMEM(shape, F32),
            pltpu.SemaphoreType.DMA((FETCHED,)),
            pltpu.SemaphoreType.DMA((SENT,)),
        ],
        compiler_params=PARAMS,
    )(blocks)


def angles(mode_list, total_time):
    steps = jnp.arange(total_time, dtype=jnp.int32)
    phase = (mode_list[:, None] * steps[None, :]) % total_time
    angle = phase.astype(F32) * (2.0 * math.pi / total_time)
    both = jnp.stack([jnp.cos(angle), -jnp.sin(angle)], axis=1)
    return both.reshape(2 * mode_list.shape[0], total_time)


def widened(value):
    rows, cols = value.shape
    spread = lax.broadcasted_iota(jnp.int32, (cols, cols * J), 1) // J
    spread = (spread == lax.broadcasted_iota(jnp.int32, (cols, cols * J), 0)).astype(BF16)
    shape = (rows * J, cols * J)
    same = (
        lax.broadcasted_iota(jnp.int32, shape, 0) % J
        == lax.broadcasted_iota(jnp.int32, shape, 1) % J
    )
    for piece in split(value):
        wide = jnp.dot(piece, spread, preferred_element_type=F32)
        wide = jnp.broadcast_to(wide[:, None, :], (rows, J, cols * J)).reshape(shape)
        yield jnp.where(same, wide, 0.0).astype(BF16)


def blocks_of(kernel, places, cols):
    zero = jnp.zeros((C, C), F32)
    rows = [
        jnp.concatenate([kernel[p[y]] if y in p else zero for y in range(cols)], axis=1)
        for p in places
    ]
    return jnp.concatenate(rows, axis=0)


def band(kernel):
    cells = 2 * XB
    own = [{y: x - y + 1 for y in range(cells) if abs(x - y) <= 1} for x in range(cells)]
    before, after = {0: 0}, {cells - 1: 2}
    own = split(blocks_of(kernel, own, cells))
    both = split(blocks_of(kernel, [after, before, after, before], cells))
    edge = split(blocks_of(kernel, [after, {}, {}, before], cells))
    return jnp.concatenate([own[0], own[0], own[1], both[0], edge[1]], axis=0)


def prepare_kernel(scale, tab_ref, tabt_ref, w_ref, k_ref, at, st, wt, vt, fb, bb):
    at[0], at[1] = widened(tab_ref[...])
    st[0], st[1] = widened(tabt_ref[...])
    for l in range(w_ref.shape[0]):

        def body(m, _):
            re, im = w_ref[l, 0, m] * scale, w_ref[l, 1, m] * scale
            wt[0, l, m], wt[1, l, m] = split(jnp.concatenate([re] * XB + [im] * XB, axis=1))
            re, im = re.T, -im.T
            vt[0, l, m], vt[1, l, m] = split(jnp.concatenate([re] * XB + [im] * XB, axis=1))
            return 0

        lax.fori_loop(0, w_ref.shape[2], body, 0)
        taps = [k_ref[l, j] for j in range(3)]
        fb[l] = band(taps)
        bb[l] = band([t.T for t in taps[::-1]])


def prepare(scale, spectral_weights, conv_kernel, mode_list, total_time):
    layers, _, modes, channels, _ = spectral_weights.shape
    tab = angles(mode_list, total_time)
    rows, cols = 2 * modes * J, total_time * J
    shapes = [(2, rows, cols), (2, cols, rows)]
    shapes += [(2, layers, modes, channels, 2 * LANES)] * 2 + [(layers, 8 * LANES, 2 * LANES)] * 2
    return pl.pallas_call(
        functools.partial(prepare_kernel, scale),
        in_specs=[VMEM] * 4,
        out_specs=[VMEM] * 6,
        out_shape=[pltpu.HBM(shape, BF16) for shape in shapes],
        compiler_params=PARAMS,
    )(tab, tab.T, spectral_weights, conv_kernel)


def lane_block():
    return lax.broadcasted_iota(jnp.int32, (1, LANES), 1) // C


def put_split(value, s, high_ref, low_ref):
    high, low = split(value)
    high_ref[s] = high
    low_ref[s] = low


def with_neighbours(ref, s):
    own = ref[s]
    x = lane_block()
    zero = jnp.zeros_like(own)
    before = ref[s - 1] if s > 0 else zero
    after = ref[s + 1] if s + 1 < ref.shape[0] else zero
    edge = jnp.where(x == XB - 1, before, jnp.where(x == 0, after, zero))
    return jnp.concatenate([own, edge], axis=1)


def pair_operand(high_ref, low_ref, s):
    x = lane_block()
    bricks = high_ref.shape[0]

    def edges(ref):
        zero = jnp.zeros_like(ref[s])
        before = ref[s - 1] if s > 0 else zero
        after = ref[s + 2] if s + 2 < bricks else zero
        return jnp.where(x == XB - 1, before, jnp.where(x == 0, after, zero))

    high = [high_ref[s], high_ref[s + 1]]
    low = [low_ref[s], low_ref[s + 1]]
    edge, edge_low = edges(high_ref), edges(low_ref)
    half = LANES // 2
    swapped = jnp.concatenate([edge_low[:, half:], edge_low[:, :half]], axis=1)
    both = jnp.where((x == 0) | (x == XB - 1), edge, swapped)
    return jnp.concatenate([*high, *low, *high, both, edge], axis=1)


def analyse_pair(table, high_ref, low_ref, coef_ref, s):
    right = [jnp.concatenate([r[s], r[s + 1]], axis=1) for r in (high_ref, low_ref)]
    result = dot3(table, right)
    coef_ref[s] = result[:, :LANES]
    coef_ref[s + 1] = result[:, LANES:]


def analyse(table, high_ref, low_ref, coef_ref):
    for s in range(0, high_ref.shape[0], 2):
        analyse_pair(table, high_ref, low_ref, coef_ref, s)


def mixing_rows(w_ref, piece, l, m):
    row = lax.broadcasted_iota(jnp.int32, (LANES, 2 * LANES), 0) // C
    col = lax.broadcasted_iota(jnp.int32, (LANES, 2 * LANES), 1) // C % XB
    wide = jnp.concatenate([w_ref[piece, l, m]] * XB, axis=0)
    return jnp.where(row == col, wide, jnp.zeros_like(wide))


def mix(coef_ref, w_ref, l, mixed_ref):
    bricks = coef_ref.shape[0]
    rows = bricks * J
    for m in range(w_ref.shape[2]):
        re, im = slice(2 * J * m, 2 * J * m + J), slice(2 * J * m + J, 2 * J * (m + 1))
        rh, rl = split(coef_ref[:, re].reshape(rows, LANES))
        ih, il = split(coef_ref[:, im].reshape(rows, LANES))
        left = jnp.concatenate([rh, ih, rl, il], axis=0)
        matrix = jnp.concatenate([mixing_rows(w_ref, piece, l, m) for piece in range(2)], axis=0)
        product = jnp.dot(
            jnp.concatenate([left, left], axis=1), matrix, preferred_element_type=F32
        )
        a = product[:rows] + product[2 * rows : 3 * rows]
        b = product[rows : 2 * rows] + product[3 * rows :]
        mixed_ref[:, re] = (a[:, :LANES] - b[:, LANES:]).reshape(bricks, J, LANES)
        mixed_ref[:, im] = (a[:, LANES:] + b[:, :LANES]).reshape(bricks, J, LANES)


def synthesise(table, mixed_ref, matrix, high_ref, low_ref, emit):
    for s in range(0, mixed_ref.shape[0], 2):
        right = split(jnp.concatenate([mixed_ref[s], mixed_ref[s + 1]], axis=1))
        total = dot3(table, right) + jnp.dot(
            pair_operand(high_ref, low_ref, s), matrix, preferred_element_type=F32
        )
        emit(s, total[:, :LANES])
        emit(s + 1, total[:, LANES:])


def gelu_parts(z):
    cdf = 0.5 * (1.0 + lax.erf(z * math.sqrt(0.5)))
    slope = cdf + z * (jnp.exp(-0.5 * z * z) * (1.0 / math.sqrt(2.0 * math.pi)))
    return z * cdf, slope


STORED = 4


def layers_kernel(*refs):
    both = refs[0]
    small_any = refs[1:7]
    out_any = refs[7]
    kept_any = refs[8:20]
    small = refs[20:26]
    kept = refs[26:38]
    field, sens, slope1, out, mixed, load_sem, small_sem, store_sem = refs[38:]
    analysis_ref, synthesis_ref, mix_forward, mix_backward, band_forward, band_backward = small
    coef1, coef2, sens1, sens2, x1h, x1l, x2h, x2l, z1h, z1l, z2h, z2l = kept
    groups, bricks, lines, _ = both.shape
    lines = lines // 2
    copy = pltpu.make_async_copy

    tables = [copy(a, r, small_sem.at[i]) for i, (a, r) in enumerate(zip(small_any, small))]
    half = bricks // 2
    loads = [
        copy(both.at[:, at, pl.ds(0, lines)], field.at[:, at], load_sem.at[i])
        for i, at in enumerate((pl.ds(0, half), pl.ds(half, half)))
    ]
    loads.append(copy(both.at[:, :, pl.ds(lines, lines)], sens, load_sem.at[2]))
    for load in (tables[0], loads[0], loads[1], tables[2], tables[1], tables[4]):
        load.start()
    stores = []

    def store(source, target):
        stores.append(copy(source, target, store_sem.at[len(stores)]))
        stores[-1].start()

    def keep(*places):
        for i in places:
            store(kept[i], kept_any[i])

    def brick(ref, s):
        return ref[:, s].reshape(-1, LANES)

    def first_out(s, value):
        value, slope = gelu_parts(value)
        slope1[s] = slope
        put_split(value, s, x2h, x2l)

    def second_out(s, value):
        put_split(brick(sens, s) * gelu_parts(value)[1], s, z2h, z2l)

    def second_back(s, value):
        put_split(value * slope1[s], s, z1h, z1l)

    def first_back(s, value):
        out[:, s] = value.reshape(groups, lines, LANES)
        if s % STORED == STORED - 1:
            done = pl.ds(s - STORED + 1, STORED)
            store(out.at[:, done], out_any.at[:, done])

    tables[0].wait()
    analysis = (analysis_ref[0], analysis_ref[1])
    for s in range(0, bricks, 2):
        if s % half == 0:
            loads[s // half].wait()
        for o in (s, s + 1):
            put_split(brick(field, o), o, x1h, x1l)
        analyse_pair(analysis, x1h, x1l, coef1, s)
    for load in (loads[2], tables[3], tables[5]):
        load.start()
    keep(0, 4, 5)
    tables[2].wait()
    mix(coef1, mix_forward, 0, mixed)
    tables[1].wait()
    tables[4].wait()
    synthesis = (synthesis_ref[0], synthesis_ref[1])
    synthesise(synthesis, mixed, band_forward[0], x1h, x1l, first_out)
    analyse(analysis, x2h, x2l, coef2)
    keep(1, 6, 7)
    mix(coef2, mix_forward, 1, mixed)
    loads[2].wait()
    synthesise(synthesis, mixed, band_forward[1], x2h, x2l, second_out)
    analyse(analysis, z2h, z2l, sens2)
    keep(3, 10, 11)
    tables[3].wait()
    mix(sens2, mix_backward, 1, mixed)
    tables[5].wait()
    synthesise(synthesis, mixed, band_backward[1], z2h, z2l, second_back)
    analyse(analysis, z1h, z1l, sens1)
    keep(2, 8, 9)
    mix(sens1, mix_backward, 0, mixed)
    synthesise(synthesis, mixed, band_backward[0], z1h, z1l, first_back)
    for done in stores:
        done.wait()


def run_layers(both, *tables):
    groups, bricks, lines, _ = both.shape
    _, modes, rows = tables[0].shape
    coef = ((bricks, modes, LANES), F32)
    full = ((bricks, rows, LANES), F32)
    half = ((bricks, rows, LANES), BF16)
    result = ((groups, bricks, lines // 2, LANES), F32)
    kept = [coef] * 4 + [half] * 8
    scratch = [(t.shape, t.dtype) for t in tables] + kept + [result, result, full, result, coef]
    return pl.pallas_call(
        layers_kernel,
        in_specs=[ANY] + [HBM] * 6,
        out_specs=[HBM] * 13,
        out_shape=[pltpu.HBM(*o) for o in (result, *kept)],
        scratch_shapes=[pltpu.VMEM(*o) for o in scratch]
        + [
            pltpu.SemaphoreType.DMA((3,)),
            pltpu.SemaphoreType.DMA((6,)),
            pltpu.SemaphoreType.DMA((len(kept) + bricks // STORED,)),
        ],
        compiler_params=PARAMS,
    )(both, *in_hbm(*tables))


ROWS = ((0,), (0,))
TAPS = 3
RADIX = 4


def weight_kernel(scale, me_ref, *refs):
    coef1_any, coef2_any, sens1_any, sens2_any = refs[:4]
    half_any = refs[4:12]
    modes = refs[0].shape[1] // (2 * J)
    outs = refs[12 : 12 + RADIX]
    coef1, coef2, sens1, sens2 = refs[12 + RADIX : 16 + RADIX]
    half = refs[16 + RADIX : 24 + RADIX]
    spectral, load_sem, half_sem = refs[24 + RADIX :]
    bricks = coef1.shape[0]
    copy = pltpu.make_async_copy

    halves = [
        [
            copy(a.at[s], r.at[s], half_sem.at[i, s])
            for i, (a, r) in enumerate(zip(half_any, half))
        ]
        for s in range(bricks)
    ]
    pairs = zip((coef1_any, coef2_any, sens1_any, sens2_any), (coef1, coef2, sens1, sens2))
    loads = [copy(a, r, load_sem.at[i]) for i, (a, r) in enumerate(pairs)]
    x1h, x1l, x2h, x2l, z1h, z1l, z2h, z2l = half
    for l in range(2):
        for s in range(bricks):
            for i in (0, 1, 4, 5) if l == 0 else (2, 3, 6, 7):
                halves[s][i].start()
    for c in loads:
        c.start()

    blocks = []
    for l, (xh, xl, zh, zl) in enumerate(((x1h, x1l, z1h, z1l), (x2h, x2l, z2h, z2l))):
        total = jnp.zeros((LANES, 2 * LANES), F32)
        for s in range(bricks):
            for ahead in (0, 1) if s == 0 else (s + 1,):
                if ahead < bricks:
                    for i in (0, 1, 4, 5) if l == 0 else (2, 3, 6, 7):
                        halves[ahead][i].wait()
            value = (with_neighbours(xh, s), with_neighbours(xl, s))
            total = total + dot3((zh[s], zl[s]), value, ROWS)
        for j in range(TAPS):
            pairs = [(x, x - j + 1) for x in range(XB) if 0 <= x - j + 1 < XB]
            tap = sum(total[y * C : (y + 1) * C, x * C : (x + 1) * C] for x, y in pairs)
            if j == 0:
                tap = tap + total[:C, LANES + (XB - 1) * C :]
            if j == 2:
                tap = tap + total[(XB - 1) * C :, LANES : LANES + C]
            blocks.append(tap)
    half_rows = C // 2
    first = jnp.concatenate(blocks[:4], axis=1)
    rest = [b[i * half_rows : (i + 1) * half_rows] for b in blocks[4:] for i in range(2)]
    kernels = jnp.concatenate([first, jnp.concatenate(rest, axis=1)], axis=0)

    for c in loads:
        c.wait()
    for m in range(modes):
        re, im = slice(2 * J * m, 2 * J * m + J), slice(2 * J * m + J, 2 * J * (m + 1))
        pieces = []
        for coef, sens in ((coef1, sens1), (coef2, sens2)):
            cr, ci, zr, zi = (
                r[:, p].reshape(bricks * J, LANES)
                for r, p in ((coef, re), (coef, im), (sens, re), (sens, im))
            )
            left = jnp.concatenate([cr, ci], axis=0)
            right = jnp.concatenate(
                [jnp.concatenate([zr, zi], axis=1), jnp.concatenate([zi, -zr], axis=1)], axis=0
            )
            product = dot3(split(left), split(right), ROWS) * scale
            for part in range(2):
                pieces.append(
                    sum(
                        product[x * C : (x + 1) * C, part * LANES + x * C : part * LANES + (x + 1) * C]
                        for x in range(XB)
                    )
                )
        spectral[m] = jnp.concatenate(pieces, axis=1)
    for r, out in enumerate(outs):
        high = (me_ref[0] + r) % RADIX
        for q in range(RADIX):
            low = (me_ref[1] + q) % RADIX
            out[q * C : (q + 1) * C] = spectral[high * RADIX + low]
        out[RADIX * C :] = kernels


def weight_gradients(scale, me, *operands):
    modes = operands[0].shape[1] // (2 * J)
    rows = RADIX * C + 2 * TAPS * C // XB
    return pl.pallas_call(
        functools.partial(weight_kernel, scale),
        in_specs=[pl.BlockSpec(memory_space=pltpu.SMEM)] + [HBM] * 12,
        out_specs=[VMEM] * RADIX,
        out_shape=[jax.ShapeDtypeStruct((rows, LANES), F32)] * RADIX,
        scratch_shapes=[pltpu.VMEM(o.shape, o.dtype) for o in operands]
        + [
            pltpu.VMEM((modes, C, LANES), F32),
            pltpu.SemaphoreType.DMA((4,)),
            pltpu.SemaphoreType.DMA((8, operands[0].shape[0])),
        ],
        compiler_params=PARAMS,
    )(me, *in_hbm(*operands))


def shifted(pieces, axis, size, stride):
    count = len(pieces)
    got = [pieces[0]]
    for r in range(1, count):
        perm = []
        for i in range(size):
            digit = i // stride % count
            perm.append((i, i + ((digit + r) % count - digit) * stride))
        got.append(lax.ppermute(pieces[r], axis, perm))
    return got


def ring_sum(values):
    while len(values) > 1:
        half = len(values) // 2
        values = [values[i] + values[i + half] for i in range(half)]
    return values[0]


def split_sum_kernel(*refs):
    total = ring_sum([r[...] for r in refs[:RADIX]])
    for q, out in enumerate(refs[RADIX:]):
        out[:C] = total[q * C : (q + 1) * C]
        out[C:] = total[RADIX * C :]


def split_sum(pieces):
    rows = pieces[0].shape[0] - (RADIX - 1) * C
    return pl.pallas_call(
        split_sum_kernel,
        in_specs=[VMEM] * RADIX,
        out_specs=[VMEM] * RADIX,
        out_shape=[jax.ShapeDtypeStruct((rows, LANES), F32)] * RADIX,
        compiler_params=PARAMS,
    )(*pieces)


def finish_kernel(one_ref, other_ref, mode_ref, kernel_ref):
    total = one_ref[...] + other_ref[...]
    layers = mode_ref.shape[0]
    for l in range(layers):
        for part in range(2):
            at = (2 * l + part) * C
            mode_ref[l, part, 0] = total[:C, at : at + C]
    low = C // 2
    blocks = [total[C : 2 * C, b * C : (b + 1) * C] for b in range(XB)]
    for b in range(2):
        top, bottom = (total[2 * C :, (2 * b + i) * C : (2 * b + i + 1) * C] for i in range(2))
        blocks.append(jnp.concatenate([top, bottom], axis=0))
    for i, block in enumerate(blocks):
        kernel_ref[i // TAPS, i % TAPS] = block.T


def finish(one, other, layers):
    return pl.pallas_call(
        finish_kernel,
        in_specs=[VMEM] * 2,
        out_specs=[VMEM] * 2,
        out_shape=[
            jax.ShapeDtypeStruct((layers, 2, 1, C, C), F32),
            jax.ShapeDtypeStruct((layers, TAPS, C, C), F32),
        ],
        compiler_params=PARAMS,
    )(one, other)


def on_device(input_field, cotangent, spectral_weights, conv_kernel, mode_list):
    groups = lax.axis_size("tm")
    bricks = lax.axis_size("space")
    everyone = ("tm", "space")
    steps = input_field.shape[0]
    total_time = steps * groups
    layers, _, modes, _, _ = spectral_weights.shape
    scale = 2.0 / total_time
    exchange = functools.partial(lax.all_to_all, split_axis=0, concat_axis=0, tiled=True)

    received = exchange(to_blocks(input_field, cotangent), everyone)
    prepared = prepare(scale, spectral_weights, conv_kernel, mode_list, total_time)
    received, prepared = lax.optimization_barrier((received, prepared))
    grad, *kept = run_layers(
        received.reshape(groups, bricks, 2 * steps * J, LANES), *prepared
    )
    returned = exchange(grad.reshape(groups * bricks, steps * J, LANES), everyone)
    me = lax.axis_index("tm").astype(jnp.int32)
    place = jnp.stack([me // RADIX, me % RADIX])
    pieces = weight_gradients(scale, place, *kept)
    pieces = split_sum(shifted(pieces, "tm", groups, RADIX))
    grad_input, pieces = lax.optimization_barrier(
        (from_blocks(returned), shifted(pieces, "tm", groups, 1))
    )
    total = ring_sum(pieces)
    total = ring_sum(shifted([total] * RADIX, "space", bricks, bricks // RADIX))
    mode_total, kernel_total = finish(*shifted([total] * 2, "space", bricks, 1), layers)
    return (grad_input, mode_total, kernel_total)


def solution(mesh):
    placed = (P("tm", None, "space", None), P("tm", None, "space", None), P(), P(), P())
    return jax.shard_map(
        on_device,
        mesh=mesh,
        in_specs=placed,
        out_specs=(P("tm", None, "space", None), P(None, None, "tm", None, None), P()),
        check_vma=False,
    )
```

```python
import functools
import math

import jax
import jax.numpy as jnp
from jax import lax
from jax.experimental import pallas as pl
from jax.experimental.pallas import tpu as pltpu
from jax.sharding import PartitionSpec as P

F32 = jnp.float32
BF16 = jnp.bfloat16
LANES = 128
J = 8
XB = 4
C = 32
VMEM = pl.BlockSpec(memory_space=pltpu.VMEM)
ANY = pl.BlockSpec(memory_space=pl.ANY)
HBM = pl.BlockSpec(memory_space=pltpu.HBM)
PARAMS = pltpu.CompilerParams(vmem_limit_bytes=40 * 1024 * 1024)


def in_hbm(*values):
    return [pltpu.with_memory_space_constraint(v, pltpu.HBM) for v in values]


def split(value):
    high = value.astype(BF16)
    low = (value - high.astype(F32)).astype(BF16)
    return high, low


def dot3(left, right, dims=((1,), (0,))):
    (lh, ll), (rh, rl) = left, right
    (lc,), (rc,) = dims
    a = jnp.concatenate([lh, ll, lh], axis=lc)
    b = jnp.concatenate([rh, rh, rl], axis=rc)
    return lax.dot_general(a, b, (dims, ((), ())), preferred_element_type=F32)


FETCHED = 1
SENT = 4


def scatter_kernel(first_any, second_any, out_any, field, out, load_sem, store_sem):
    _, _, steps, _, columns = field.shape
    groups = LANES // J
    loads = [
        pltpu.make_async_copy(
            source.at[:, :, x, :], field.at[which, x], load_sem.at[which, x]
        )
        for which, source in enumerate((first_any, second_any))
        for x in range(XB)
    ]
    for load in loads:
        load.start()
    stores = []
    count = columns // LANES
    for which in range(2):
        for load in loads[which * XB : (which + 1) * XB]:
            load.wait()
        for q in range(count):
            lanes = slice(q * LANES, (q + 1) * LANES)
            for t in range(steps):
                at = (which * steps + t) * J
                rows = jnp.concatenate([field[which, x, t, :, lanes] for x in range(XB)], axis=0)
                rows = rows.T.reshape(groups, J, LANES)
                out[q * groups : (q + 1) * groups, at : at + J] = rows
            if (q + 1) % (count // SENT) == 0:
                size = groups * count // SENT
                part = pl.ds((q + 1) * groups - size, size)
                lines = pl.ds(which * steps * J, steps * J)
                stores.append(
                    pltpu.make_async_copy(
                        out.at[part, lines], out_any.at[part, lines], store_sem.at[len(stores)]
                    )
                )
                stores[-1].start()
    for store in stores:
        store.wait()


def gather_kernel(blocks_any, out_any, blocks, out, load_sem, store_sem):
    steps, _, _, columns = out.shape
    groups = LANES // J
    count = columns // LANES
    loads = []
    for i in range(FETCHED):
        part = pl.ds(i * groups * count // FETCHED, groups * count // FETCHED)
        loads.append(pltpu.make_async_copy(blocks_any.at[part], blocks.at[part], load_sem.at[i]))
        loads[-1].start()
    stores = []
    for t in range(steps):
        for q in range(count):
            lanes = slice(q * LANES, (q + 1) * LANES)
            if t == 0 and q % (count // FETCHED) == 0:
                loads[q // (count // FETCHED)].wait()
            rows = blocks[q * groups : (q + 1) * groups, t * J : (t + 1) * J]
            rows = rows.reshape(LANES, LANES).T
            for x in range(XB):
                out[t, :, x, lanes] = rows[x * C : (x + 1) * C]
        if (t + 1) % (steps // SENT) == 0:
            part = pl.ds(t + 1 - steps // SENT, steps // SENT)
            sem = store_sem.at[len(stores)]
            stores.append(pltpu.make_async_copy(out.at[part], out_any.at[part], sem))
            stores[-1].start()
    for store in stores:
        store.wait()


def to_blocks(first, second):
    steps, _, _, columns = first.shape
    shape = (columns // J, 2 * steps * J, LANES)
    return pl.pallas_call(
        scatter_kernel,
        in_specs=[HBM] * 2,
        out_specs=HBM,
        out_shape=pltpu.HBM(shape, F32),
        scratch_shapes=[
            pltpu.VMEM((2, XB, steps, C, columns), F32),
            pltpu.VMEM(shape, F32),
            pltpu.SemaphoreType.DMA((2, XB)),
            pltpu.SemaphoreType.DMA((2 * SENT,)),
        ],
        compiler_params=PARAMS,
    )(*in_hbm(first, second))


def from_blocks(blocks):
    parts, rows, _ = blocks.shape
    shape = (rows // J, C, XB, parts * J)
    return pl.pallas_call(
        gather_kernel,
        in_specs=[ANY],
        out_specs=HBM,
        out_shape=pltpu.HBM(shape, F32),
        scratch_shapes=[
            pltpu.VMEM(blocks.shape, F32),
            pltpu.VMEM(shape, F32),
            pltpu.SemaphoreType.DMA((FETCHED,)),
            pltpu.SemaphoreType.DMA((SENT,)),
        ],
        compiler_params=PARAMS,
    )(blocks)


def angles(mode_list, total_time):
    steps = jnp.arange(total_time, dtype=jnp.int32)
    phase = (mode_list[:, None] * steps[None, :]) % total_time
    angle = phase.astype(F32) * (2.0 * math.pi / total_time)
    both = jnp.stack([jnp.cos(angle), -jnp.sin(angle)], axis=1)
    return both.reshape(2 * mode_list.shape[0], total_time)


def widened(value):
    rows, cols = value.shape
    spread = lax.broadcasted_iota(jnp.int32, (cols, cols * J), 1) // J
    spread = (spread == lax.broadcasted_iota(jnp.int32, (cols, cols * J), 0)).astype(BF16)
    shape = (rows * J, cols * J)
    same = (
        lax.broadcasted_iota(jnp.int32, shape, 0) % J
        == lax.broadcasted_iota(jnp.int32, shape, 1) % J
    )
    for piece in split(value):
        wide = jnp.dot(piece, spread, preferred_element_type=F32)
        wide = jnp.broadcast_to(wide[:, None, :], (rows, J, cols * J)).reshape(shape)
        yield jnp.where(same, wide, 0.0).astype(BF16)


def blocks_of(kernel, places, cols):
    zero = jnp.zeros((C, C), F32)
    rows = [
        jnp.concatenate([kernel[p[y]] if y in p else zero for y in range(cols)], axis=1)
        for p in places
    ]
    return jnp.concatenate(rows, axis=0)


def band(kernel):
    cells = 2 * XB
    own = [{y: x - y + 1 for y in range(cells) if abs(x - y) <= 1} for x in range(cells)]
    before, after = {0: 0}, {cells - 1: 2}
    own = split(blocks_of(kernel, own, cells))
    both = split(blocks_of(kernel, [after, before, after, before], cells))
    edge = split(blocks_of(kernel, [after, {}, {}, before], cells))
    return jnp.concatenate([own[0], own[0], own[1], both[0], edge[1]], axis=0)


def prepare_kernel(scale, tab_ref, tabt_ref, w_ref, k_ref, at, st, wt, vt, fb, bb):
    at[0], at[1] = widened(tab_ref[...])
    st[0], st[1] = widened(tabt_ref[...])
    for l in range(w_ref.shape[0]):

        def body(m, _):
            re, im = w_ref[l, 0, m] * scale, w_ref[l, 1, m] * scale
            wt[0, l, m], wt[1, l, m] = split(jnp.concatenate([re] * XB + [im] * XB, axis=1))
            re, im = re.T, -im.T
            vt[0, l, m], vt[1, l, m] = split(jnp.concatenate([re] * XB + [im] * XB, axis=1))
            return 0

        lax.fori_loop(0, w_ref.shape[2], body, 0)
        taps = [k_ref[l, j] for j in range(3)]
        fb[l] = band(taps)
        bb[l] = band([t.T for t in taps[::-1]])


def prepare(scale, spectral_weights, conv_kernel, mode_list, total_time):
    layers, _, modes, channels, _ = spectral_weights.shape
    tab = angles(mode_list, total_time)
    rows, cols = 2 * modes * J, total_time * J
    shapes = [(2, rows, cols), (2, cols, rows)]
    shapes += [(2, layers, modes, channels, 2 * LANES)] * 2 + [(layers, 8 * LANES, 2 * LANES)] * 2
    return pl.pallas_call(
        functools.partial(prepare_kernel, scale),
        in_specs=[VMEM] * 4,
        out_specs=[VMEM] * 6,
        out_shape=[pltpu.HBM(shape, BF16) for shape in shapes],
        compiler_params=PARAMS,
    )(tab, tab.T, spectral_weights, conv_kernel)


def lane_block():
    return lax.broadcasted_iota(jnp.int32, (1, LANES), 1) // C


def put_split(value, s, high_ref, low_ref):
    high, low = split(value)
    high_ref[s] = high
    low_ref[s] = low


def with_neighbours(ref, s):
    own = ref[s]
    x = lane_block()
    zero = jnp.zeros_like(own)
    before = ref[s - 1] if s > 0 else zero
    after = ref[s + 1] if s + 1 < ref.shape[0] else zero
    edge = jnp.where(x == XB - 1, before, jnp.where(x == 0, after, zero))
    return jnp.concatenate([own, edge], axis=1)


def pair_operand(high_ref, low_ref, s):
    x = lane_block()
    bricks = high_ref.shape[0]

    def edges(ref):
        zero = jnp.zeros_like(ref[s])
        before = ref[s - 1] if s > 0 else zero
        after = ref[s + 2] if s + 2 < bricks else zero
        return jnp.where(x == XB - 1, before, jnp.where(x == 0, after, zero))

    high = [high_ref[s], high_ref[s + 1]]
    low = [low_ref[s], low_ref[s + 1]]
    edge, edge_low = edges(high_ref), edges(low_ref)
    half = LANES // 2
    swapped = jnp.concatenate([edge_low[:, half:], edge_low[:, :half]], axis=1)
    both = jnp.where((x == 0) | (x == XB - 1), edge, swapped)
    return jnp.concatenate([*high, *low, *high, both, edge], axis=1)


def analyse_pair(table, high_ref, low_ref, coef_ref, s):
    right = [jnp.concatenate([r[s], r[s + 1]], axis=1) for r in (high_ref, low_ref)]
    result = dot3(table, right)
    coef_ref[s] = result[:, :LANES]
    coef_ref[s + 1] = result[:, LANES:]


def analyse(table, high_ref, low_ref, coef_ref):
    for s in range(0, high_ref.shape[0], 2):
        analyse_pair(table, high_ref, low_ref, coef_ref, s)


def mixing_rows(w_ref, piece, l, m):
    row = lax.broadcasted_iota(jnp.int32, (LANES, 2 * LANES), 0) // C
    col = lax.broadcasted_iota(jnp.int32, (LANES, 2 * LANES), 1) // C % XB
    wide = jnp.concatenate([w_ref[piece, l, m]] * XB, axis=0)
    return jnp.where(row == col, wide, jnp.zeros_like(wide))


def mix(coef_ref, w_ref, l, mixed_ref):
    bricks = coef_ref.shape[0]
    rows = bricks * J
    for m in range(w_ref.shape[2]):
        re, im = slice(2 * J * m, 2 * J * m + J), slice(2 * J * m + J, 2 * J * (m + 1))
        rh, rl = split(coef_ref[:, re].reshape(rows, LANES))
        ih, il = split(coef_ref[:, im].reshape(rows, LANES))
        left = jnp.concatenate([rh, ih, rl, il], axis=0)
        matrix = jnp.concatenate([mixing_rows(w_ref, piece, l, m) for piece in range(2)], axis=0)
        product = jnp.dot(
            jnp.concatenate([left, left], axis=1), matrix, preferred_element_type=F32
        )
        a = product[:rows] + product[2 * rows : 3 * rows]
        b = product[rows : 2 * rows] + product[3 * rows :]
        mixed_ref[:, re] = (a[:, :LANES] - b[:, LANES:]).reshape(bricks, J, LANES)
        mixed_ref[:, im] = (a[:, LANES:] + b[:, :LANES]).reshape(bricks, J, LANES)


def synthesise(table, mixed_ref, matrix, high_ref, low_ref, emit):
    for s in range(0, mixed_ref.shape[0], 2):
        right = split(jnp.concatenate([mixed_ref[s], mixed_ref[s + 1]], axis=1))
        total = dot3(table, right) + jnp.dot(
            pair_operand(high_ref, low_ref, s), matrix, preferred_element_type=F32
        )
        emit(s, total[:, :LANES])
        emit(s + 1, total[:, LANES:])


def gelu_parts(z):
    cdf = 0.5 * (1.0 + lax.erf(z * math.sqrt(0.5)))
    slope = cdf + z * (jnp.exp(-0.5 * z * z) * (1.0 / math.sqrt(2.0 * math.pi)))
    return z * cdf, slope


STORED = 4


def layers_kernel(*refs):
    both = refs[0]
    small_any = refs[1:7]
    out_any = refs[7]
    kept_any = refs[8:20]
    small = refs[20:26]
    kept = refs[26:38]
    field, sens, slope1, out, mixed, load_sem, small_sem, store_sem = refs[38:]
    analysis_ref, synthesis_ref, mix_forward, mix_backward, band_forward, band_backward = small
    coef1, coef2, sens1, sens2, x1h, x1l, x2h, x2l, z1h, z1l, z2h, z2l = kept
    groups, bricks, lines, _ = both.shape
    lines = lines // 2
    copy = pltpu.make_async_copy

    tables = [copy(a, r, small_sem.at[i]) for i, (a, r) in enumerate(zip(small_any, small))]
    half = bricks // 2
    loads = [
        copy(both.at[:, at, pl.ds(0, lines)], field.at[:, at], load_sem.at[i])
        for i, at in enumerate((pl.ds(0, half), pl.ds(half, half)))
    ]
    loads.append(copy(both.at[:, :, pl.ds(lines, lines)], sens, load_sem.at[2]))
    for load in (tables[0], loads[0], loads[1], tables[2], tables[1], tables[4]):
        load.start()
    stores = []

    def store(source, target):
        stores.append(copy(source, target, store_sem.at[len(stores)]))
        stores[-1].start()

    def keep(*places):
        for i in places:
            store(kept[i], kept_any[i])

    def brick(ref, s):
        return ref[:, s].reshape(-1, LANES)

    def first_out(s, value):
        value, slope = gelu_parts(value)
        slope1[s] = slope
        put_split(value, s, x2h, x2l)

    def second_out(s, value):
        put_split(brick(sens, s) * gelu_parts(value)[1], s, z2h, z2l)

    def second_back(s, value):
        put_split(value * slope1[s], s, z1h, z1l)

    def first_back(s, value):
        out[:, s] = value.reshape(groups, lines, LANES)
        if s % STORED == STORED - 1:
            done = pl.ds(s - STORED + 1, STORED)
            store(out.at[:, done], out_any.at[:, done])

    tables[0].wait()
    analysis = (analysis_ref[0], analysis_ref[1])
    for s in range(0, bricks, 2):
        if s % half == 0:
            loads[s // half].wait()
        for o in (s, s + 1):
            put_split(brick(field, o), o, x1h, x1l)
        analyse_pair(analysis, x1h, x1l, coef1, s)
    for load in (loads[2], tables[3], tables[5]):
        load.start()
    keep(0, 4, 5)
    tables[2].wait()
    mix(coef1, mix_forward, 0, mixed)
    tables[1].wait()
    tables[4].wait()
    synthesis = (synthesis_ref[0], synthesis_ref[1])
    synthesise(synthesis, mixed, band_forward[0], x1h, x1l, first_out)
    analyse(analysis, x2h, x2l, coef2)
    keep(1, 6, 7)
    mix(coef2, mix_forward, 1, mixed)
    loads[2].wait()
    synthesise(synthesis, mixed, band_forward[1], x2h, x2l, second_out)
    analyse(analysis, z2h, z2l, sens2)
    keep(3, 10, 11)
    tables[3].wait()
    mix(sens2, mix_backward, 1, mixed)
    tables[5].wait()
    synthesise(synthesis, mixed, band_backward[1], z2h, z2l, second_back)
    analyse(analysis, z1h, z1l, sens1)
    keep(2, 8, 9)
    mix(sens1, mix_backward, 0, mixed)
    synthesise(synthesis, mixed, band_backward[0], z1h, z1l, first_back)
    for done in stores:
        done.wait()


def run_layers(both, *tables):
    groups, bricks, lines, _ = both.shape
    _, modes, rows = tables[0].shape
    coef = ((bricks, modes, LANES), F32)
    full = ((bricks, rows, LANES), F32)
    half = ((bricks, rows, LANES), BF16)
    result = ((groups, bricks, lines // 2, LANES), F32)
    kept = [coef] * 4 + [half] * 8
    scratch = [(t.shape, t.dtype) for t in tables] + kept + [result, result, full, result, coef]
    return pl.pallas_call(
        layers_kernel,
        in_specs=[ANY] + [HBM] * 6,
        out_specs=[HBM] * 13,
        out_shape=[pltpu.HBM(*o) for o in (result, *kept)],
        scratch_shapes=[pltpu.VMEM(*o) for o in scratch]
        + [
            pltpu.SemaphoreType.DMA((3,)),
            pltpu.SemaphoreType.DMA((6,)),
            pltpu.SemaphoreType.DMA((len(kept) + bricks // STORED,)),
        ],
        compiler_params=PARAMS,
    )(both, *in_hbm(*tables))


ROWS = ((0,), (0,))
TAPS = 3
RADIX = 4


def weight_kernel(scale, me_ref, *refs):
    coef1_any, coef2_any, sens1_any, sens2_any = refs[:4]
    half_any = refs[4:12]
    modes = refs[0].shape[1] // (2 * J)
    outs = refs[12 : 12 + RADIX]
    coef1, coef2, sens1, sens2 = refs[12 + RADIX : 16 + RADIX]
    half = refs[16 + RADIX : 24 + RADIX]
    spectral, load_sem, half_sem = refs[24 + RADIX :]
    bricks = coef1.shape[0]
    copy = pltpu.make_async_copy

    halves = [
        [
            copy(a.at[s], r.at[s], half_sem.at[i, s])
            for i, (a, r) in enumerate(zip(half_any, half))
        ]
        for s in range(bricks)
    ]
    pairs = zip((coef1_any, coef2_any, sens1_any, sens2_any), (coef1, coef2, sens1, sens2))
    loads = [copy(a, r, load_sem.at[i]) for i, (a, r) in enumerate(pairs)]
    x1h, x1l, x2h, x2l, z1h, z1l, z2h, z2l = half
    for l in range(2):
        for s in range(bricks):
            for i in (0, 1, 4, 5) if l == 0 else (2, 3, 6, 7):
                halves[s][i].start()
    for c in loads:
        c.start()

    blocks = []
    for l, (xh, xl, zh, zl) in enumerate(((x1h, x1l, z1h, z1l), (x2h, x2l, z2h, z2l))):
        total = jnp.zeros((LANES, 2 * LANES), F32)
        for s in range(bricks):
            for ahead in (0, 1) if s == 0 else (s + 1,):
                if ahead < bricks:
                    for i in (0, 1, 4, 5) if l == 0 else (2, 3, 6, 7):
                        halves[ahead][i].wait()
            value = (with_neighbours(xh, s), with_neighbours(xl, s))
            total = total + dot3((zh[s], zl[s]), value, ROWS)
        for j in range(TAPS):
            pairs = [(x, x - j + 1) for x in range(XB) if 0 <= x - j + 1 < XB]
            tap = sum(total[y * C : (y + 1) * C, x * C : (x + 1) * C] for x, y in pairs)
            if j == 0:
                tap = tap + total[:C, LANES + (XB - 1) * C :]
            if j == 2:
                tap = tap + total[(XB - 1) * C :, LANES : LANES + C]
            blocks.append(tap)
    half_rows = C // 2
    first = jnp.concatenate(blocks[:4], axis=1)
    rest = [b[i * half_rows : (i + 1) * half_rows] for b in blocks[4:] for i in range(2)]
    kernels = jnp.concatenate([first, jnp.concatenate(rest, axis=1)], axis=0)

    for c in loads:
        c.wait()
    for m in range(modes):
        re, im = slice(2 * J * m, 2 * J * m + J), slice(2 * J * m + J, 2 * J * (m + 1))
        pieces = []
        for coef, sens in ((coef1, sens1), (coef2, sens2)):
            cr, ci, zr, zi = (
                r[:, p].reshape(bricks * J, LANES)
                for r, p in ((coef, re), (coef, im), (sens, re), (sens, im))
            )
            left = jnp.concatenate([cr, ci], axis=0)
            right = jnp.concatenate(
                [jnp.concatenate([zr, zi], axis=1), jnp.concatenate([zi, -zr], axis=1)], axis=0
            )
            product = dot3(split(left), split(right), ROWS) * scale
            for part in range(2):
                pieces.append(
                    sum(
                        product[x * C : (x + 1) * C, part * LANES + x * C : part * LANES + (x + 1) * C]
                        for x in range(XB)
                    )
                )
        spectral[m] = jnp.concatenate(pieces, axis=1)
    for r, out in enumerate(outs):
        high = (me_ref[0] + r) % RADIX
        for q in range(RADIX):
            low = (me_ref[1] + q) % RADIX
            out[q * C : (q + 1) * C] = spectral[high * RADIX + low]
        out[RADIX * C :] = kernels


def weight_gradients(scale, me, *operands):
    modes = operands[0].shape[1] // (2 * J)
    rows = RADIX * C + 2 * TAPS * C // XB
    return pl.pallas_call(
        functools.partial(weight_kernel, scale),
        in_specs=[pl.BlockSpec(memory_space=pltpu.SMEM)] + [HBM] * 12,
        out_specs=[VMEM] * RADIX,
        out_shape=[jax.ShapeDtypeStruct((rows, LANES), F32)] * RADIX,
        scratch_shapes=[pltpu.VMEM(o.shape, o.dtype) for o in operands]
        + [
            pltpu.VMEM((modes, C, LANES), F32),
            pltpu.SemaphoreType.DMA((4,)),
            pltpu.SemaphoreType.DMA((8, operands[0].shape[0])),
        ],
        compiler_params=PARAMS,
    )(me, *in_hbm(*operands))


def shifted(pieces, axis, size, stride):
    count = len(pieces)
    got = [pieces[0]]
    for r in range(1, count):
        perm = []
        for i in range(size):
            digit = i // stride % count
            perm.append((i, i + ((digit + r) % count - digit) * stride))
        got.append(lax.ppermute(pieces[r], axis, perm))
    return got


def ring_sum(values):
    while len(values) > 1:
        half = len(values) // 2
        values = [values[i] + values[i + half] for i in range(half)]
    return values[0]


def split_sum_kernel(*refs):
    total = ring_sum([r[...] for r in refs[:RADIX]])
    for q, out in enumerate(refs[RADIX:]):
        out[:C] = total[q * C : (q + 1) * C]
        out[C:] = total[RADIX * C :]


def split_sum(pieces):
    rows = pieces[0].shape[0] - (RADIX - 1) * C
    return pl.pallas_call(
        split_sum_kernel,
        in_specs=[VMEM] * RADIX,
        out_specs=[VMEM] * RADIX,
        out_shape=[jax.ShapeDtypeStruct((rows, LANES), F32)] * RADIX,
        compiler_params=PARAMS,
    )(*pieces)


def finish_kernel(one_ref, other_ref, mode_ref, kernel_ref):
    total = one_ref[...] + other_ref[...]
    layers = mode_ref.shape[0]
    for l in range(layers):
        for part in range(2):
            at = (2 * l + part) * C
            mode_ref[l, part, 0] = total[:C, at : at + C]
    low = C // 2
    blocks = [total[C : 2 * C, b * C : (b + 1) * C] for b in range(XB)]
    for b in range(2):
        top, bottom = (total[2 * C :, (2 * b + i) * C : (2 * b + i + 1) * C] for i in range(2))
        blocks.append(jnp.concatenate([top, bottom], axis=0))
    for i, block in enumerate(blocks):
        kernel_ref[i // TAPS, i % TAPS] = block.T


def finish(one, other, layers):
    return pl.pallas_call(
        finish_kernel,
        in_specs=[VMEM] * 2,
        out_specs=[VMEM] * 2,
        out_shape=[
            jax.ShapeDtypeStruct((layers, 2, 1, C, C), F32),
            jax.ShapeDtypeStruct((layers, TAPS, C, C), F32),
        ],
        compiler_params=PARAMS,
    )(one, other)


def on_device(input_field, cotangent, spectral_weights, conv_kernel, mode_list):
    groups = lax.axis_size("tm")
    bricks = lax.axis_size("space")
    everyone = ("tm", "space")
    steps = input_field.shape[0]
    total_time = steps * groups
    layers, _, modes, _, _ = spectral_weights.shape
    scale = 2.0 / total_time
    exchange = functools.partial(lax.all_to_all, split_axis=0, concat_axis=0, tiled=True)

    received = exchange(to_blocks(input_field, cotangent), everyone)
    prepared = prepare(scale, spectral_weights, conv_kernel, mode_list, total_time)
    received, prepared = lax.optimization_barrier((received, prepared))
    grad, *kept = run_layers(
        received.reshape(groups, bricks, 2 * steps * J, LANES), *prepared
    )
    returned = exchange(grad.reshape(groups * bricks, steps * J, LANES), everyone)
    me = lax.axis_index("tm").astype(jnp.int32)
    place = jnp.stack([me // RADIX, me % RADIX])
    pieces = weight_gradients(scale, place, *kept)
    pieces = split_sum(shifted(pieces, "tm", groups, RADIX))
    grad_input, pieces = lax.optimization_barrier(
        (from_blocks(returned), shifted(pieces, "tm", groups, 1))
    )
    total = ring_sum(pieces)
    total = ring_sum(shifted([total] * RADIX, "space", bricks, bricks // RADIX))
    mode_total, kernel_total = finish(*shifted([total] * 2, "space", bricks, 1), layers)
    return (grad_input, mode_total, kernel_total)


def solution(mesh):
    placed = (P("tm", None, "space", None), P("tm", None, "space", None), P(), P(), P())
    return jax.shard_map(
        on_device,
        mesh=mesh,
        in_specs=placed,
        out_specs=(P("tm", None, "space", None), P(None, None, "tm", None, None), P()),
        check_vma=False,
    )
```

```python
import functools
import math

import jax
import jax.numpy as jnp
from jax import lax
from jax.experimental import pallas as pl
from jax.experimental.pallas import tpu as pltpu
from jax.sharding import PartitionSpec as P

F32 = jnp.float32
BF16 = jnp.bfloat16
LANES = 128
J = 8
XB = 4
C = 32
VMEM = pl.BlockSpec(memory_space=pltpu.VMEM)
ANY = pl.BlockSpec(memory_space=pl.ANY)
HBM = pl.BlockSpec(memory_space=pltpu.HBM)
PARAMS = pltpu.CompilerParams(vmem_limit_bytes=40 * 1024 * 1024)


def in_hbm(*values):
    return [pltpu.with_memory_space_constraint(v, pltpu.HBM) for v in values]


def split(value):
    high = value.astype(BF16)
    low = (value - high.astype(F32)).astype(BF16)
    return high, low


def dot3(left, right, dims=((1,), (0,))):
    (lh, ll), (rh, rl) = left, right
    (lc,), (rc,) = dims
    a = jnp.concatenate([lh, ll, lh], axis=lc)
    b = jnp.concatenate([rh, rh, rl], axis=rc)
    return lax.dot_general(a, b, (dims, ((), ())), preferred_element_type=F32)


FETCHED = 1
SENT = 4


def scatter_kernel(first_any, second_any, out_any, field, out, load_sem, store_sem):
    _, _, steps, _, columns = field.shape
    groups = LANES // J
    loads = [
        pltpu.make_async_copy(
            source.at[:, :, x, :], field.at[which, x], load_sem.at[which, x]
        )
        for which, source in enumerate((first_any, second_any))
        for x in range(XB)
    ]
    for load in loads:
        load.start()
    stores = []
    count = columns // LANES
    for which in range(2):
        for load in loads[which * XB : (which + 1) * XB]:
            load.wait()
        for q in range(count):
            lanes = slice(q * LANES, (q + 1) * LANES)
            for t in range(steps):
                at = (which * steps + t) * J
                rows = jnp.concatenate([field[which, x, t, :, lanes] for x in range(XB)], axis=0)
                rows = rows.T.reshape(groups, J, LANES)
                out[q * groups : (q + 1) * groups, at : at + J] = rows
            if (q + 1) % (count // SENT) == 0:
                size = groups * count // SENT
                part = pl.ds((q + 1) * groups - size, size)
                lines = pl.ds(which * steps * J, steps * J)
                stores.append(
                    pltpu.make_async_copy(
                        out.at[part, lines], out_any.at[part, lines], store_sem.at[len(stores)]
                    )
                )
                stores[-1].start()
    for store in stores:
        store.wait()


def gather_kernel(blocks_any, out_any, blocks, out, load_sem, store_sem):
    steps, _, _, columns = out.shape
    groups = LANES // J
    count = columns // LANES
    loads = []
    for i in range(FETCHED):
        part = pl.ds(i * groups * count // FETCHED, groups * count // FETCHED)
        loads.append(pltpu.make_async_copy(blocks_any.at[part], blocks.at[part], load_sem.at[i]))
        loads[-1].start()
    stores = []
    for t in range(steps):
        for q in range(count):
            lanes = slice(q * LANES, (q + 1) * LANES)
            if t == 0 and q % (count // FETCHED) == 0:
                loads[q // (count // FETCHED)].wait()
            rows = blocks[q * groups : (q + 1) * groups, t * J : (t + 1) * J]
            rows = rows.reshape(LANES, LANES).T
            for x in range(XB):
                out[t, :, x, lanes] = rows[x * C : (x + 1) * C]
        if (t + 1) % (steps // SENT) == 0:
            part = pl.ds(t + 1 - steps // SENT, steps // SENT)
            sem = store_sem.at[len(stores)]
            stores.append(pltpu.make_async_copy(out.at[part], out_any.at[part], sem))
            stores[-1].start()
    for store in stores:
        store.wait()


def to_blocks(first, second):
    steps, _, _, columns = first.shape
    shape = (columns // J, 2 * steps * J, LANES)
    return pl.pallas_call(
        scatter_kernel,
        in_specs=[HBM] * 2,
        out_specs=HBM,
        out_shape=pltpu.HBM(shape, F32),
        scratch_shapes=[
            pltpu.VMEM((2, XB, steps, C, columns), F32),
            pltpu.VMEM(shape, F32),
            pltpu.SemaphoreType.DMA((2, XB)),
            pltpu.SemaphoreType.DMA((2 * SENT,)),
        ],
        compiler_params=PARAMS,
    )(*in_hbm(first, second))


def from_blocks(blocks):
    parts, rows, _ = blocks.shape
    shape = (rows // J, C, XB, parts * J)
    return pl.pallas_call(
        gather_kernel,
        in_specs=[ANY],
        out_specs=HBM,
        out_shape=pltpu.HBM(shape, F32),
        scratch_shapes=[
            pltpu.VMEM(blocks.shape, F32),
            pltpu.VMEM(shape, F32),
            pltpu.SemaphoreType.DMA((FETCHED,)),
            pltpu.SemaphoreType.DMA((SENT,)),
        ],
        compiler_params=PARAMS,
    )(blocks)


def angles(mode_list, total_time):
    steps = jnp.arange(total_time, dtype=jnp.int32)
    phase = (mode_list[:, None] * steps[None, :]) % total_time
    angle = phase.astype(F32) * (2.0 * math.pi / total_time)
    both = jnp.stack([jnp.cos(angle), -jnp.sin(angle)], axis=1)
    return both.reshape(2 * mode_list.shape[0], total_time)


def widened(value):
    rows, cols = value.shape
    spread = lax.broadcasted_iota(jnp.int32, (cols, cols * J), 1) // J
    spread = (spread == lax.broadcasted_iota(jnp.int32, (cols, cols * J), 0)).astype(BF16)
    shape = (rows * J, cols * J)
    same = (
        lax.broadcasted_iota(jnp.int32, shape, 0) % J
        == lax.broadcasted_iota(jnp.int32, shape, 1) % J
    )
    for piece in split(value):
        wide = jnp.dot(piece, spread, preferred_element_type=F32)
        wide = jnp.broadcast_to(wide[:, None, :], (rows, J, cols * J)).reshape(shape)
        yield jnp.where(same, wide, 0.0).astype(BF16)


def blocks_of(kernel, places, cols):
    zero = jnp.zeros((C, C), F32)
    rows = [
        jnp.concatenate([kernel[p[y]] if y in p else zero for y in range(cols)], axis=1)
        for p in places
    ]
    return jnp.concatenate(rows, axis=0)


def band(kernel):
    cells = 2 * XB
    own = [{y: x - y + 1 for y in range(cells) if abs(x - y) <= 1} for x in range(cells)]
    before, after = {0: 0}, {cells - 1: 2}
    own = split(blocks_of(kernel, own, cells))
    both = split(blocks_of(kernel, [after, before, after, before], cells))
    edge = split(blocks_of(kernel, [after, {}, {}, before], cells))
    return jnp.concatenate([own[0], own[0], own[1], both[0], edge[1]], axis=0)


def prepare_kernel(scale, tab_ref, tabt_ref, w_ref, k_ref, at, st, wt, vt, fb, bb):
    at[0], at[1] = widened(tab_ref[...])
    st[0], st[1] = widened(tabt_ref[...])
    for l in range(w_ref.shape[0]):

        def body(m, _):
            re, im = w_ref[l, 0, m] * scale, w_ref[l, 1, m] * scale
            wt[0, l, m], wt[1, l, m] = split(jnp.concatenate([re] * XB + [im] * XB, axis=1))
            re, im = re.T, -im.T
            vt[0, l, m], vt[1, l, m] = split(jnp.concatenate([re] * XB + [im] * XB, axis=1))
            return 0

        lax.fori_loop(0, w_ref.shape[2], body, 0)
        taps = [k_ref[l, j] for j in range(3)]
        fb[l] = band(taps)
        bb[l] = band([t.T for t in taps[::-1]])


def prepare(scale, spectral_weights, conv_kernel, mode_list, total_time):
    layers, _, modes, channels, _ = spectral_weights.shape
    tab = angles(mode_list, total_time)
    rows, cols = 2 * modes * J, total_time * J
    shapes = [(2, rows, cols), (2, cols, rows)]
    shapes += [(2, layers, modes, channels, 2 * LANES)] * 2 + [(layers, 8 * LANES, 2 * LANES)] * 2
    return pl.pallas_call(
        functools.partial(prepare_kernel, scale),
        in_specs=[VMEM] * 4,
        out_specs=[VMEM] * 6,
        out_shape=[pltpu.HBM(shape, BF16) for shape in shapes],
        compiler_params=PARAMS,
    )(tab, tab.T, spectral_weights, conv_kernel)


def lane_block():
    return lax.broadcasted_iota(jnp.int32, (1, LANES), 1) // C


def put_split(value, s, high_ref, low_ref):
    high, low = split(value)
    high_ref[s] = high
    low_ref[s] = low


def with_neighbours(ref, s):
    own = ref[s]
    x = lane_block()
    zero = jnp.zeros_like(own)
    before = ref[s - 1] if s > 0 else zero
    after = ref[s + 1] if s + 1 < ref.shape[0] else zero
    edge = jnp.where(x == XB - 1, before, jnp.where(x == 0, after, zero))
    return jnp.concatenate([own, edge], axis=1)


def pair_operand(high_ref, low_ref, s):
    x = lane_block()
    bricks = high_ref.shape[0]

    def edges(ref):
        zero = jnp.zeros_like(ref[s])
        before = ref[s - 1] if s > 0 else zero
        after = ref[s + 2] if s + 2 < bricks else zero
        return jnp.where(x == XB - 1, before, jnp.where(x == 0, after, zero))

    high = [high_ref[s], high_ref[s + 1]]
    low = [low_ref[s], low_ref[s + 1]]
    edge, edge_low = edges(high_ref), edges(low_ref)
    half = LANES // 2
    swapped = jnp.concatenate([edge_low[:, half:], edge_low[:, :half]], axis=1)
    both = jnp.where((x == 0) | (x == XB - 1), edge, swapped)
    return jnp.concatenate([*high, *low, *high, both, edge], axis=1)


def analyse_pair(table, high_ref, low_ref, coef_ref, s):
    right = [jnp.concatenate([r[s], r[s + 1]], axis=1) for r in (high_ref, low_ref)]
    result = dot3(table, right)
    coef_ref[s] = result[:, :LANES]
    coef_ref[s + 1] = result[:, LANES:]


def analyse(table, high_ref, low_ref, coef_ref):
    for s in range(0, high_ref.shape[0], 2):
        analyse_pair(table, high_ref, low_ref, coef_ref, s)


def mixing_rows(w_ref, piece, l, m):
    row = lax.broadcasted_iota(jnp.int32, (LANES, 2 * LANES), 0) // C
    col = lax.broadcasted_iota(jnp.int32, (LANES, 2 * LANES), 1) // C % XB
    wide = jnp.concatenate([w_ref[piece, l, m]] * XB, axis=0)
    return jnp.where(row == col, wide, jnp.zeros_like(wide))


def mix(coef_ref, w_ref, l, mixed_ref):
    bricks = coef_ref.shape[0]
    rows = bricks * J
    for m in range(w_ref.shape[2]):
        re, im = slice(2 * J * m, 2 * J * m + J), slice(2 * J * m + J, 2 * J * (m + 1))
        rh, rl = split(coef_ref[:, re].reshape(rows, LANES))
        ih, il = split(coef_ref[:, im].reshape(rows, LANES))
        left = jnp.concatenate([rh, ih, rl, il], axis=0)
        matrix = jnp.concatenate([mixing_rows(w_ref, piece, l, m) for piece in range(2)], axis=0)
        product = jnp.dot(
            jnp.concatenate([left, left], axis=1), matrix, preferred_element_type=F32
        )
        a = product[:rows] + product[2 * rows : 3 * rows]
        b = product[rows : 2 * rows] + product[3 * rows :]
        mixed_ref[:, re] = (a[:, :LANES] - b[:, LANES:]).reshape(bricks, J, LANES)
        mixed_ref[:, im] = (a[:, LANES:] + b[:, :LANES]).reshape(bricks, J, LANES)


def synthesise(table, mixed_ref, matrix, high_ref, low_ref, emit):
    for s in range(0, mixed_ref.shape[0], 2):
        right = split(jnp.concatenate([mixed_ref[s], mixed_ref[s + 1]], axis=1))
        total = dot3(table, right) + jnp.dot(
            pair_operand(high_ref, low_ref, s), matrix, preferred_element_type=F32
        )
        emit(s, total[:, :LANES])
        emit(s + 1, total[:, LANES:])


def gelu_parts(z):
    cdf = 0.5 * (1.0 + lax.erf(z * math.sqrt(0.5)))
    slope = cdf + z * (jnp.exp(-0.5 * z * z) * (1.0 / math.sqrt(2.0 * math.pi)))
    return z * cdf, slope


STORED = 4


def layers_kernel(*refs):
    both = refs[0]
    small_any = refs[1:7]
    out_any = refs[7]
    kept_any = refs[8:20]
    small = refs[20:26]
    kept = refs[26:38]
    field, sens, slope1, out, mixed, load_sem, small_sem, store_sem = refs[38:]
    analysis_ref, synthesis_ref, mix_forward, mix_backward, band_forward, band_backward = small
    coef1, coef2, sens1, sens2, x1h, x1l, x2h, x2l, z1h, z1l, z2h, z2l = kept
    groups, bricks, lines, _ = both.shape
    lines = lines // 2
    copy = pltpu.make_async_copy

    tables = [copy(a, r, small_sem.at[i]) for i, (a, r) in enumerate(zip(small_any, small))]
    half = bricks // 2
    loads = [
        copy(both.at[:, at, pl.ds(0, lines)], field.at[:, at], load_sem.at[i])
        for i, at in enumerate((pl.ds(0, half), pl.ds(half, half)))
    ]
    loads.append(copy(both.at[:, :, pl.ds(lines, lines)], sens, load_sem.at[2]))
    for load in (tables[0], loads[0], loads[1], tables[2], tables[1], tables[4]):
        load.start()
    stores = []

    def store(source, target):
        stores.append(copy(source, target, store_sem.at[len(stores)]))
        stores[-1].start()

    def keep(*places):
        for i in places:
            store(kept[i], kept_any[i])

    def brick(ref, s):
        return ref[:, s].reshape(-1, LANES)

    def first_out(s, value):
        value, slope = gelu_parts(value)
        slope1[s] = slope
        put_split(value, s, x2h, x2l)

    def second_out(s, value):
        put_split(brick(sens, s) * gelu_parts(value)[1], s, z2h, z2l)

    def second_back(s, value):
        put_split(value * slope1[s], s, z1h, z1l)

    def first_back(s, value):
        out[:, s] = value.reshape(groups, lines, LANES)
        if s % STORED == STORED - 1:
            done = pl.ds(s - STORED + 1, STORED)
            store(out.at[:, done], out_any.at[:, done])

    tables[0].wait()
    analysis = (analysis_ref[0], analysis_ref[1])
    for s in range(0, bricks, 2):
        if s % half == 0:
            loads[s // half].wait()
        for o in (s, s + 1):
            put_split(brick(field, o), o, x1h, x1l)
        analyse_pair(analysis, x1h, x1l, coef1, s)
    for load in (loads[2], tables[3], tables[5]):
        load.start()
    keep(0, 4, 5)
    tables[2].wait()
    mix(coef1, mix_forward, 0, mixed)
    tables[1].wait()
    tables[4].wait()
    synthesis = (synthesis_ref[0], synthesis_ref[1])
    synthesise(synthesis, mixed, band_forward[0], x1h, x1l, first_out)
    analyse(analysis, x2h, x2l, coef2)
    keep(1, 6, 7)
    mix(coef2, mix_forward, 1, mixed)
    loads[2].wait()
    synthesise(synthesis, mixed, band_forward[1], x2h, x2l, second_out)
    analyse(analysis, z2h, z2l, sens2)
    keep(3, 10, 11)
    tables[3].wait()
    mix(sens2, mix_backward, 1, mixed)
    tables[5].wait()
    synthesise(synthesis, mixed, band_backward[1], z2h, z2l, second_back)
    analyse(analysis, z1h, z1l, sens1)
    keep(2, 8, 9)
    mix(sens1, mix_backward, 0, mixed)
    synthesise(synthesis, mixed, band_backward[0], z1h, z1l, first_back)
    for done in stores:
        done.wait()


def run_layers(both, *tables):
    groups, bricks, lines, _ = both.shape
    _, modes, rows = tables[0].shape
    coef = ((bricks, modes, LANES), F32)
    full = ((bricks, rows, LANES), F32)
    half = ((bricks, rows, LANES), BF16)
    result = ((groups, bricks, lines // 2, LANES), F32)
    kept = [coef] * 4 + [half] * 8
    scratch = [(t.shape, t.dtype) for t in tables] + kept + [result, result, full, result, coef]
    return pl.pallas_call(
        layers_kernel,
        in_specs=[ANY] + [HBM] * 6,
        out_specs=[HBM] * 13,
        out_shape=[pltpu.HBM(*o) for o in (result, *kept)],
        scratch_shapes=[pltpu.VMEM(*o) for o in scratch]
        + [
            pltpu.SemaphoreType.DMA((3,)),
            pltpu.SemaphoreType.DMA((6,)),
            pltpu.SemaphoreType.DMA((len(kept) + bricks // STORED,)),
        ],
        compiler_params=PARAMS,
    )(both, *in_hbm(*tables))


ROWS = ((0,), (0,))
TAPS = 3
RADIX = 4


def weight_kernel(scale, me_ref, *refs):
    coef1_any, coef2_any, sens1_any, sens2_any = refs[:4]
    half_any = refs[4:12]
    modes = refs[0].shape[1] // (2 * J)
    outs = refs[12 : 12 + RADIX]
    coef1, coef2, sens1, sens2 = refs[12 + RADIX : 16 + RADIX]
    half = refs[16 + RADIX : 24 + RADIX]
    spectral, load_sem, half_sem = refs[24 + RADIX :]
    bricks = coef1.shape[0]
    copy = pltpu.make_async_copy

    halves = [
        [
            copy(a.at[s], r.at[s], half_sem.at[i, s])
            for i, (a, r) in enumerate(zip(half_any, half))
        ]
        for s in range(bricks)
    ]
    pairs = zip((coef1_any, coef2_any, sens1_any, sens2_any), (coef1, coef2, sens1, sens2))
    loads = [copy(a, r, load_sem.at[i]) for i, (a, r) in enumerate(pairs)]
    x1h, x1l, x2h, x2l, z1h, z1l, z2h, z2l = half
    for l in range(2):
        for s in range(bricks):
            for i in (0, 1, 4, 5) if l == 0 else (2, 3, 6, 7):
                halves[s][i].start()
    for c in loads:
        c.start()

    blocks = []
    for l, (xh, xl, zh, zl) in enumerate(((x1h, x1l, z1h, z1l), (x2h, x2l, z2h, z2l))):
        total = jnp.zeros((LANES, 2 * LANES), F32)
        for s in range(bricks):
            for ahead in (0, 1) if s == 0 else (s + 1,):
                if ahead < bricks:
                    for i in (0, 1, 4, 5) if l == 0 else (2, 3, 6, 7):
                        halves[ahead][i].wait()
            value = (with_neighbours(xh, s), with_neighbours(xl, s))
            total = total + dot3((zh[s], zl[s]), value, ROWS)
        for j in range(TAPS):
            pairs = [(x, x - j + 1) for x in range(XB) if 0 <= x - j + 1 < XB]
            tap = sum(total[y * C : (y + 1) * C, x * C : (x + 1) * C] for x, y in pairs)
            if j == 0:
                tap = tap + total[:C, LANES + (XB - 1) * C :]
            if j == 2:
                tap = tap + total[(XB - 1) * C :, LANES : LANES + C]
            blocks.append(tap)
    half_rows = C // 2
    first = jnp.concatenate(blocks[:4], axis=1)
    rest = [b[i * half_rows : (i + 1) * half_rows] for b in blocks[4:] for i in range(2)]
    kernels = jnp.concatenate([first, jnp.concatenate(rest, axis=1)], axis=0)

    for c in loads:
        c.wait()
    for m in range(modes):
        re, im = slice(2 * J * m, 2 * J * m + J), slice(2 * J * m + J, 2 * J * (m + 1))
        pieces = []
        for coef, sens in ((coef1, sens1), (coef2, sens2)):
            cr, ci, zr, zi = (
                r[:, p].reshape(bricks * J, LANES)
                for r, p in ((coef, re), (coef, im), (sens, re), (sens, im))
            )
            left = jnp.concatenate([cr, ci], axis=0)
            right = jnp.concatenate(
                [jnp.concatenate([zr, zi], axis=1), jnp.concatenate([zi, -zr], axis=1)], axis=0
            )
            product = dot3(split(left), split(right), ROWS) * scale
            for part in range(2):
                pieces.append(
                    sum(
                        product[x * C : (x + 1) * C, part * LANES + x * C : part * LANES + (x + 1) * C]
                        for x in range(XB)
                    )
                )
        spectral[m] = jnp.concatenate(pieces, axis=1)
    for r, out in enumerate(outs):
        high = (me_ref[0] + r) % RADIX
        for q in range(RADIX):
            low = (me_ref[1] + q) % RADIX
            out[q * C : (q + 1) * C] = spectral[high * RADIX + low]
        out[RADIX * C :] = kernels


def weight_gradients(scale, me, *operands):
    modes = operands[0].shape[1] // (2 * J)
    rows = RADIX * C + 2 * TAPS * C // XB
    return pl.pallas_call(
        functools.partial(weight_kernel, scale),
        in_specs=[pl.BlockSpec(memory_space=pltpu.SMEM)] + [HBM] * 12,
        out_specs=[VMEM] * RADIX,
        out_shape=[jax.ShapeDtypeStruct((rows, LANES), F32)] * RADIX,
        scratch_shapes=[pltpu.VMEM(o.shape, o.dtype) for o in operands]
        + [
            pltpu.VMEM((modes, C, LANES), F32),
            pltpu.SemaphoreType.DMA((4,)),
            pltpu.SemaphoreType.DMA((8, operands[0].shape[0])),
        ],
        compiler_params=PARAMS,
    )(me, *in_hbm(*operands))


def shifted(pieces, axis, size, stride):
    count = len(pieces)
    got = [pieces[0]]
    for r in range(1, count):
        perm = []
        for i in range(size):
            digit = i // stride % count
            perm.append((i, i + ((digit + r) % count - digit) * stride))
        got.append(lax.ppermute(pieces[r], axis, perm))
    return got


def ring_sum(values):
    while len(values) > 1:
        half = len(values) // 2
        values = [values[i] + values[i + half] for i in range(half)]
    return values[0]


def split_sum_kernel(*refs):
    total = ring_sum([r[...] for r in refs[:RADIX]])
    for q, out in enumerate(refs[RADIX:]):
        out[:C] = total[q * C : (q + 1) * C]
        out[C:] = total[RADIX * C :]


def split_sum(pieces):
    rows = pieces[0].shape[0] - (RADIX - 1) * C
    return pl.pallas_call(
        split_sum_kernel,
        in_specs=[VMEM] * RADIX,
        out_specs=[VMEM] * RADIX,
        out_shape=[jax.ShapeDtypeStruct((rows, LANES), F32)] * RADIX,
        compiler_params=PARAMS,
    )(*pieces)


def finish_kernel(one_ref, other_ref, mode_ref, kernel_ref):
    total = one_ref[...] + other_ref[...]
    layers = mode_ref.shape[0]
    for l in range(layers):
        for part in range(2):
            at = (2 * l + part) * C
            mode_ref[l, part, 0] = total[:C, at : at + C]
    low = C // 2
    blocks = [total[C : 2 * C, b * C : (b + 1) * C] for b in range(XB)]
    for b in range(2):
        top, bottom = (total[2 * C :, (2 * b + i) * C : (2 * b + i + 1) * C] for i in range(2))
        blocks.append(jnp.concatenate([top, bottom], axis=0))
    for i, block in enumerate(blocks):
        kernel_ref[i // TAPS, i % TAPS] = block.T


def finish(one, other, layers):
    return pl.pallas_call(
        finish_kernel,
        in_specs=[VMEM] * 2,
        out_specs=[VMEM] * 2,
        out_shape=[
            jax.ShapeDtypeStruct((layers, 2, 1, C, C), F32),
            jax.ShapeDtypeStruct((layers, TAPS, C, C), F32),
        ],
        compiler_params=PARAMS,
    )(one, other)


def on_device(input_field, cotangent, spectral_weights, conv_kernel, mode_list):
    groups = lax.axis_size("tm")
    bricks = lax.axis_size("space")
    everyone = ("tm", "space")
    steps = input_field.shape[0]
    total_time = steps * groups
    layers, _, modes, _, _ = spectral_weights.shape
    scale = 2.0 / total_time
    exchange = functools.partial(lax.all_to_all, split_axis=0, concat_axis=0, tiled=True)

    received = exchange(to_blocks(input_field, cotangent), everyone)
    prepared = prepare(scale, spectral_weights, conv_kernel, mode_list, total_time)
    received, prepared = lax.optimization_barrier((received, prepared))
    grad, *kept = run_layers(
        received.reshape(groups, bricks, 2 * steps * J, LANES), *prepared
    )
    returned = exchange(grad.reshape(groups * bricks, steps * J, LANES), everyone)
    me = lax.axis_index("tm").astype(jnp.int32)
    place = jnp.stack([me // RADIX, me % RADIX])
    pieces = weight_gradients(scale, place, *kept)
    pieces = split_sum(shifted(pieces, "tm", groups, RADIX))
    total = ring_sum(shifted(pieces, "tm", groups, 1))
    grad_input, pieces = lax.optimization_barrier(
        (
            from_blocks(returned),
            shifted([total] * RADIX, "space", bricks, bricks // RADIX),
        )
    )
    total = ring_sum(pieces)
    mode_total, kernel_total = finish(*shifted([total] * 2, "space", bricks, 1), layers)
    return (grad_input, mode_total, kernel_total)


def solution(mesh):
    placed = (P("tm", None, "space", None), P("tm", None, "space", None), P(), P(), P())
    return jax.shard_map(
        on_device,
        mesh=mesh,
        in_specs=placed,
        out_specs=(P("tm", None, "space", None), P(None, None, "tm", None, None), P()),
        check_vma=False,
    )
```
